32 devices in a mesh: dp: 8 (over y, x, core), tensor: 4 (over z).
Axes of the slice: x: 2, y: 2, z: 4, core: 2. Of those that a mesh axis runs over, the one named last changes fastest.
Arguments:
- hidden_in: bfloat16 [4096, 1536], P(('dp', 'tensor')), may hold values from -6 to 6
- positions: int32 [4096], P(('dp', 'tensor')), may hold values from 0 to 511, as said below
- gain_attn: bfloat16 [1536], P(('dp', 'tensor')), may hold values from 0.5 to 1.5
- w_query: bfloat16 [1536, 1536], P(('dp', 'tensor')), may hold values from -0.15625 to 0.15625
- key_matrix: bfloat16 [1536, 768], P(('dp', 'tensor')), may hold values from -0.15625 to 0.15625
- value_matrix: bfloat16 [1536, 768], P(('dp', 'tensor')), may hold values from -0.15625 to 0.15625
- w_output: bfloat16 [1536, 1536], P(('dp', 'tensor')), may hold values from -3.5 to 3.5
- gain_mlp: bfloat16 [1536], P(('dp', 'tensor')), may hold values from 0.5 to 1.5
- w_gate: bfloat16 [1536, 4096], P(None, 'tensor'), may hold values from -0.15625 to 0.15625
- w_up: bfloat16 [1536, 4096], P(None, 'tensor'), may hold values from -0.15625 to 0.15625
- w_down: bfloat16 [4096, 1536], P('tensor'), may hold values from -0.09375 to 0.09375
- cotangent: bfloat16 [4096, 1536], P(('dp', 'tensor')), may hold values from -6 to 6
Outputs:
- layer_out: bfloat16 [4096, 1536], P(('dp', 'tensor'))
- grad_input: float32 [4096, 1536], P(('dp', 'tensor'))
- grad_gain_attn: float32 [1536], P(('dp', 'tensor'))
- grad_w_query: float32 [1536, 1536], P(('dp', 'tensor'))
- grad_w_key: float32 [1536, 768], P(('dp', 'tensor'))
- grad_w_value: float32 [1536, 768], P(('dp', 'tensor'))
- grad_w_output: float32 [1536, 1536], P(('dp', 'tensor'))
- grad_gain_mlp: float32 [1536], P(('dp', 'tensor'))
- grad_w_gate: float32 [1536, 4096], P('dp', 'tensor')
- grad_w_up: float32 [1536, 4096], P('dp', 'tensor')
- grad_w_down: float32 [4096, 1536], P('tensor', 'dp')
The draws below stay inside these ranges and needn't reach their ends.
Inputs may be any that keep to these rules, and one draw needn't show every extreme that they name: positions is 0 at the first token of every document and at every sequence's first row (multiples of 512), and rises by one from each token to the next within a document; documents are runs of consecutive tokens; the first sequence is a single document of 512 tokens.
All inputs are finite; a program needn't handle non-finite values.
Results may differ from the reference program's by a relative error of at most 0.015.
Values may be sent and summed in bfloat16 or wider, within the bound.
A program may use at most 192 MiB of HBM per device.

```python
import math
import jax
import jax.numpy as jnp
from jax import lax

MODEL_DIMENSION = 1536
QUERY_HEADS = 16
KEY_VALUE_HEADS = 8
HEAD_DIMENSION = 96
FF = 4096
DOC_LEN = 1024
SEQUENCE_TOKENS = 512
TOKENS = 4096
N_DP = 8


def draw_positions(key, part):
    base = jax.random.fold_in(key, 11)
    index = jnp.arange(TOKENS, dtype=jnp.int32)
    starts = (jax.random.randint(base, (TOKENS,), 0, DOC_LEN) == 0) & (index >= SEQUENCE_TOKENS) | (index % SEQUENCE_TOKENS == 0)
    first = lax.cummax(jnp.where(starts, index, 0), axis=0)
    return (index - first).astype(jnp.int32)


def with_spikes(values, own_key, source, target, parts, factor):
    def block_of(axis_at):
        return (jnp.arange(values.shape[axis_at]) // (values.shape[axis_at] // parts)).reshape((-1,) + (1,) * (values.ndim - 1 - axis_at))

    first = jax.random.permutation(own_key, parts)[block_of(target)]
    other_side = (block_of(target) + parts // 2) % parts
    return jnp.where((block_of(source) == first) | (block_of(source) == other_side), factor * values, values)


def block_levels(stream_key, extent, pieces, least, largest):
    gain = 1.0
    for axis_at, shards_of in pieces:
        draws = jax.random.uniform(jax.random.fold_in(jax.random.fold_in(stream_key, 6), axis_at), (shards_of,), jnp.float32, least / len(pieces), largest / len(pieces))
        gain = gain * jnp.repeat(jnp.exp(draws), extent[axis_at] // shards_of).reshape((-1,) + (1,) * (len(extent) - 1 - axis_at))
    return gain


def scatter_about(own_key, shape, spread, bound, cuts=(), held_as=jnp.bfloat16):
    result = spread * jax.random.normal(own_key, shape, jnp.float32)
    if cuts:
        result = result * block_levels(own_key, shape, cuts, -0.22, 0.18)
    return jnp.clip(result, -bound, bound).astype(held_as)


def bell_draw_with(rng, shape, scale, bound, split, heavy, held_as=jnp.bfloat16):
    values = scale * jax.random.normal(rng, shape, jnp.float32)
    if split:
        values = values * block_levels(rng, shape, split, -0.22, 0.18)
    return jnp.clip(with_spikes(values, jax.random.fold_in(rng, 3), *heavy), -bound, bound).astype(held_as)


def setup_inputs(seed: int = 0) -> dict:
    splits = jax.random.split(jax.random.key(seed), 13)
    hidden_in = bell_draw_with(splits[0], (TOKENS, MODEL_DIMENSION), 1.0, 6.0, ((0, 32),), (0, 1, 32, 2.75))
    positions = draw_positions(jax.random.fold_in(splits[12], 71), 0)
    gain_attn = jnp.clip(1.0 + 0.1 * jax.random.normal(splits[2], (MODEL_DIMENSION,), jnp.float32), 0.5, 1.5).astype(jnp.bfloat16)
    w_query = scatter_about(splits[3], (MODEL_DIMENSION, MODEL_DIMENSION), MODEL_DIMENSION ** -0.5, 0.15625, ((0, 32),))
    key_matrix = scatter_about(splits[4], (MODEL_DIMENSION, KEY_VALUE_HEADS * HEAD_DIMENSION), MODEL_DIMENSION ** -0.5, 0.15625, ((0, 32),))
    value_matrix = scatter_about(splits[5], (MODEL_DIMENSION, KEY_VALUE_HEADS * HEAD_DIMENSION), MODEL_DIMENSION ** -0.5, 0.15625, ((0, 32),))
    w_output = scatter_about(splits[6], (MODEL_DIMENSION, MODEL_DIMENSION), (max(MODEL_DIMENSION // 512, 1)) ** -0.5, 3.5, ((0, 32),))
    gain_mlp = jnp.clip(1.0 + 0.1 * jax.random.normal(splits[7], (MODEL_DIMENSION,), jnp.float32), 0.5, 1.5).astype(jnp.bfloat16)
    w_gate = scatter_about(splits[8], (MODEL_DIMENSION, FF), MODEL_DIMENSION ** -0.5, 0.15625, ((1, 4),))
    w_up = scatter_about(splits[9], (MODEL_DIMENSION, FF), MODEL_DIMENSION ** -0.5, 0.15625, ((1, 4),))
    w_down = scatter_about(splits[10], (FF, MODEL_DIMENSION), FF ** -0.5, 0.09375, ((0, 4),))
    cotangent = scatter_about(splits[11], (TOKENS, MODEL_DIMENSION), 1.0, 6.0, ((0, 32),))
    return {"hidden_in": hidden_in, "positions": positions, "gain_attn": gain_attn, "w_query": w_query, "key_matrix": key_matrix, "value_matrix": value_matrix, "w_output": w_output, "gain_mlp": gain_mlp, "w_gate": w_gate, "w_up": w_up, "w_down": w_down, "cotangent": cotangent}


@jax.custom_vjp
def low(v):
    return lax.optimization_barrier(v.astype(jnp.bfloat16)).astype(jnp.float32)

@jax.custom_vjp
def low_back(v):
    return v

def low_keep(v):
    return (low(v), None)

def low_pass(kept, grad):
    return (grad,)

def back_keep(v):
    return (v, None)

def back_low(kept, grad):
    return (low(grad),)
low.defvjp(low_keep, low_pass)
low_back.defvjp(back_keep, back_low)
EPSILON = 1e-05
ROPE_BASE = 100000.0
MASKED = -1e+30

def matmul_hi(left, right):
    return jnp.dot(left, right, precision=lax.Precision.HIGHEST, preferred_element_type=jnp.float32)

def angle_tables(pos_seq, head_size):
    half_size = head_size // 2
    freq_rates = ROPE_BASE ** (-(jnp.arange(half_size, dtype=jnp.float32) * 2.0) / head_size)
    turned = pos_seq.astype(jnp.float32)[:, None] * freq_rates[None, :]
    return (jnp.cos(turned)[:, None, :], jnp.sin(turned)[:, None, :])

def apply_rotary(tensor_in, cosine_table, sine_table):
    half_size = tensor_in.shape[-1] // 2
    lo_half = tensor_in[..., :half_size]
    hi_half = tensor_in[..., half_size:]
    return jnp.concatenate([lo_half * cosine_table - hi_half * sine_table, hi_half * cosine_table + lo_half * sine_table], axis=-1)

def seq_layer(x_seq, pos_seq, params):
    gain_one, query_w, key_w, value_w, output_w, gain_two, gate_w, up_w, down_w = params
    queries_per_group = QUERY_HEADS // KEY_VALUE_HEADS
    score_scale = 1.0 / math.sqrt(HEAD_DIMENSION)
    inv_one = lax.rsqrt(lax.optimization_barrier(jnp.mean(x_seq * x_seq, axis=-1, keepdims=True)) + EPSILON)
    normed_one = low(x_seq * inv_one * gain_one)
    queries = low_back(matmul_hi(normed_one, query_w))
    key_projected = low_back(matmul_hi(normed_one, key_w))
    value_rows_lowered = low(low_back(matmul_hi(normed_one, value_w)))
    cosine_table, sine_table = angle_tables(pos_seq, HEAD_DIMENSION)
    rotated_query_rows = low(apply_rotary(queries.reshape(SEQUENCE_TOKENS, QUERY_HEADS, HEAD_DIMENSION), cosine_table, sine_table))
    rotated_key_rows = low(apply_rotary(key_projected.reshape(SEQUENCE_TOKENS, KEY_VALUE_HEADS, HEAD_DIMENSION), cosine_table, sine_table))
    seq_index = jnp.arange(SEQUENCE_TOKENS, dtype=jnp.int32)
    visible = (seq_index[None, :] <= seq_index[:, None]) & (seq_index[None, :] >= (seq_index - pos_seq)[:, None])
    visible = jnp.tile(visible, (queries_per_group, 1))
    query_heads = rotated_query_rows.reshape(SEQUENCE_TOKENS, KEY_VALUE_HEADS, queries_per_group, HEAD_DIMENSION).transpose(1, 2, 0, 3).reshape(KEY_VALUE_HEADS, queries_per_group * SEQUENCE_TOKENS, HEAD_DIMENSION)
    k_heads = rotated_key_rows.transpose(1, 0, 2)
    value_heads = value_rows_lowered.reshape(SEQUENCE_TOKENS, KEY_VALUE_HEADS, HEAD_DIMENSION).transpose(1, 0, 2)

    def attend(head_items):
        q_block, k_block, v_block = head_items
        scores = low_back(jnp.einsum('qd,kd->qk', q_block, k_block, precision=lax.Precision.HIGHEST) * score_scale)
        scores = jnp.where(visible, scores, MASKED)
        peak = lax.optimization_barrier(jnp.max(scores, axis=-1, keepdims=True))
        exp_vals = jnp.exp(scores - peak)
        probs = exp_vals / lax.optimization_barrier(jnp.sum(exp_vals, axis=-1, keepdims=True))
        return jnp.einsum('qk,kd->qd', low(probs), v_block, precision=lax.Precision.HIGHEST)
    attended_rows = lax.map(jax.checkpoint(attend), (query_heads, k_heads, value_heads))
    attended_rows = attended_rows.reshape(KEY_VALUE_HEADS, queries_per_group, SEQUENCE_TOKENS, HEAD_DIMENSION).transpose(2, 0, 1, 3).reshape(SEQUENCE_TOKENS, QUERY_HEADS * HEAD_DIMENSION)
    attended_low = low(low_back(attended_rows))
    resid_sum = x_seq + low_back(matmul_hi(attended_low, output_w))
    inv_two = lax.rsqrt(lax.optimization_barrier(jnp.mean(resid_sum * resid_sum, axis=-1, keepdims=True)) + EPSILON)
    normed_two = low(resid_sum * inv_two * gain_two)
    gate_val = low_back(matmul_hi(normed_two, gate_w))
    up_val = low_back(matmul_hi(normed_two, up_w))
    act_low = low(jax.nn.silu(gate_val) * up_val)
    return resid_sum + low_back(matmul_hi(act_low, down_w))

def reference(hidden_in, positions, gain_attn, w_query, key_matrix, value_matrix, w_output, gain_mlp, w_gate, w_up, w_down, cotangent):
    pos_all = positions.reshape(N_DP, SEQUENCE_TOKENS)
    per_seq = jax.checkpoint(seq_layer)

    def forward(x_all, gain_one, query_w, key_w, value_w, output_w, gain_two, gate_w, up_w, down_w):
        params = (gain_one, query_w, key_w, value_w, output_w, gain_two, gate_w, up_w, down_w)
        outs = lax.map(lambda pair: per_seq(pair[0], pair[1], params), (x_all.reshape(N_DP, SEQUENCE_TOKENS, MODEL_DIMENSION), pos_all))
        return outs.reshape(TOKENS, MODEL_DIMENSION)
    layer_out, pull = jax.vjp(forward, hidden_in.astype(jnp.float32), gain_attn.astype(jnp.float32), w_query.astype(jnp.float32), key_matrix.astype(jnp.float32), value_matrix.astype(jnp.float32), w_output.astype(jnp.float32), gain_mlp.astype(jnp.float32), w_gate.astype(jnp.float32), w_up.astype(jnp.float32), w_down.astype(jnp.float32))
    grads = pull(cotangent.astype(jnp.float32))
    return (layer_out.astype(jnp.bfloat16), grads[0], grads[1], grads[2], grads[3], grads[4], grads[5], grads[6], grads[7], grads[8], grads[9])
```

```python
import math

import jax
import jax.numpy as jnp
from jax import lax
from jax.sharding import PartitionSpec as P

QUERY_HEADS = 16
KEY_VALUE_HEADS = 8
HEAD_DIMENSION = 96


EPSILON = 1e-05
ROPE_BASE = 100000.0
MASKED = -1e30


def angle_tables(pos_rows, head_size):
    half_size = head_size // 2
    freq_rates = ROPE_BASE ** (-(jnp.arange(half_size, dtype=jnp.float32) * 2.0) / head_size)
    turned = pos_rows.astype(jnp.float32)[:, None] * freq_rates[None, :]
    return (jnp.cos(turned)[:, None, :], jnp.sin(turned)[:, None, :])


def apply_rotary(tensor_in, cosine_table, sine_table):
    half_size = tensor_in.shape[-1] // 2
    lo_half = tensor_in[..., :half_size]
    hi_half = tensor_in[..., half_size:]
    return jnp.concatenate(
        [
            lo_half * cosine_table - hi_half * sine_table,
            hi_half * cosine_table + lo_half * sine_table,
        ],
        axis=-1,
    )


def shards(
    hidden_in,
    positions,
    gain_attn,
    w_query,
    key_matrix,
    value_matrix,
    w_output,
    gain_mlp,
    w_gate,
    w_up,
    w_down,
    cotangent,
):
    tok_rows = hidden_in.shape[0]
    model_width = hidden_in.shape[1]
    num_heads = QUERY_HEADS
    key_value_count = KEY_VALUE_HEADS
    head_size = HEAD_DIMENSION
    kv_width = key_value_count * head_size
    queries_per_group = num_heads // key_value_count
    seq_len = tok_rows * lax.axis_size("tensor")
    score_scale = 1.0 / math.sqrt(head_size)
    gathered = (
        lax.all_gather(gain_attn, ("dp", "tensor"), axis=0, tiled=True),
        lax.all_gather(w_query, ("dp", "tensor"), axis=0, tiled=True),
        lax.all_gather(key_matrix, ("dp", "tensor"), axis=0, tiled=True),
        lax.all_gather(value_matrix, ("dp", "tensor"), axis=0, tiled=True),
        lax.all_gather(w_output, ("dp", "tensor"), axis=0, tiled=True),
        lax.all_gather(gain_mlp, ("dp", "tensor"), axis=0, tiled=True),
    )
    gain_one, query_full, key_full, value_full, output_full, gain_two = gathered
    gain_one_f = gain_one.astype(jnp.float32)
    gain_two_f = gain_two.astype(jnp.float32)
    x_float = hidden_in.astype(jnp.float32)
    inv_one = lax.rsqrt(jnp.mean(x_float * x_float, axis=-1, keepdims=True) + EPSILON)
    normed_one = (x_float * inv_one * gain_one_f).astype(jnp.bfloat16)
    queries = jnp.dot(normed_one, query_full, preferred_element_type=jnp.float32)
    key_projected = jnp.dot(normed_one, key_full, preferred_element_type=jnp.float32)
    value_proj = jnp.dot(normed_one, value_full, preferred_element_type=jnp.float32)
    cosine_table, sine_table = angle_tables(positions, head_size)
    rotated_query_rows = apply_rotary(
        queries.reshape(tok_rows, num_heads, head_size), cosine_table, sine_table
    ).astype(jnp.bfloat16)
    rotated_key_rows = (
        apply_rotary(
            key_projected.reshape(tok_rows, key_value_count, head_size), cosine_table, sine_table
        )
        .astype(jnp.bfloat16)
        .reshape(tok_rows, kv_width)
    )
    value_rows_lowered = value_proj.astype(jnp.bfloat16)
    keys_all, values_all = (
        lax.all_gather(rotated_key_rows, "tensor", axis=0, tiled=True),
        lax.all_gather(value_rows_lowered, "tensor", axis=0, tiled=True),
    )
    offset = lax.axis_index("tensor") * tok_rows
    query_index = offset + jnp.arange(tok_rows, dtype=jnp.int32)
    key_index = jnp.arange(seq_len, dtype=jnp.int32)
    visible = (key_index[None, :] <= query_index[:, None]) & (
        key_index[None, :] >= (query_index - positions)[:, None]
    )
    visible = jnp.tile(visible, (queries_per_group, 1))

    def split_queries(tensor_in):
        return (
            tensor_in.reshape(tok_rows, key_value_count, queries_per_group, head_size)
            .transpose(1, 2, 0, 3)
            .reshape(key_value_count, queries_per_group * tok_rows, head_size)
        )

    def split_keys(tensor_in):
        return tensor_in.reshape(seq_len, key_value_count, head_size).transpose(1, 0, 2)

    def merge_heads(tensor_in):
        return (
            tensor_in.reshape(key_value_count, queries_per_group, tok_rows, head_size)
            .transpose(2, 0, 1, 3)
            .reshape(tok_rows, model_width)
        )

    query_heads = split_queries(rotated_query_rows)
    k_heads = split_keys(keys_all)
    value_heads = split_keys(values_all)

    def attend(head_items):
        q_block, k_block, v_block = head_items
        scores = (
            jnp.einsum("qd,kd->qk", q_block, k_block, preferred_element_type=jnp.float32)
            * score_scale
        )
        scores = jnp.where(visible, scores, MASKED)
        peak = jnp.max(scores, axis=-1, keepdims=True)
        exp_vals = jnp.exp(scores - peak)
        total = jnp.sum(exp_vals, axis=-1, keepdims=True)
        probs = exp_vals / total
        out_block = jnp.einsum(
            "qk,kd->qd", probs.astype(jnp.bfloat16), v_block, preferred_element_type=jnp.float32
        )
        return (out_block, peak[:, 0] + jnp.log(total[:, 0]))

    attended_rows, log_total = lax.map(attend, (query_heads, k_heads, value_heads))
    attended_low = merge_heads(attended_rows).astype(jnp.bfloat16)
    resid_sum = x_float + jnp.dot(attended_low, output_full, preferred_element_type=jnp.float32)
    inv_two = lax.rsqrt(jnp.mean(resid_sum * resid_sum, axis=-1, keepdims=True) + EPSILON)
    normed_two = (resid_sum * inv_two * gain_two_f).astype(jnp.bfloat16)
    rows_all = lax.all_gather(normed_two, "tensor", axis=0, tiled=True)
    gate_val = jnp.dot(rows_all, w_gate, preferred_element_type=jnp.float32)
    up_val = jnp.dot(rows_all, w_up, preferred_element_type=jnp.float32)
    sig_gate = jax.nn.sigmoid(gate_val)
    silu_gate = gate_val * sig_gate
    act_low = (silu_gate * up_val).astype(jnp.bfloat16)
    mlp_sum = lax.psum_scatter(
        jnp.dot(act_low, w_down, preferred_element_type=jnp.float32).astype(jnp.bfloat16),
        "tensor",
        scatter_dimension=0,
        tiled=True,
    ).astype(jnp.float32)
    layer_out = (resid_sum + mlp_sum).astype(jnp.bfloat16)
    grad_float = cotangent.astype(jnp.float32)
    grad_all = lax.all_gather(cotangent, "tensor", axis=0, tiled=True)
    grad_down = jnp.einsum("sf,sd->fd", act_low, grad_all, preferred_element_type=jnp.float32)
    g_act = jnp.einsum("sd,fd->sf", grad_all, w_down, preferred_element_type=jnp.float32)
    g_gate = (g_act * up_val * sig_gate * (1.0 + gate_val * (1.0 - sig_gate))).astype(jnp.bfloat16)
    g_up = (g_act * silu_gate).astype(jnp.bfloat16)
    grad_gate = jnp.einsum("sd,sf->df", rows_all, g_gate, preferred_element_type=jnp.float32)
    grad_up = jnp.einsum("sd,sf->df", rows_all, g_up, preferred_element_type=jnp.float32)
    g_norm_two = lax.psum_scatter(
        (
            jnp.einsum("sf,df->sd", g_gate, w_gate, preferred_element_type=jnp.float32)
            + jnp.einsum("sf,df->sd", g_up, w_up, preferred_element_type=jnp.float32)
        ).astype(jnp.bfloat16),
        "tensor",
        scatter_dimension=0,
        tiled=True,
    ).astype(jnp.float32)
    scaled_two = gain_two_f * g_norm_two
    grad_gain_two = jnp.sum(g_norm_two * resid_sum * inv_two, axis=0)
    g_resid = (
        grad_float
        + inv_two * scaled_two
        - resid_sum * inv_two**3 * jnp.mean(scaled_two * resid_sum, axis=-1, keepdims=True)
    )
    g_resid_low = g_resid.astype(jnp.bfloat16)
    grad_output = jnp.einsum(
        "tc,td->cd", attended_low, g_resid_low, preferred_element_type=jnp.float32
    )
    g_att = jnp.einsum(
        "td,cd->tc", g_resid_low, output_full, preferred_element_type=jnp.float32
    ).astype(jnp.bfloat16)
    g_heads = split_queries(g_att)

    def attend_back(head_items):
        q_block, k_block, v_block, log_block, g_block = head_items
        scores = (
            jnp.einsum("qd,kd->qk", q_block, k_block, preferred_element_type=jnp.float32)
            * score_scale
        )
        scores = jnp.where(visible, scores, MASKED)
        probs = jnp.exp(scores - log_block[:, None])
        g_probs = jnp.einsum("qd,kd->qk", g_block, v_block, preferred_element_type=jnp.float32)
        g_scores = (probs * (g_probs - jnp.sum(probs * g_probs, axis=-1, keepdims=True))).astype(
            jnp.bfloat16
        )
        g_rq = (
            jnp.einsum("qk,kd->qd", g_scores, k_block, preferred_element_type=jnp.float32)
            * score_scale
        )
        g_rk = (
            jnp.einsum("qk,qd->kd", g_scores, q_block, preferred_element_type=jnp.float32)
            * score_scale
        )
        g_val = jnp.einsum(
            "qk,qd->kd", probs.astype(jnp.bfloat16), g_block, preferred_element_type=jnp.float32
        )
        return (g_rq, g_rk, g_val)

    g_rq, g_rk, g_val = lax.map(
        attend_back, (query_heads, k_heads, value_heads, log_total, g_heads)
    )
    g_rk_flat = g_rk.transpose(1, 0, 2).reshape(seq_len, kv_width)
    g_val_flat = g_val.transpose(1, 0, 2).reshape(seq_len, kv_width)
    key_part, value_part = (
        lax.psum_scatter(
            g_rk_flat.astype(jnp.bfloat16), "tensor", scatter_dimension=0, tiled=True
        ).astype(jnp.float32),
        lax.psum_scatter(
            g_val_flat.astype(jnp.bfloat16), "tensor", scatter_dimension=0, tiled=True
        ).astype(jnp.float32),
    )
    g_queries = (
        apply_rotary(
            merge_heads(g_rq).reshape(tok_rows, num_heads, head_size), cosine_table, -sine_table
        )
        .reshape(tok_rows, model_width)
        .astype(jnp.bfloat16)
    )
    g_keys = (
        apply_rotary(
            key_part.reshape(tok_rows, key_value_count, head_size), cosine_table, -sine_table
        )
        .reshape(tok_rows, kv_width)
        .astype(jnp.bfloat16)
    )
    g_values = value_part.astype(jnp.bfloat16)
    grad_query = jnp.einsum("tc,td->cd", normed_one, g_queries, preferred_element_type=jnp.float32)
    grad_key = jnp.einsum("tc,td->cd", normed_one, g_keys, preferred_element_type=jnp.float32)
    grad_value = jnp.einsum("tc,td->cd", normed_one, g_values, preferred_element_type=jnp.float32)
    g_norm_one = (
        jnp.einsum("td,cd->tc", g_queries, query_full, preferred_element_type=jnp.float32)
        + jnp.einsum("td,cd->tc", g_keys, key_full, preferred_element_type=jnp.float32)
        + jnp.einsum("td,cd->tc", g_values, value_full, preferred_element_type=jnp.float32)
    )
    scaled_one = gain_one_f * g_norm_one
    grad_gain_one = jnp.sum(g_norm_one * x_float * inv_one, axis=0)
    grad_input = (
        g_resid
        + inv_one * scaled_one
        - x_float * inv_one**3 * jnp.mean(scaled_one * x_float, axis=-1, keepdims=True)
    )
    packed = jnp.concatenate([grad_query, grad_key, grad_value, grad_output], axis=1)
    packed_part = lax.psum_scatter(
        packed.astype(jnp.bfloat16), ("dp", "tensor"), scatter_dimension=0, tiled=True
    ).astype(jnp.float32)
    query_part = packed_part[:, :model_width]
    keyw_part = packed_part[:, model_width : model_width + kv_width]
    valuew_part = packed_part[:, model_width + kv_width : model_width + 2 * kv_width]
    out_part = packed_part[:, model_width + 2 * kv_width :]
    gain_one_part, gain_two_part = (
        lax.psum_scatter(grad_gain_one, ("dp", "tensor"), scatter_dimension=0, tiled=True),
        lax.psum_scatter(grad_gain_two, ("dp", "tensor"), scatter_dimension=0, tiled=True),
    )
    gate_sum, up_sum, down_sum = (
        lax.psum_scatter(
            grad_gate.astype(jnp.bfloat16), "dp", scatter_dimension=0, tiled=True
        ).astype(jnp.float32),
        lax.psum_scatter(
            grad_up.astype(jnp.bfloat16), "dp", scatter_dimension=0, tiled=True
        ).astype(jnp.float32),
        lax.psum_scatter(
            grad_down.astype(jnp.bfloat16), "dp", scatter_dimension=1, tiled=True
        ).astype(jnp.float32),
    )
    return (
        layer_out,
        grad_input,
        gain_one_part,
        query_part,
        keyw_part,
        valuew_part,
        out_part,
        gain_two_part,
        gate_sum,
        up_sum,
        down_sum,
    )


def solution(mesh):
    placed = (
        P(("dp", "tensor"), None),
        P(("dp", "tensor")),
        P(("dp", "tensor")),
        P(("dp", "tensor"), None),
        P(("dp", "tensor"), None),
        P(("dp", "tensor"), None),
        P(("dp", "tensor"), None),
        P(("dp", "tensor")),
        P(None, "tensor"),
        P(None, "tensor"),
        P("tensor", None),
        P(("dp", "tensor"), None),
    )
    return jax.shard_map(
        shards,
        mesh=mesh,
        in_specs=placed,
        out_specs=(
            P(("dp", "tensor"), None),
            P(("dp", "tensor"), None),
            P(("dp", "tensor")),
            P(("dp", "tensor"), None),
            P(("dp", "tensor"), None),
            P(("dp", "tensor"), None),
            P(("dp", "tensor"), None),
            P(("dp", "tensor")),
            P("dp", "tensor"),
            P("dp", "tensor"),
            P("tensor", "dp"),
        ),
        check_vma=False,
    )
```

```python
import functools
import math

import jax
import jax.numpy as jnp
import numpy as np
from jax import lax
from jax.experimental import pallas as pl
from jax.experimental.pallas import tpu as pltpu
from jax.sharding import PartitionSpec as P

F32 = jnp.float32
BF16 = jnp.bfloat16
MESH = pl.DeviceIdType.MESH
EPSILON = 1e-05
ROPE_BASE = 100000.0
MASKED = -1e30
HEAD = 96
VMEM_LIMIT = 64 * 2**20 - 65536


def rotary_tables(rows, shards_in_sequence):
    half = HEAD // 2
    lanes = np.arange(4 * HEAD) % half
    rates = ROPE_BASE ** (-(lanes * 2.0) / HEAD)
    near = np.arange(rows)[:, None] * rates[None, :]
    far = (np.arange(shards_in_sequence) * rows)[:, None] * rates[None, :]
    shift = np.concatenate([np.cos(far), np.sin(far)], axis=0)
    return (
        np.cos(near).astype(np.float32),
        np.sin(near).astype(np.float32),
        shift.astype(np.float32),
    )


def tensor_peer(t, m):
    if m == 1:
        return t + 1 - 2 * lax.rem(t, 2)
    if m == 2:
        return lax.rem(t + 2, 4)
    return 3 - t


def dp_peer(d, m):
    if m & 1:
        d = d + 1 - 2 * lax.rem(d, 2)
    if m & 2:
        d = d + 2 - 4 * lax.rem(lax.div(d, 2), 2)
    if m & 4:
        d = lax.rem(d + 4, 8)
    return d


class Links:
    def __init__(self, tsend, trecv, dsend, drecv):
        self.t = lax.axis_index("tensor")
        self.d = lax.axis_index("dp")
        self.mid = lax.rem(lax.div(self.t + 1, 2), 2)
        self.tsend, self.trecv, self.dsend, self.drecv = tsend, trecv, dsend, drecv

    def shard_at(self, i):
        t, mid = self.t, self.mid
        near, two, three = (tensor_peer(t, m) for m in (1, 2, 3))
        if isinstance(i, int):
            if i == 0:
                return t, 0
            if i == 1:
                return near, 1
            if i == 2:
                return two + mid * (three - two), 2 + mid
            return three + mid * (two - three), 3 - mid
        one_if = [1 - jnp.minimum(jnp.abs(i - k), 1) for k in range(4)]
        pairs = [self.shard_at(k) for k in range(4)]
        return (
            sum(f * p[0] for f, p in zip(one_if, pairs)),
            sum(f * p[1] for f, p in zip(one_if, pairs)),
        )

    def over_tensor(self, kind, m, src, dst, recv=None):
        peer = tensor_peer(self.t, m)
        return pltpu.make_async_remote_copy(
            src_ref=src,
            dst_ref=dst,
            send_sem=self.tsend.at[kind, m],
            recv_sem=self.trecv.at[kind, m if recv is None else recv],
            device_id={"dp": self.d, "tensor": peer},
            device_id_type=MESH,
        )

    def over_dp(self, kind, m, src, dst, to=None):
        peer = dp_peer(self.d, m if to is None else to)
        return pltpu.make_async_remote_copy(
            src_ref=src,
            dst_ref=dst,
            send_sem=self.dsend.at[kind, m],
            recv_sem=self.drecv.at[kind, m],
            device_id={"dp": peer, "tensor": self.t},
            device_id_type=MESH,
        )

    def landed_tensor(self, kind, m, ref):
        pltpu.make_async_copy(ref, ref, self.trecv.at[kind, m]).wait()

    def landed_dp(self, kind, m, ref):
        pltpu.make_async_copy(ref, ref, self.drecv.at[kind, m]).wait()

    def gather_start(self, kind, src, at):
        own = at(self.t)
        self.over_tensor(kind, 1, src, own).start()

        @pl.when(self.mid == 0)
        def _():
            self.over_tensor(kind, 2, src, own).start()

        @pl.when(self.mid == 1)
        def _():
            self.over_tensor(kind, 3, src, own).start()

    def gather_take(self, kind, i, at):
        shard, m = self.shard_at(i)
        block = at(shard)
        self.landed_tensor(kind, m, block)

        def hand_on():
            pltpu.make_async_remote_copy(
                src_ref=block,
                dst_ref=block,
                send_sem=self.tsend.at[kind, 2 + i],
                recv_sem=self.trecv.at[kind, 5 - m],
                device_id={"dp": self.d, "tensor": tensor_peer(self.t, 1)},
                device_id_type=MESH,
            ).start()

        if isinstance(i, int):
            if i >= 2:
                pl.when(self.mid == 1)(hand_on)
        else:
            pl.when((self.mid == 1) & (i >= 2))(hand_on)

    def gather_end(self, kind, src, at):
        own = at(self.t)
        self.over_tensor(kind, 1, src, own).wait_send()

        @pl.when(self.mid == 0)
        def _():
            self.over_tensor(kind, 2, src, own).wait_send()

        @pl.when(self.mid == 1)
        def _():
            self.over_tensor(kind, 3, src, own).wait_send()
            for i in (2, 3):
                shard, m = self.shard_at(i)
                pltpu.make_async_copy(at(shard), at(shard), self.tsend.at[kind, 2 + i]).wait()

    def barrier(self, tensor_peers, dp_peers):
        sem = pltpu.get_barrier_semaphore()
        for m in tensor_peers:
            pl.semaphore_signal(
                sem,
                inc=1,
                device_id={"dp": self.d, "tensor": tensor_peer(self.t, m)},
                device_id_type=MESH,
            )
        for m in dp_peers:
            pl.semaphore_signal(
                sem,
                inc=1,
                device_id={"dp": dp_peer(self.d, m), "tensor": self.t},
                device_id_type=MESH,
            )
        pl.semaphore_wait(sem, len(tensor_peers) + len(dp_peers))


def mm(a, b, dims=((1,), (0,))):
    return lax.dot_general(a, b, (dims, ((), ())), preferred_element_type=F32)


NN = ((1,), (0,))
NT = ((1,), (1,))
TN = ((0,), (0,))


def lane_roll(u, by):
    return pltpu.roll(u, by % u.shape[-1], u.ndim - 1)


def swap_halves(u):
    lane = lax.broadcasted_iota(jnp.int32, u.shape, 1)
    low = lax.rem(lane, HEAD) < HEAD // 2
    return jnp.where(low, -lane_roll(u, -(HEAD // 2)), lane_roll(u, HEAD // 2))


def turn_tables(near_cos, near_sin, shift, shard):
    c = shift[pl.ds(shard, 1), :]
    s = shift[pl.ds(shard + 4, 1), :]
    a, b = near_cos[...], near_sin[...]
    return a * c - b * s, b * c + a * s


def front_kernel(
    hid, cot, tile, wpack, wo, near_cos, near_sin, shift,
    normed_out, w_out, wo_out, heads_out, lse_out, start_out, cot_out, rows_out, resid_out,
    normed2_out, gains_out,
    xall, nall, call, w, wof, tiles, qh, kh, vh, att, arow, outh, lse, start, gains, resid, normed2,
    tsend, trecv, dsend, drecv, local, store,
):
    ln = Links(tsend, trecv, dsend, drecv)
    t, d = ln.t, ln.d
    rows = hid.shape[0]
    width = hid.shape[1]
    wrows = wo.shape[0]
    srows = 4 * wrows
    TILE, W, X, O, C, A = range(6)
    DT, DW, FW, DO, FO = range(5)

    def rows_at(ref, shard):
        return ref.at[pl.ds(pl.multiple_of(shard * rows, rows), rows), :]

    def w_at(ref, dd, tt=None):
        if tt is None:
            return ref.at[pl.ds(pl.multiple_of(dd * srows, 16), srows), :]
        return ref.at[pl.ds(pl.multiple_of(dd * srows + tt * wrows, 16), wrows), :]

    x_of = functools.partial(rows_at, xall)
    c_of = functools.partial(rows_at, call)

    def wo_of(tt):
        return w_at(wof, d, tt)

    mine = [
        pltpu.make_async_copy(tile, tiles.at[d, t], local.at[0]),
        pltpu.make_async_copy(wpack.at[t], w_at(w, d, t), local.at[1]),
        pltpu.make_async_copy(wo, wo_of(t), local.at[2]),
        pltpu.make_async_copy(hid, x_of(t), local.at[3]),
        pltpu.make_async_copy(cot, c_of(t), local.at[4]),
    ]
    for c in mine:
        c.start()
    ln.barrier((1, 2, 3), (1, 2, 3, 4, 5, 6, 7))
    for m in (1, 2, 3):
        ln.over_tensor(TILE, m, tile, tiles.at[d, t]).start()
    for m in (1, 2, 3):
        ln.over_tensor(W, m, wpack.at[tensor_peer(t, m)], w_at(w, d, t)).start()
    ln.gather_start(O, wo, wo_of)
    ln.gather_start(X, hid, x_of)

    mine[0].wait()
    for m in (1, 2, 3):
        ln.landed_tensor(TILE, m, tiles.at[d, tensor_peer(t, m)])
    for m in range(1, 8):
        ln.over_dp(DT, m, tiles.at[d], tiles.at[d]).start()
    mine[1].wait()
    for m in (1, 2, 3):
        ln.landed_tensor(W, m, w_at(w, d, tensor_peer(t, m)))
    for m in (2, 4, 6, 1):
        ln.over_dp(DW, m, w_at(w, d), w_at(w, d)).start()
    mine[2].wait()
    for i in (1, 2, 3):
        ln.gather_take(O, i, wo_of)
    for m in (2, 4, 6, 1):
        ln.over_dp(DO, m, w_at(wof, d), w_at(wof, d)).start()
    for m in range(1, 8):
        ln.landed_dp(DT, m, tiles.at[dp_peer(d, m)])
    for m in (2, 4, 6):
        dd = dp_peer(d, m)
        ln.landed_dp(DW, m, w_at(w, dd))
        ln.over_dp(FW, m, w_at(w, dd), w_at(w, dd), to=1).start()

    for g in range(4):
        acc = jnp.zeros((8, 8 * wrows), F32)
        for j in range(8):
            r = 8 * g + j
            piece = jnp.concatenate(
                [tiles[r // 4, r % 4], jnp.zeros((8, 8 * wrows - 128), F32)], axis=1
            )
            acc = acc + lane_roll(piece, wrows * j)
        gains[:, g * 8 * wrows : (g + 1) * 8 * wrows] = acc
    for s in range(4):
        start[:, s * rows : (s + 1) * rows] = tiles[d, s, 2:3, :]

    mine[3].wait()
    for i in (1, 2, 3):
        ln.gather_take(X, i, x_of)
    mine[4].wait()
    ln.gather_start(C, cot, c_of)
    for m in (1,):
        ln.landed_dp(DW, m, w_at(w, dp_peer(d, m)))
    for m in (2, 4, 6):
        ln.landed_dp(FW, m, w_at(w, dp_peer(d, m ^ 1)))

    def project(s, carry):
        at = pl.ds(pl.multiple_of(s * rows, rows), rows)
        x = xall[at, :].astype(F32)
        inv = lax.rsqrt(jnp.mean(x * x, axis=1, keepdims=True) + EPSILON)
        normed = (x * inv * gains[0:1, :]).astype(BF16)
        nall[at, :] = normed
        cosine, sine = turn_tables(near_cos, near_sin, shift, s)
        q = mm(normed, w[:, : 4 * HEAD])
        q = q * cosine + swap_halves(q) * sine
        kv = mm(normed, w[:, 4 * HEAD :])
        lane = lax.broadcasted_iota(jnp.int32, kv.shape, 1)
        kv = jnp.where(lane < 2 * HEAD, kv * cosine + swap_halves(kv) * sine, kv)
        keep = lax.broadcasted_iota(jnp.int32, (rows, 128), 1) < HEAD
        for h in range(4):
            qh[h, at, :] = jnp.where(keep, lane_roll(q, -HEAD * h)[:, :128], 0.0).astype(BF16)
        for c in range(2):
            kh[c, at, :] = jnp.where(keep, lane_roll(kv, -HEAD * c)[:, :128], 0.0).astype(BF16)
            vh[c, at, :] = jnp.where(keep, lane_roll(kv, -HEAD * (c + 2))[:, :128], 0.0).astype(BF16)
        return carry

    lax.fori_loop(0, 4, project, 0)

    def forward_wo(m):
        dd = dp_peer(d, m)
        ln.landed_dp(DO, m, w_at(wof, dd))
        ln.over_dp(FO, m, w_at(wof, dd), w_at(wof, dd), to=1).start()

    scale = 1.0 / math.sqrt(HEAD)

    def attend(h, carry):
        c = lax.div(h, 2)
        for b in range(4):
            span = (b + 1) * rows
            sc = mm(kh[c, :span, :], qh[h, b * rows : span, :], NT) * scale
            key = lax.broadcasted_iota(jnp.int32, sc.shape, 0)
            query = lax.broadcasted_iota(jnp.int32, sc.shape, 1) + b * rows
            first = start[:, b * rows : span].astype(jnp.int32)
            sc = jnp.where((key <= query) & (key >= first), sc, MASKED)
            peak = jnp.max(sc, axis=0, keepdims=True)
            e = jnp.exp(sc - peak)
            total = jnp.sum(e, axis=0, keepdims=True)
            p = (e * (1.0 / total)).astype(BF16)
            outh[h, b * rows : span, :] = mm(p, vh[c, :span, :], TN)
            lse[h, :, b * rows : span] = peak + jnp.log(total)
        return carry

    lax.fori_loop(0, 4, attend, 0)

    def pack(b, carry):
        at = pl.ds(pl.multiple_of(b * rows, rows), rows)
        acc = jnp.zeros((rows, 4 * HEAD), F32)
        for h in range(4):
            piece = jnp.concatenate([outh[h, at, :], jnp.zeros((rows, 4 * HEAD - 128), F32)], axis=1)
            acc = acc + lane_roll(piece, HEAD * h)
        att[b] = acc.astype(BF16)
        return carry

    lax.fori_loop(0, 4, pack, 0)

    def columns(tt):
        return arow.at[:, pl.ds(pl.multiple_of(tt * 4 * HEAD, 128), 4 * HEAD)]

    for m in (1, 2, 3):
        ln.over_tensor(A, m, att.at[tensor_peer(t, m)], columns(t)).start()
    own = pltpu.make_async_copy(att.at[t], columns(t), local.at[0])
    own.start()
    for m in (2, 4, 6):
        forward_wo(m)
    ln.landed_dp(DO, 1, w_at(wof, dp_peer(d, 1)))
    for m in (2, 4, 6):
        ln.landed_dp(FO, m, w_at(wof, dp_peer(d, m ^ 1)))
    own.wait()
    for m in (1, 2, 3):
        ln.landed_tensor(A, m, columns(tensor_peer(t, m)))

    at = pl.ds(pl.multiple_of(t * rows, rows), rows)
    third = width // 3

    def project_out(n, carry):
        cols = pl.ds(pl.multiple_of(n * third, 128), third)
        resid[:, cols] = xall[at, cols].astype(F32) + mm(arow[...], wof[:, cols])
        return carry

    lax.fori_loop(0, 3, project_out, 0)
    r = resid[...]
    inv = lax.rsqrt(jnp.mean(r * r, axis=1, keepdims=True) + EPSILON)
    normed2[...] = (r * inv * gains[1:2, :]).astype(BF16)

    for i in (1, 2, 3):
        ln.gather_take(C, i, c_of)

    results = [
        (nall, normed_out), (w, w_out), (wof, wo_out), (qh, heads_out.at[0:4]),
        (kh, heads_out.at[4:6]), (vh, heads_out.at[6:8]), (lse, lse_out), (start, start_out),
        (call, cot_out), (arow, rows_out), (resid, resid_out), (normed2, normed2_out),
        (gains, gains_out),
    ]
    stores = [pltpu.make_async_copy(a, b, store.at[i]) for i, (a, b) in enumerate(results)]
    for c in stores:
        c.start()
    for m in (1, 2, 3):
        ln.over_tensor(TILE, m, tile, tiles.at[d, t]).wait_send()
        ln.over_tensor(W, m, wpack.at[tensor_peer(t, m)], w_at(w, d, t)).wait_send()
        ln.over_tensor(A, m, att.at[tensor_peer(t, m)], columns(t)).wait_send()
    ln.gather_end(O, wo, wo_of)
    ln.gather_end(X, hid, x_of)
    ln.gather_end(C, cot, c_of)
    for m in range(1, 8):
        ln.over_dp(DT, m, tiles.at[d], tiles.at[d]).wait_send()
    for m in (2, 4, 6, 1):
        ln.over_dp(DW, m, w_at(w, d), w_at(w, d)).wait_send()
        ln.over_dp(DO, m, w_at(wof, d), w_at(wof, d)).wait_send()
    for m in (2, 4, 6):
        dd = dp_peer(d, m)
        ln.over_dp(FW, m, w_at(w, dd), w_at(w, dd), to=1).wait_send()
        ln.over_dp(FO, m, w_at(wof, dd), w_at(wof, dd), to=1).wait_send()
    for c in stores:
        c.wait()


def front(hid, cot, positions, gain_attn, gain_mlp, wq, wk, wv, wo):
    rows, width = hid.shape
    wrows = wq.shape[0]
    seq = 4 * rows
    t = lax.axis_index("tensor")
    index = t * rows + jnp.arange(rows, dtype=jnp.int32)
    pad = (0, 128 - wrows)
    tile = jnp.stack(
        [
            jnp.pad(gain_attn.astype(F32), pad),
            jnp.pad(gain_mlp.astype(F32), pad),
            (index - positions).astype(F32),
        ]
        + [jnp.zeros((128,), F32)] * 5
    )
    wpack = jnp.concatenate(
        [a.reshape(wrows, 4, a.shape[1] // 4).transpose(1, 0, 2) for a in (wq, wk, wv)], axis=2
    )
    near_cos, near_sin, shift = rotary_tables(rows, 4)
    hbm = pl.BlockSpec(memory_space=pl.ANY)
    vmem = pl.BlockSpec(memory_space=pltpu.VMEM)
    sds = jax.ShapeDtypeStruct
    shapes = dict(
        normed=((seq, width), BF16), w=((width, 8 * HEAD), BF16), wo=((width, width), BF16),
        heads=((8, seq, 128), BF16), lse=((4, 1, seq), F32), start=((1, seq), F32),
        cot=((seq, width), BF16), rows=((rows, width), BF16), resid=((rows, width), F32),
        normed2=((rows, width), BF16), gains=((8, width), F32),
    )
    S = {k: pltpu.VMEM(*v) for k, v in shapes.items()}
    outs = pl.pallas_call(
        front_kernel,
        out_shape=[sds(*v) for v in shapes.values()],
        in_specs=[hbm] * 5 + [vmem] * 3,
        out_specs=[hbm] * len(shapes),
        scratch_shapes=[
            pltpu.VMEM((seq, width), BF16),
            S["normed"], S["cot"], S["w"], S["wo"],
            pltpu.VMEM((8, 4, 8, 128), F32),
            pltpu.VMEM((4, seq, 128), BF16), pltpu.VMEM((2, seq, 128), BF16),
            pltpu.VMEM((2, seq, 128), BF16),
            pltpu.VMEM((4, rows, 4 * HEAD), BF16),
            S["rows"],
            pltpu.VMEM((4, seq, 128), F32),
            S["lse"], S["start"], S["gains"], S["resid"], S["normed2"],
            pltpu.SemaphoreType.DMA((6, 6)), pltpu.SemaphoreType.DMA((6, 4)),
            pltpu.SemaphoreType.DMA((5, 8)), pltpu.SemaphoreType.DMA((5, 8)),
            pltpu.SemaphoreType.DMA((5,)), pltpu.SemaphoreType.DMA((13,)),
        ],
        name="front",
        compiler_params=pltpu.CompilerParams(
            collective_id=0, has_side_effects=True, vmem_limit_bytes=VMEM_LIMIT
        ),
    )(hid, cot, tile, wpack, wo, near_cos, near_sin, shift)
    return dict(zip(shapes, outs))


QUERY_HEADS = 16
KEY_VALUE_HEADS = 8
HEAD_DIMENSION = 96


def angle_tables(pos_rows, head_size):
    half_size = head_size // 2
    freq_rates = ROPE_BASE ** (-(jnp.arange(half_size, dtype=jnp.float32) * 2.0) / head_size)
    turned = pos_rows.astype(jnp.float32)[:, None] * freq_rates[None, :]
    return (jnp.cos(turned)[:, None, :], jnp.sin(turned)[:, None, :])


def apply_rotary(tensor_in, cosine_table, sine_table):
    half_size = tensor_in.shape[-1] // 2
    lo_half = tensor_in[..., :half_size]
    hi_half = tensor_in[..., half_size:]
    return jnp.concatenate(
        [
            lo_half * cosine_table - hi_half * sine_table,
            hi_half * cosine_table + lo_half * sine_table,
        ],
        axis=-1,
    )


def shards(
    hidden_in,
    positions,
    gain_attn,
    w_query,
    key_matrix,
    value_matrix,
    w_output,
    gain_mlp,
    w_gate,
    w_up,
    w_down,
    cotangent,
):
    tok_rows = hidden_in.shape[0]
    model_width = hidden_in.shape[1]
    num_heads = QUERY_HEADS
    key_value_count = KEY_VALUE_HEADS
    head_size = HEAD_DIMENSION
    kv_width = key_value_count * head_size
    queries_per_group = num_heads // key_value_count
    seq_len = tok_rows * lax.axis_size("tensor")
    score_scale = 1.0 / math.sqrt(head_size)
    gathered = (
        lax.all_gather(gain_attn, ("dp", "tensor"), axis=0, tiled=True),
        lax.all_gather(w_query, ("dp", "tensor"), axis=0, tiled=True),
        lax.all_gather(key_matrix, ("dp", "tensor"), axis=0, tiled=True),
        lax.all_gather(value_matrix, ("dp", "tensor"), axis=0, tiled=True),
        lax.all_gather(w_output, ("dp", "tensor"), axis=0, tiled=True),
        lax.all_gather(gain_mlp, ("dp", "tensor"), axis=0, tiled=True),
    )
    gain_one, query_full, key_full, value_full, output_full, gain_two = gathered
    gain_one_f = gain_one.astype(jnp.float32)
    gain_two_f = gain_two.astype(jnp.float32)
    x_float = hidden_in.astype(jnp.float32)
    inv_one = lax.rsqrt(jnp.mean(x_float * x_float, axis=-1, keepdims=True) + EPSILON)
    normed_one = (x_float * inv_one * gain_one_f).astype(jnp.bfloat16)
    queries = jnp.dot(normed_one, query_full, preferred_element_type=jnp.float32)
    key_projected = jnp.dot(normed_one, key_full, preferred_element_type=jnp.float32)
    value_proj = jnp.dot(normed_one, value_full, preferred_element_type=jnp.float32)
    cosine_table, sine_table = angle_tables(positions, head_size)
    rotated_query_rows = apply_rotary(
        queries.reshape(tok_rows, num_heads, head_size), cosine_table, sine_table
    ).astype(jnp.bfloat16)
    rotated_key_rows = (
        apply_rotary(
            key_projected.reshape(tok_rows, key_value_count, head_size), cosine_table, sine_table
        )
        .astype(jnp.bfloat16)
        .reshape(tok_rows, kv_width)
    )
    value_rows_lowered = value_proj.astype(jnp.bfloat16)
    keys_all, values_all = (
        lax.all_gather(rotated_key_rows, "tensor", axis=0, tiled=True),
        lax.all_gather(value_rows_lowered, "tensor", axis=0, tiled=True),
    )
    offset = lax.axis_index("tensor") * tok_rows
    query_index = offset + jnp.arange(tok_rows, dtype=jnp.int32)
    key_index = jnp.arange(seq_len, dtype=jnp.int32)
    visible = (key_index[None, :] <= query_index[:, None]) & (
        key_index[None, :] >= (query_index - positions)[:, None]
    )
    visible = jnp.tile(visible, (queries_per_group, 1))

    def split_queries(tensor_in):
        return (
            tensor_in.reshape(tok_rows, key_value_count, queries_per_group, head_size)
            .transpose(1, 2, 0, 3)
            .reshape(key_value_count, queries_per_group * tok_rows, head_size)
        )

    def split_keys(tensor_in):
        return tensor_in.reshape(seq_len, key_value_count, head_size).transpose(1, 0, 2)

    def merge_heads(tensor_in):
        return (
            tensor_in.reshape(key_value_count, queries_per_group, tok_rows, head_size)
            .transpose(2, 0, 1, 3)
            .reshape(tok_rows, model_width)
        )

    query_heads = split_queries(rotated_query_rows)
    k_heads = split_keys(keys_all)
    value_heads = split_keys(values_all)

    def attend(head_items):
        q_block, k_block, v_block = head_items
        scores = (
            jnp.einsum("qd,kd->qk", q_block, k_block, preferred_element_type=jnp.float32)
            * score_scale
        )
        scores = jnp.where(visible, scores, MASKED)
        peak = jnp.max(scores, axis=-1, keepdims=True)
        exp_vals = jnp.exp(scores - peak)
        total = jnp.sum(exp_vals, axis=-1, keepdims=True)
        probs = exp_vals / total
        out_block = jnp.einsum(
            "qk,kd->qd", probs.astype(jnp.bfloat16), v_block, preferred_element_type=jnp.float32
        )
        return (out_block, peak[:, 0] + jnp.log(total[:, 0]))

    attended_rows, log_total = lax.map(attend, (query_heads, k_heads, value_heads))
    attended_low = merge_heads(attended_rows).astype(jnp.bfloat16)
    resid_sum = x_float + jnp.dot(attended_low, output_full, preferred_element_type=jnp.float32)
    inv_two = lax.rsqrt(jnp.mean(resid_sum * resid_sum, axis=-1, keepdims=True) + EPSILON)
    normed_two = (resid_sum * inv_two * gain_two_f).astype(jnp.bfloat16)
    rows_all = lax.all_gather(normed_two, "tensor", axis=0, tiled=True)
    gate_val = jnp.dot(rows_all, w_gate, preferred_element_type=jnp.float32)
    up_val = jnp.dot(rows_all, w_up, preferred_element_type=jnp.float32)
    sig_gate = jax.nn.sigmoid(gate_val)
    silu_gate = gate_val * sig_gate
    act_low = (silu_gate * up_val).astype(jnp.bfloat16)
    mlp_sum = lax.psum_scatter(
        jnp.dot(act_low, w_down, preferred_element_type=jnp.float32).astype(jnp.bfloat16),
        "tensor",
        scatter_dimension=0,
        tiled=True,
    ).astype(jnp.float32)
    layer_out = (resid_sum + mlp_sum).astype(jnp.bfloat16)
    grad_float = cotangent.astype(jnp.float32)
    grad_all = lax.all_gather(cotangent, "tensor", axis=0, tiled=True)
    grad_down = jnp.einsum("sf,sd->fd", act_low, grad_all, preferred_element_type=jnp.float32)
    g_act = jnp.einsum("sd,fd->sf", grad_all, w_down, preferred_element_type=jnp.float32)
    g_gate = (g_act * up_val * sig_gate * (1.0 + gate_val * (1.0 - sig_gate))).astype(jnp.bfloat16)
    g_up = (g_act * silu_gate).astype(jnp.bfloat16)
    grad_gate = jnp.einsum("sd,sf->df", rows_all, g_gate, preferred_element_type=jnp.float32)
    grad_up = jnp.einsum("sd,sf->df", rows_all, g_up, preferred_element_type=jnp.float32)
    g_norm_two = lax.psum_scatter(
        (
            jnp.einsum("sf,df->sd", g_gate, w_gate, preferred_element_type=jnp.float32)
            + jnp.einsum("sf,df->sd", g_up, w_up, preferred_element_type=jnp.float32)
        ).astype(jnp.bfloat16),
        "tensor",
        scatter_dimension=0,
        tiled=True,
    ).astype(jnp.float32)
    scaled_two = gain_two_f * g_norm_two
    grad_gain_two = jnp.sum(g_norm_two * resid_sum * inv_two, axis=0)
    g_resid = (
        grad_float
        + inv_two * scaled_two
        - resid_sum * inv_two**3 * jnp.mean(scaled_two * resid_sum, axis=-1, keepdims=True)
    )
    g_resid_low = g_resid.astype(jnp.bfloat16)
    grad_output = jnp.einsum(
        "tc,td->cd", attended_low, g_resid_low, preferred_element_type=jnp.float32
    )
    g_att = jnp.einsum(
        "td,cd->tc", g_resid_low, output_full, preferred_element_type=jnp.float32
    ).astype(jnp.bfloat16)
    g_heads = split_queries(g_att)

    def attend_back(head_items):
        q_block, k_block, v_block, log_block, g_block = head_items
        scores = (
            jnp.einsum("qd,kd->qk", q_block, k_block, preferred_element_type=jnp.float32)
            * score_scale
        )
        scores = jnp.where(visible, scores, MASKED)
        probs = jnp.exp(scores - log_block[:, None])
        g_probs = jnp.einsum("qd,kd->qk", g_block, v_block, preferred_element_type=jnp.float32)
        g_scores = (probs * (g_probs - jnp.sum(probs * g_probs, axis=-1, keepdims=True))).astype(
            jnp.bfloat16
        )
        g_rq = (
            jnp.einsum("qk,kd->qd", g_scores, k_block, preferred_element_type=jnp.float32)
            * score_scale
        )
        g_rk = (
            jnp.einsum("qk,qd->kd", g_scores, q_block, preferred_element_type=jnp.float32)
            * score_scale
        )
        g_val = jnp.einsum(
            "qk,qd->kd", probs.astype(jnp.bfloat16), g_block, preferred_element_type=jnp.float32
        )
        return (g_rq, g_rk, g_val)

    g_rq, g_rk, g_val = lax.map(
        attend_back, (query_heads, k_heads, value_heads, log_total, g_heads)
    )
    g_rk_flat = g_rk.transpose(1, 0, 2).reshape(seq_len, kv_width)
    g_val_flat = g_val.transpose(1, 0, 2).reshape(seq_len, kv_width)
    key_part, value_part = (
        lax.psum_scatter(
            g_rk_flat.astype(jnp.bfloat16), "tensor", scatter_dimension=0, tiled=True
        ).astype(jnp.float32),
        lax.psum_scatter(
            g_val_flat.astype(jnp.bfloat16), "tensor", scatter_dimension=0, tiled=True
        ).astype(jnp.float32),
    )
    g_queries = (
        apply_rotary(
            merge_heads(g_rq).reshape(tok_rows, num_heads, head_size), cosine_table, -sine_table
        )
        .reshape(tok_rows, model_width)
        .astype(jnp.bfloat16)
    )
    g_keys = (
        apply_rotary(
            key_part.reshape(tok_rows, key_value_count, head_size), cosine_table, -sine_table
        )
        .reshape(tok_rows, kv_width)
        .astype(jnp.bfloat16)
    )
    g_values = value_part.astype(jnp.bfloat16)
    grad_query = jnp.einsum("tc,td->cd", normed_one, g_queries, preferred_element_type=jnp.float32)
    grad_key = jnp.einsum("tc,td->cd", normed_one, g_keys, preferred_element_type=jnp.float32)
    grad_value = jnp.einsum("tc,td->cd", normed_one, g_values, preferred_element_type=jnp.float32)
    g_norm_one = (
        jnp.einsum("td,cd->tc", g_queries, query_full, preferred_element_type=jnp.float32)
        + jnp.einsum("td,cd->tc", g_keys, key_full, preferred_element_type=jnp.float32)
        + jnp.einsum("td,cd->tc", g_values, value_full, preferred_element_type=jnp.float32)
    )
    scaled_one = gain_one_f * g_norm_one
    grad_gain_one = jnp.sum(g_norm_one * x_float * inv_one, axis=0)
    grad_input = (
        g_resid
        + inv_one * scaled_one
        - x_float * inv_one**3 * jnp.mean(scaled_one * x_float, axis=-1, keepdims=True)
    )
    packed = jnp.concatenate([grad_query, grad_key, grad_value, grad_output], axis=1)
    packed_part = lax.psum_scatter(
        packed.astype(jnp.bfloat16), ("dp", "tensor"), scatter_dimension=0, tiled=True
    ).astype(jnp.float32)
    query_part = packed_part[:, :model_width]
    keyw_part = packed_part[:, model_width : model_width + kv_width]
    valuew_part = packed_part[:, model_width + kv_width : model_width + 2 * kv_width]
    out_part = packed_part[:, model_width + 2 * kv_width :]
    gain_one_part, gain_two_part = (
        lax.psum_scatter(grad_gain_one, ("dp", "tensor"), scatter_dimension=0, tiled=True),
        lax.psum_scatter(grad_gain_two, ("dp", "tensor"), scatter_dimension=0, tiled=True),
    )
    gate_sum, up_sum, down_sum = (
        lax.psum_scatter(
            grad_gate.astype(jnp.bfloat16), "dp", scatter_dimension=0, tiled=True
        ).astype(jnp.float32),
        lax.psum_scatter(
            grad_up.astype(jnp.bfloat16), "dp", scatter_dimension=0, tiled=True
        ).astype(jnp.float32),
        lax.psum_scatter(
            grad_down.astype(jnp.bfloat16), "dp", scatter_dimension=1, tiled=True
        ).astype(jnp.float32),
    )
    return (
        layer_out,
        grad_input,
        gain_one_part,
        query_part,
        keyw_part,
        valuew_part,
        out_part,
        gain_two_part,
        gate_sum,
        up_sum,
        down_sum,
    )


def rest_of_layer(hidden, gain_one_rows, o, w_gate, w_up, w_down):
    rows, width = hidden.shape
    seq = 4 * rows
    gain_one, gain_two = o["gains"][0:1], o["gains"][1:2]
    resid, normed_two = o["resid"], o["normed2"]
    grad_all = o["cot"]
    t = lax.axis_index("tensor")
    grad_float = lax.dynamic_slice_in_dim(grad_all, t * rows, rows, 0).astype(F32)

    def over_tokens(a):
        return lax.psum_scatter(
            a.astype(BF16), "tensor", scatter_dimension=0, tiled=True
        ).astype(F32)

    def dot(spec, a, b):
        return jnp.einsum(spec, a, b, preferred_element_type=F32)

    inv_two = lax.rsqrt(jnp.mean(resid * resid, axis=-1, keepdims=True) + EPSILON)
    rows_all = lax.all_gather(normed_two, "tensor", axis=0, tiled=True)
    gate = dot("sd,df->sf", rows_all, w_gate)
    up = dot("sd,df->sf", rows_all, w_up)
    sig = jax.nn.sigmoid(gate)
    silu = gate * sig
    act = (silu * up).astype(BF16)
    g_act = dot("sd,fd->sf", grad_all, w_down)
    g_gate = (g_act * up * sig * (1.0 + gate * (1.0 - sig))).astype(BF16)
    g_up = (g_act * silu).astype(BF16)
    g_norm_two = over_tokens(dot("sf,df->sd", g_gate, w_gate) + dot("sf,df->sd", g_up, w_up))
    layer_out = (resid + over_tokens(dot("sf,fd->sd", act, w_down))).astype(BF16)
    scaled = gain_two * g_norm_two
    g_resid = (
        grad_float
        + inv_two * scaled
        - resid * inv_two**3 * jnp.mean(scaled * resid, axis=-1, keepdims=True)
    )
    g_resid_low = g_resid.astype(BF16)
    gain_two_grad = jnp.sum(g_norm_two * resid * inv_two, axis=0)
    grad_out = dot("tc,td->cd", o["rows"], g_resid_low)
    g_att = dot("td,cd->tc", g_resid_low, o["wo"]).astype(BF16)
    g_att = lax.all_to_all(g_att, "tensor", split_axis=1, concat_axis=0, tiled=True)
    g_heads = g_att.reshape(seq, 4, HEAD).transpose(1, 0, 2)
    q = o["heads"][0:4, :, :HEAD]
    k = jnp.repeat(o["heads"][4:6, :, :HEAD], 2, axis=0)
    v = jnp.repeat(o["heads"][6:8, :, :HEAD], 2, axis=0)
    scale = 1.0 / math.sqrt(HEAD)
    index = jnp.arange(seq, dtype=jnp.int32)
    first = o["start"][0].astype(jnp.int32)
    visible = (index[None, :] <= index[:, None]) & (index[None, :] >= first[:, None])
    scores = jnp.where(visible[None], dot("hqd,hkd->hqk", q, k) * scale, MASKED)
    probs = jnp.exp(scores - o["lse"][:, 0, :, None])
    g_probs = dot("hqd,hkd->hqk", g_heads, v)
    g_scores = (probs * (g_probs - jnp.sum(probs * g_probs, axis=-1, keepdims=True))).astype(BF16)
    g_rq = dot("hqk,hkd->hqd", g_scores, k) * scale
    g_rk = dot("hqk,hqd->hkd", g_scores, q) * scale
    g_v = dot("hqk,hqd->hkd", probs.astype(BF16), g_heads)
    g_rk = g_rk.reshape(2, 2, seq, HEAD).sum(1)
    g_v = g_v.reshape(2, 2, seq, HEAD).sum(1)
    rates = ROPE_BASE ** (-(jnp.arange(HEAD // 2, dtype=F32) * 2.0) / HEAD)
    turned = index.astype(F32)[:, None] * rates[None, :]
    cosine, sine = jnp.cos(turned), jnp.sin(turned)

    def turn_back(u):
        a, b = u[..., : HEAD // 2], u[..., HEAD // 2 :]
        return jnp.concatenate([a * cosine + b * sine, b * cosine - a * sine], axis=-1)

    g = jnp.concatenate([turn_back(g_rq), turn_back(g_rk), g_v], axis=0).astype(BF16)
    g = g.transpose(1, 0, 2).reshape(seq, 8 * HEAD)
    grad_w = dot("sc,sd->cd", o["normed"], g)
    g_norm_one = over_tokens(dot("sd,cd->sc", g, o["w"]))
    x = hidden.astype(F32)
    inv_one = lax.rsqrt(jnp.mean(x * x, axis=-1, keepdims=True) + EPSILON)
    scaled = gain_one * g_norm_one
    grad_input = (
        g_resid + inv_one * scaled - x * inv_one**3 * jnp.mean(scaled * x, axis=-1, keepdims=True)
    )
    gain_one_grad = jnp.sum(g_norm_one * x * inv_one, axis=0)
    gains = lax.psum_scatter(
        jnp.stack([gain_one_grad, gain_two_grad], axis=1),
        ("dp", "tensor"), scatter_dimension=0, tiled=True,
    )
    grad_w = lax.psum_scatter(grad_w.astype(BF16), "dp", scatter_dimension=0, tiled=True)
    wrows = grad_w.shape[0] // 4
    grad_w = lax.all_to_all(
        grad_w.reshape(4, wrows, 8 * HEAD), "tensor", split_axis=0, concat_axis=0, tiled=True
    )
    grad_w = grad_w.astype(F32).transpose(1, 0, 2)
    query = grad_w[:, :, : 4 * HEAD].reshape(wrows, 16 * HEAD)
    key = grad_w[:, :, 4 * HEAD : 6 * HEAD].reshape(wrows, 8 * HEAD)
    value = grad_w[:, :, 6 * HEAD :].reshape(wrows, 8 * HEAD)
    out = lax.psum_scatter(
        grad_out.astype(BF16), ("dp", "tensor"), scatter_dimension=0, tiled=True
    ).astype(F32)

    def owners(a, dim):
        return lax.psum_scatter(
            a.astype(BF16), "dp", scatter_dimension=dim, tiled=True
        ).astype(F32)

    gate_sum = owners(dot("sd,sf->df", rows_all, g_gate), 0)
    up_sum = owners(dot("sd,sf->df", rows_all, g_up), 0)
    down_sum = owners(dot("sf,sd->fd", act, grad_all), 1)
    return (
        layer_out, grad_input, gains[:, 0], query, key, value, out, gains[:, 1],
        gate_sum, up_sum, down_sum,
    )


def fast_shards(
    hidden_in, positions, gain_attn, w_query, key_matrix, value_matrix, w_output, gain_mlp,
    w_gate, w_up, w_down, cotangent,
):
    o = front(
        hidden_in, cotangent, positions, gain_attn, gain_mlp, w_query, key_matrix, value_matrix,
        w_output,
    )
    return rest_of_layer(hidden_in, gain_attn, o, w_gate, w_up, w_down)


def solution(mesh):
    placed = (
        P(("dp", "tensor"), None),
        P(("dp", "tensor")),
        P(("dp", "tensor")),
        P(("dp", "tensor"), None),
        P(("dp", "tensor"), None),
        P(("dp", "tensor"), None),
        P(("dp", "tensor"), None),
        P(("dp", "tensor")),
        P(None, "tensor"),
        P(None, "tensor"),
        P("tensor", None),
        P(("dp", "tensor"), None),
    )
    fits = mesh.shape["dp"] == 8 and mesh.shape["tensor"] == 4
    return jax.shard_map(
        fast_shards if fits else shards,
        mesh=mesh,
        in_specs=placed,
        out_specs=(
            P(("dp", "tensor"), None),
            P(("dp", "tensor"), None),
            P(("dp", "tensor")),
            P(("dp", "tensor"), None),
            P(("dp", "tensor"), None),
            P(("dp", "tensor"), None),
            P(("dp", "tensor"), None),
            P(("dp", "tensor")),
            P("dp", "tensor"),
            P("dp", "tensor"),
            P("tensor", "dp"),
        ),
        check_vma=False,
    )
```

```python
import functools
import math

import jax
import jax.numpy as jnp
import numpy as np
from jax import lax
from jax.experimental import pallas as pl
from jax.experimental.pallas import tpu as pltpu
from jax.sharding import PartitionSpec as P

F32 = jnp.float32
BF16 = jnp.bfloat16
MESH = pl.DeviceIdType.MESH
EPSILON = 1e-05
ROPE_BASE = 100000.0
MASKED = -1e30
HEAD = 96
VMEM_LIMIT = 64 * 2**20 - 65536


def rotary_tables(rows, shards_in_sequence):
    half = HEAD // 2
    lanes = np.arange(4 * HEAD) % half
    rates = ROPE_BASE ** (-(lanes * 2.0) / HEAD)
    near = np.arange(rows)[:, None] * rates[None, :]
    far = (np.arange(shards_in_sequence) * rows)[:, None] * rates[None, :]
    shift = np.concatenate([np.cos(far), np.sin(far)], axis=0)
    return (
        np.cos(near).astype(np.float32),
        np.sin(near).astype(np.float32),
        shift.astype(np.float32),
    )


def tensor_peer(t, m):
    if m == 1:
        return t + 1 - 2 * lax.rem(t, 2)
    if m == 2:
        return lax.rem(t + 2, 4)
    return 3 - t


def dp_peer(d, m):
    if m & 1:
        d = d + 1 - 2 * lax.rem(d, 2)
    if m & 2:
        d = d + 2 - 4 * lax.rem(lax.div(d, 2), 2)
    if m & 4:
        d = lax.rem(d + 4, 8)
    return d


class Links:
    def __init__(self, tsend, trecv, dsend, drecv):
        self.t = lax.axis_index("tensor")
        self.d = lax.axis_index("dp")
        self.mid = lax.rem(lax.div(self.t + 1, 2), 2)
        self.tsend, self.trecv, self.dsend, self.drecv = tsend, trecv, dsend, drecv

    def shard_at(self, i):
        t, mid = self.t, self.mid
        near, two, three = (tensor_peer(t, m) for m in (1, 2, 3))
        if isinstance(i, int):
            if i == 0:
                return t, 0
            if i == 1:
                return near, 1
            if i == 2:
                return two + mid * (three - two), 2 + mid
            return three + mid * (two - three), 3 - mid
        one_if = [1 - jnp.minimum(jnp.abs(i - k), 1) for k in range(4)]
        pairs = [self.shard_at(k) for k in range(4)]
        return (
            sum(f * p[0] for f, p in zip(one_if, pairs)),
            sum(f * p[1] for f, p in zip(one_if, pairs)),
        )

    def over_tensor(self, kind, m, src, dst, recv=None):
        peer = tensor_peer(self.t, m)
        return pltpu.make_async_remote_copy(
            src_ref=src,
            dst_ref=dst,
            send_sem=self.tsend.at[kind, m],
            recv_sem=self.trecv.at[kind, m if recv is None else recv],
            device_id={"dp": self.d, "tensor": peer},
            device_id_type=MESH,
        )

    def over_dp(self, kind, m, src, dst, to=None):
        peer = dp_peer(self.d, m if to is None else to)
        return pltpu.make_async_remote_copy(
            src_ref=src,
            dst_ref=dst,
            send_sem=self.dsend.at[kind, m],
            recv_sem=self.drecv.at[kind, m],
            device_id={"dp": peer, "tensor": self.t},
            device_id_type=MESH,
        )

    def landed_tensor(self, kind, m, ref):
        pltpu.make_async_copy(ref, ref, self.trecv.at[kind, m]).wait()

    def landed_dp(self, kind, m, ref):
        pltpu.make_async_copy(ref, ref, self.drecv.at[kind, m]).wait()

    def gather_start(self, kind, src, at):
        own = at(self.t)
        self.over_tensor(kind, 1, src, own).start()

        @pl.when(self.mid == 0)
        def _():
            self.over_tensor(kind, 2, src, own).start()

        @pl.when(self.mid == 1)
        def _():
            self.over_tensor(kind, 3, src, own).start()

    def gather_take(self, kind, i, at):
        shard, m = self.shard_at(i)
        block = at(shard)
        self.landed_tensor(kind, m, block)

        def hand_on():
            pltpu.make_async_remote_copy(
                src_ref=block,
                dst_ref=block,
                send_sem=self.tsend.at[kind, 2 + i],
                recv_sem=self.trecv.at[kind, 5 - m],
                device_id={"dp": self.d, "tensor": tensor_peer(self.t, 1)},
                device_id_type=MESH,
            ).start()

        if isinstance(i, int):
            if i >= 2:
                pl.when(self.mid == 1)(hand_on)
        else:
            pl.when((self.mid == 1) & (i >= 2))(hand_on)

    def gather_end(self, kind, src, at):
        own = at(self.t)
        self.over_tensor(kind, 1, src, own).wait_send()

        @pl.when(self.mid == 0)
        def _():
            self.over_tensor(kind, 2, src, own).wait_send()

        @pl.when(self.mid == 1)
        def _():
            self.over_tensor(kind, 3, src, own).wait_send()
            for i in (2, 3):
                shard, m = self.shard_at(i)
                pltpu.make_async_copy(at(shard), at(shard), self.tsend.at[kind, 2 + i]).wait()

    def barrier(self, tensor_peers, dp_peers):
        sem = pltpu.get_barrier_semaphore()
        for m in tensor_peers:
            pl.semaphore_signal(
                sem,
                inc=1,
                device_id={"dp": self.d, "tensor": tensor_peer(self.t, m)},
                device_id_type=MESH,
            )
        for m in dp_peers:
            pl.semaphore_signal(
                sem,
                inc=1,
                device_id={"dp": dp_peer(self.d, m), "tensor": self.t},
                device_id_type=MESH,
            )
        pl.semaphore_wait(sem, len(tensor_peers) + len(dp_peers))


def mm(a, b, dims=((1,), (0,))):
    return lax.dot_general(a, b, (dims, ((), ())), preferred_element_type=F32)


NN = ((1,), (0,))
NT = ((1,), (1,))
TN = ((0,), (0,))


def lane_roll(u, by):
    return pltpu.roll(u, by % u.shape[-1], u.ndim - 1)


def swap_halves(u):
    lane = lax.broadcasted_iota(jnp.int32, u.shape, 1)
    low = lax.rem(lane, HEAD) < HEAD // 2
    return jnp.where(low, -lane_roll(u, -(HEAD // 2)), lane_roll(u, HEAD // 2))


def turn_tables(near_cos, near_sin, shift, shard):
    c = shift[pl.ds(shard, 1), :]
    s = shift[pl.ds(shard + 4, 1), :]
    a, b = near_cos[...], near_sin[...]
    return a * c - b * s, b * c + a * s


def front_kernel(
    hid, cot, tile, wpack, wo, near_cos, near_sin, shift,
    normed_out, w_out, wo_out, heads_out, lse_out, start_out, cot_out, rows_out, resid_out,
    normed2_out, gains_out,
    xall, nall, call, w, wof, tiles, qh, kh, vh, att, arow, outh, lse, start, gains, resid, normed2,
    tsend, trecv, dsend, drecv, local, store,
):
    ln = Links(tsend, trecv, dsend, drecv)
    t, d = ln.t, ln.d
    rows = hid.shape[0]
    width = hid.shape[1]
    wrows = wo.shape[0]
    srows = 4 * wrows
    TILE, W, X, O, C, A = range(6)
    DT, DW, FW, DO, FO = range(5)

    def rows_at(ref, shard):
        return ref.at[pl.ds(pl.multiple_of(shard * rows, rows), rows), :]

    def w_at(ref, dd, tt=None):
        if tt is None:
            return ref.at[pl.ds(pl.multiple_of(dd * srows, 16), srows), :]
        return ref.at[pl.ds(pl.multiple_of(dd * srows + tt * wrows, 16), wrows), :]

    x_of = functools.partial(rows_at, xall)
    c_of = functools.partial(rows_at, call)

    def wo_of(tt):
        return w_at(wof, d, tt)

    mine = [
        pltpu.make_async_copy(tile, tiles.at[d, t], local.at[0]),
        pltpu.make_async_copy(wpack.at[t], w_at(w, d, t), local.at[1]),
        pltpu.make_async_copy(wo, wo_of(t), local.at[2]),
        pltpu.make_async_copy(hid, x_of(t), local.at[3]),
        pltpu.make_async_copy(cot, c_of(t), local.at[4]),
    ]
    for c in mine:
        c.start()
    ln.barrier((1, 2, 3), (1, 2, 3, 4, 5, 6, 7))
    for m in (1, 2, 3):
        ln.over_tensor(TILE, m, tile, tiles.at[d, t]).start()
    for m in (1, 2, 3):
        ln.over_tensor(W, m, wpack.at[tensor_peer(t, m)], w_at(w, d, t)).start()
    ln.gather_start(O, wo, wo_of)
    ln.gather_start(X, hid, x_of)

    mine[0].wait()
    for m in (1, 2, 3):
        ln.landed_tensor(TILE, m, tiles.at[d, tensor_peer(t, m)])
    for m in range(1, 8):
        ln.over_dp(DT, m, tiles.at[d], tiles.at[d]).start()
    mine[1].wait()
    for m in (1, 2, 3):
        ln.landed_tensor(W, m, w_at(w, d, tensor_peer(t, m)))
    for m in (2, 4, 6, 1):
        ln.over_dp(DW, m, w_at(w, d), w_at(w, d)).start()
    mine[2].wait()
    for i in (1, 2, 3):
        ln.gather_take(O, i, wo_of)
    for m in (2, 4, 6, 1):
        ln.over_dp(DO, m, w_at(wof, d), w_at(wof, d)).start()
    for m in range(1, 8):
        ln.landed_dp(DT, m, tiles.at[dp_peer(d, m)])
    for m in (2, 4, 6):
        dd = dp_peer(d, m)
        ln.landed_dp(DW, m, w_at(w, dd))
        ln.over_dp(FW, m, w_at(w, dd), w_at(w, dd), to=1).start()

    for g in range(4):
        acc = jnp.zeros((8, 8 * wrows), F32)
        for j in range(8):
            r = 8 * g + j
            piece = jnp.concatenate(
                [tiles[r // 4, r % 4], jnp.zeros((8, 8 * wrows - 128), F32)], axis=1
            )
            acc = acc + lane_roll(piece, wrows * j)
        gains[:, g * 8 * wrows : (g + 1) * 8 * wrows] = acc
    for s in range(4):
        start[:, s * rows : (s + 1) * rows] = tiles[d, s, 2:3, :]

    mine[3].wait()
    for i in (1, 2, 3):
        ln.gather_take(X, i, x_of)
    mine[4].wait()
    ln.gather_start(C, cot, c_of)
    for m in (1,):
        ln.landed_dp(DW, m, w_at(w, dp_peer(d, m)))
    for m in (2, 4, 6):
        ln.landed_dp(FW, m, w_at(w, dp_peer(d, m ^ 1)))

    def project(s, carry):
        at = pl.ds(pl.multiple_of(s * rows, rows), rows)
        x = xall[at, :].astype(F32)
        inv = lax.rsqrt(jnp.mean(x * x, axis=1, keepdims=True) + EPSILON)
        normed = (x * inv * gains[0:1, :]).astype(BF16)
        nall[at, :] = normed
        cosine, sine = turn_tables(near_cos, near_sin, shift, s)
        q = mm(normed, w[:, : 4 * HEAD])
        q = q * cosine + swap_halves(q) * sine
        kv = mm(normed, w[:, 4 * HEAD :])
        lane = lax.broadcasted_iota(jnp.int32, kv.shape, 1)
        kv = jnp.where(lane < 2 * HEAD, kv * cosine + swap_halves(kv) * sine, kv)
        keep = lax.broadcasted_iota(jnp.int32, (rows, 128), 1) < HEAD
        for h in range(4):
            qh[h, at, :] = jnp.where(keep, lane_roll(q, -HEAD * h)[:, :128], 0.0).astype(BF16)
        for c in range(2):
            kh[c, at, :] = jnp.where(keep, lane_roll(kv, -HEAD * c)[:, :128], 0.0).astype(BF16)
            vh[c, at, :] = jnp.where(keep, lane_roll(kv, -HEAD * (c + 2))[:, :128], 0.0).astype(BF16)
        return carry

    lax.fori_loop(0, 4, project, 0)

    def forward_wo(m):
        dd = dp_peer(d, m)
        ln.landed_dp(DO, m, w_at(wof, dd))
        ln.over_dp(FO, m, w_at(wof, dd), w_at(wof, dd), to=1).start()

    scale = 1.0 / math.sqrt(HEAD)

    def attend(h, carry):
        c = lax.div(h, 2)
        for b in range(4):
            span = (b + 1) * rows
            sc = mm(kh[c, :span, :], qh[h, b * rows : span, :], NT) * scale
            key = lax.broadcasted_iota(jnp.int32, sc.shape, 0)
            query = lax.broadcasted_iota(jnp.int32, sc.shape, 1) + b * rows
            first = start[:, b * rows : span].astype(jnp.int32)
            sc = jnp.where((key <= query) & (key >= first), sc, MASKED)
            peak = jnp.max(sc, axis=0, keepdims=True)
            e = jnp.exp(sc - peak)
            total = jnp.sum(e, axis=0, keepdims=True)
            p = (e * (1.0 / total)).astype(BF16)
            outh[h, b * rows : span, :] = mm(p, vh[c, :span, :], TN)
            lse[h, :, b * rows : span] = peak + jnp.log(total)
        return carry

    lax.fori_loop(0, 4, attend, 0)

    def pack(b, carry):
        at = pl.ds(pl.multiple_of(b * rows, rows), rows)
        acc = jnp.zeros((rows, 4 * HEAD), F32)
        for h in range(4):
            piece = jnp.concatenate([outh[h, at, :], jnp.zeros((rows, 4 * HEAD - 128), F32)], axis=1)
            acc = acc + lane_roll(piece, HEAD * h)
        att[b] = acc.astype(BF16)
        return carry

    lax.fori_loop(0, 4, pack, 0)

    def columns(tt):
        return arow.at[:, pl.ds(pl.multiple_of(tt * 4 * HEAD, 128), 4 * HEAD)]

    for m in (1, 2, 3):
        ln.over_tensor(A, m, att.at[tensor_peer(t, m)], columns(t)).start()
    own = pltpu.make_async_copy(att.at[t], columns(t), local.at[0])
    own.start()
    for m in (2, 4, 6):
        forward_wo(m)
    ln.landed_dp(DO, 1, w_at(wof, dp_peer(d, 1)))
    for m in (2, 4, 6):
        ln.landed_dp(FO, m, w_at(wof, dp_peer(d, m ^ 1)))
    own.wait()
    for m in (1, 2, 3):
        ln.landed_tensor(A, m, columns(tensor_peer(t, m)))

    at = pl.ds(pl.multiple_of(t * rows, rows), rows)
    third = width // 3

    def project_out(n, carry):
        cols = pl.ds(pl.multiple_of(n * third, 128), third)
        resid[:, cols] = xall[at, cols].astype(F32) + mm(arow[...], wof[:, cols])
        return carry

    lax.fori_loop(0, 3, project_out, 0)
    r = resid[...]
    inv = lax.rsqrt(jnp.mean(r * r, axis=1, keepdims=True) + EPSILON)
    normed2[...] = (r * inv * gains[1:2, :]).astype(BF16)

    for i in (1, 2, 3):
        ln.gather_take(C, i, c_of)

    results = [
        (nall, normed_out), (w, w_out), (wof, wo_out), (qh, heads_out.at[0:4]),
        (kh, heads_out.at[4:6]), (vh, heads_out.at[6:8]), (lse, lse_out), (start, start_out),
        (call, cot_out), (arow, rows_out), (resid, resid_out), (normed2, normed2_out),
        (gains, gains_out),
    ]
    stores = [pltpu.make_async_copy(a, b, store.at[i]) for i, (a, b) in enumerate(results)]
    for c in stores:
        c.start()
    for m in (1, 2, 3):
        ln.over_tensor(TILE, m, tile, tiles.at[d, t]).wait_send()
        ln.over_tensor(W, m, wpack.at[tensor_peer(t, m)], w_at(w, d, t)).wait_send()
        ln.over_tensor(A, m, att.at[tensor_peer(t, m)], columns(t)).wait_send()
    ln.gather_end(O, wo, wo_of)
    ln.gather_end(X, hid, x_of)
    ln.gather_end(C, cot, c_of)
    for m in range(1, 8):
        ln.over_dp(DT, m, tiles.at[d], tiles.at[d]).wait_send()
    for m in (2, 4, 6, 1):
        ln.over_dp(DW, m, w_at(w, d), w_at(w, d)).wait_send()
        ln.over_dp(DO, m, w_at(wof, d), w_at(wof, d)).wait_send()
    for m in (2, 4, 6):
        dd = dp_peer(d, m)
        ln.over_dp(FW, m, w_at(w, dd), w_at(w, dd), to=1).wait_send()
        ln.over_dp(FO, m, w_at(wof, dd), w_at(wof, dd), to=1).wait_send()
    for c in stores:
        c.wait()


def front(hid, cot, positions, gain_attn, gain_mlp, wq, wk, wv, wo):
    rows, width = hid.shape
    wrows = wq.shape[0]
    seq = 4 * rows
    t = lax.axis_index("tensor")
    index = t * rows + jnp.arange(rows, dtype=jnp.int32)
    pad = (0, 128 - wrows)
    tile = jnp.stack(
        [
            jnp.pad(gain_attn.astype(F32), pad),
            jnp.pad(gain_mlp.astype(F32), pad),
            (index - positions).astype(F32),
        ]
        + [jnp.zeros((128,), F32)] * 5
    )
    wpack = jnp.concatenate(
        [a.reshape(wrows, 4, a.shape[1] // 4).transpose(1, 0, 2) for a in (wq, wk, wv)], axis=2
    )
    near_cos, near_sin, shift = rotary_tables(rows, 4)
    hbm = pl.BlockSpec(memory_space=pl.ANY)
    vmem = pl.BlockSpec(memory_space=pltpu.VMEM)
    sds = jax.ShapeDtypeStruct
    shapes = dict(
        normed=((seq, width), BF16), w=((width, 8 * HEAD), BF16), wo=((width, width), BF16),
        heads=((8, seq, 128), BF16), lse=((4, 1, seq), F32), start=((1, seq), F32),
        cot=((seq, width), BF16), rows=((rows, width), BF16), resid=((rows, width), F32),
        normed2=((rows, width), BF16), gains=((8, width), F32),
    )
    S = {k: pltpu.VMEM(*v) for k, v in shapes.items()}
    outs = pl.pallas_call(
        front_kernel,
        out_shape=[sds(*v) for v in shapes.values()],
        in_specs=[hbm] * 5 + [vmem] * 3,
        out_specs=[hbm] * len(shapes),
        scratch_shapes=[
            pltpu.VMEM((seq, width), BF16),
            S["normed"], S["cot"], S["w"], S["wo"],
            pltpu.VMEM((8, 4, 8, 128), F32),
            pltpu.VMEM((4, seq, 128), BF16), pltpu.VMEM((2, seq, 128), BF16),
            pltpu.VMEM((2, seq, 128), BF16),
            pltpu.VMEM((4, rows, 4 * HEAD), BF16),
            S["rows"],
            pltpu.VMEM((4, seq, 128), F32),
            S["lse"], S["start"], S["gains"], S["resid"], S["normed2"],
            pltpu.SemaphoreType.DMA((6, 6)), pltpu.SemaphoreType.DMA((6, 4)),
            pltpu.SemaphoreType.DMA((5, 8)), pltpu.SemaphoreType.DMA((5, 8)),
            pltpu.SemaphoreType.DMA((5,)), pltpu.SemaphoreType.DMA((13,)),
        ],
        name="front",
        compiler_params=pltpu.CompilerParams(
            collective_id=0, has_side_effects=True, vmem_limit_bytes=VMEM_LIMIT
        ),
    )(hid, cot, tile, wpack, wo, near_cos, near_sin, shift)
    return dict(zip(shapes, outs), tables=(near_cos, near_sin, shift))


def feed_forward_kernel(
    nrm, cot, gains, resid, wg, wu, wd, wo,
    mlp_out, gatt_out, gres_out, low_out, gain_out, dws_out,
    rows_all, cot_all, gate_w, up_w, down_w, out_w, act, gg, gu, msend, gsend, gown, grecv,
    gatt, gres, low, gain, part, crecv,
    tsend, trecv, csend, crsem, local, store,
):
    t, d = lax.axis_index("tensor"), lax.axis_index("dp")
    ln = Links(tsend, trecv, csend, crsem)
    rows, width = nrm.shape
    span = width // 4
    half = span // 2
    core = lax.rem(d, 2)
    N, G = range(2)

    def at_shard(ref, shard):
        return ref.at[pl.ds(pl.multiple_of(shard * rows, rows), rows), :]

    def ds_of(shard):
        return pl.ds(pl.multiple_of(shard * rows, rows), rows)

    rows_of = functools.partial(at_shard, rows_all)
    loads = [
        pltpu.make_async_copy(a, b, local.at[i])
        for i, (a, b) in enumerate(
            [(nrm, rows_of(t)), (wg, gate_w), (wu, up_w), (cot, cot_all), (wd, down_w), (wo, out_w)]
        )
    ]
    for c in loads:
        c.start()
    ln.barrier((1, 2, 3), (1,))
    ln.gather_start(N, nrm, rows_of)
    for c in loads[:5]:
        c.wait()

    def to_owner(shard, m):
        return pltpu.make_async_remote_copy(
            src_ref=gsend.at[shard],
            dst_ref=grecv.at[m - 1],
            send_sem=tsend.at[G, m],
            recv_sem=trecv.at[G, m],
            device_id={"dp": d, "tensor": shard},
            device_id_type=MESH,
        )

    def one_shard(i, carry):
        shard, m = ln.shard_at(i)

        @pl.when(i > 0)
        def _():
            ln.gather_take(N, i, rows_of)

        at = ds_of(shard)
        r = rows_all[at, :]
        gate = mm(r, gate_w[...])
        up = mm(r, up_w[...])
        sig = 1.0 / (1.0 + jnp.exp(-gate))
        silu = gate * sig
        act[at, :] = (silu * up).astype(BF16)
        g_act = mm(cot_all[at, :], down_w[...], NT)
        gg[at, :] = (g_act * up * sig * (1.0 + gate * (1.0 - sig))).astype(BF16)
        gu[at, :] = (g_act * silu).astype(BF16)
        g = mm(gg[at, :], gate_w[...], NT) + mm(gu[at, :], up_w[...], NT)

        @pl.when(i == 0)
        def _():
            gown[...] = g

        @pl.when(i > 0)
        def _():
            gsend[shard] = g.astype(BF16)
            to_owner(shard, m).start()

        msend[shard] = mm(act[at, :], down_w[...]).astype(BF16)
        return carry

    lax.fori_loop(0, 4, one_shard, 0)

    def block(ref, k, j, side):
        return ref.at[k, pl.ds(pl.multiple_of(j * span + side * half, half), half), :]

    def to_core(k, j):
        return pltpu.make_async_remote_copy(
            src_ref=block(part, k, j, 1 - core),
            dst_ref=crecv.at[j, k],
            send_sem=csend.at[k, j],
            recv_sem=crsem.at[k, j],
            device_id={"dp": dp_peer(d, 1), "tensor": t},
            device_id_type=MESH,
        )

    def weights(j, carry):
        cols = pl.ds(pl.multiple_of(j * span, 128), span)
        for k, (a, b) in enumerate(((rows_all, gg), (rows_all, gu), (cot_all, act))):
            part[k, cols, :] = mm(a[:, cols], b[...], TN).astype(BF16)
            to_core(k, j).start()
        return carry

    lax.fori_loop(0, 4, weights, 0)
    stores = [pltpu.make_async_copy(msend, mlp_out, store.at[0])]
    stores[0].start()

    def chip_sums(j, carry):
        for k in range(3):
            to_core(k, j).wait_recv()
            mine = pl.ds(pl.multiple_of(j * span + core * half, half), half)
            crecv[j, k] = (part[k, mine, :].astype(F32) + crecv[j, k].astype(F32)).astype(BF16)
        return carry

    lax.fori_loop(0, 4, chip_sums, 0)
    stores.append(pltpu.make_async_copy(crecv, dws_out, store.at[1]))
    stores[1].start()
    loads[5].wait()
    for m in (1, 2, 3):
        ln.landed_tensor(G, m, grecv.at[m - 1])
    g = gown[...]
    for m in (1, 2, 3):
        g = g + grecv[m - 1].astype(F32)
    r = resid[...]
    inv = lax.rsqrt(jnp.mean(r * r, axis=1, keepdims=True) + EPSILON)
    gain[0] = jnp.sum(g * r * inv, axis=0, keepdims=True)
    scaled = g * gains[1:2, :]
    gr = (
        cot_all[ds_of(t), :].astype(F32)
        + inv * scaled
        - r * (inv * inv * inv) * jnp.mean(scaled * r, axis=1, keepdims=True)
    )
    gres[...] = gr
    low[...] = gr.astype(BF16)
    for s in range(4):
        gatt[s] = mm(low[...], out_w[s * span : (s + 1) * span, :], NT).astype(BF16)
    for i, (a, b) in enumerate(((gatt, gatt_out), (gres, gres_out), (low, low_out), (gain, gain_out))):
        stores.append(pltpu.make_async_copy(a, b, store.at[2 + i]))
        stores[-1].start()
    ln.gather_end(N, nrm, rows_of)
    for m in (1, 2, 3):
        to_owner(tensor_peer(t, m), m).wait_send()

    def sent(j, carry):
        for k in range(3):
            to_core(k, j).wait_send()
        return carry

    lax.fori_loop(0, 4, sent, 0)
    for c in stores:
        c.wait()


def feed_forward(o, w_gate, w_up, w_down):
    rows, width = o["normed2"].shape
    units = w_gate.shape[1]
    span = width // 4
    seq = 4 * rows
    hbm = pl.BlockSpec(memory_space=pl.ANY)
    vmem = pl.BlockSpec(memory_space=pltpu.VMEM)
    shapes = dict(
        mlp=((4, rows, width), BF16), g_att=((4, rows, span), BF16), g_resid=((rows, width), F32),
        low=((rows, width), BF16), gain=((1, 1, width), F32),
        grads=((4, 3, span // 2, units), BF16),
    )
    S = {k: pltpu.VMEM(*v) for k, v in shapes.items()}
    wide = pltpu.VMEM((seq, width), BF16)
    hidden = pltpu.VMEM((seq, units), BF16)
    weight = pltpu.VMEM((width, units), BF16)
    outs = pl.pallas_call(
        feed_forward_kernel,
        out_shape=[jax.ShapeDtypeStruct(*v) for v in shapes.values()],
        in_specs=[hbm, hbm, vmem, vmem, hbm, hbm, hbm, hbm],
        out_specs=[hbm] * len(shapes),
        scratch_shapes=[
            wide, wide, weight, weight, pltpu.VMEM((units, width), BF16),
            pltpu.VMEM((width, width), BF16), hidden, hidden, hidden,
            S["mlp"], S["mlp"], S["g_resid"], pltpu.VMEM((3, rows, width), BF16),
            S["g_att"], S["g_resid"], S["low"], S["gain"],
            pltpu.VMEM((3, width, units), BF16), S["grads"],
            pltpu.SemaphoreType.DMA((2, 6)), pltpu.SemaphoreType.DMA((2, 4)),
            pltpu.SemaphoreType.DMA((3, 4)), pltpu.SemaphoreType.DMA((3, 4)),
            pltpu.SemaphoreType.DMA((6,)), pltpu.SemaphoreType.DMA((6,)),
        ],
        name="feed_forward",
        compiler_params=pltpu.CompilerParams(
            collective_id=1, has_side_effects=True, vmem_limit_bytes=VMEM_LIMIT
        ),
    )(o["normed2"], o["cot"], o["gains"], o["resid"], w_gate, w_up, w_down, o["wo"])
    return dict(zip(shapes, outs))


class LineSum:
    def __init__(self, ln, kind, src, recv):
        self.ln, self.kind, self.src, self.recv = ln, kind, src, recv
        t = ln.t
        self.near, self.two, self.three = (tensor_peer(t, m) for m in (1, 2, 3))

    def copy(self, src, to, slot, sem):
        ln, kind = self.ln, self.kind
        return pltpu.make_async_remote_copy(
            src_ref=src,
            dst_ref=self.recv.at[slot],
            send_sem=ln.tsend.at[kind, sem],
            recv_sem=ln.trecv.at[kind, slot],
            device_id={"dp": ln.d, "tensor": to},
            device_id_type=MESH,
        )

    def first(self, i, shard):
        c = self.copy(self.src.at[shard], self.near, i, i)
        if isinstance(i, int):
            if i == 2:
                c.start()
            else:
                pl.when(self.ln.mid == 0)(c.start)
        else:
            pl.when((i == 2) | ((self.ln.mid == 0) & (i < 2)))(c.start)

    def start(self):
        for i, shard in enumerate((self.three, self.two, self.near)):
            self.first(i, shard)

    def hand_on(self):
        @pl.when(self.ln.mid == 1)
        def _():
            for i, shard in enumerate((self.two, self.three)):
                self.ln.landed_tensor(self.kind, i, self.recv.at[i])
                self.recv[i] = (
                    self.recv[i].astype(F32) + self.src[shard].astype(F32)
                ).astype(BF16)
                self.copy(self.recv.at[i], shard, 3, i).start()

    def take(self):
        for i in (2, 3):
            self.ln.landed_tensor(self.kind, i, self.recv.at[i])
        return self.recv[2].astype(F32) + self.recv[3].astype(F32)

    def end(self):
        for i in range(3):
            pltpu.make_async_copy(
                self.src.at[0], self.src.at[0], self.ln.tsend.at[self.kind, i]
            ).wait()


class PlaneSum:
    def __init__(self, ln, kind, src, recv):
        self.ln, self.kind, self.src, self.recv = ln, kind, src, recv
        j = lax.div(ln.d, 2)
        self.j = j
        self.x = j + 1 - 2 * lax.rem(j, 2)
        self.y = lax.rem(j + 2, 4)
        self.diag = lax.rem(self.x + 2, 4)
        self.lanes = src.shape[-1] // 2

    def half(self, ref, h):
        spot = [slice(None)] * (len(ref.shape) - 1) + [pl.ds(h * self.lanes, self.lanes)]
        return ref.at[tuple(spot)]

    def copy(self, src, m, i):
        return self.ln.over_dp(self.kind, i, src, self.recv.at[i], to=m)

    def plan(self):
        return (
            (self.half(self.src.at[self.diag], 0), 2, 0),
            (self.half(self.src.at[self.diag], 1), 4, 2),
            (self.half(self.src.at[self.x], 0), 2, 1),
            (self.half(self.src.at[self.y], 1), 4, 3),
        )

    def start(self):
        for src, m, i in self.plan():
            self.copy(src, m, i).start()

    def hand_on(self):
        for i, h, block, m in ((0, 0, self.y, 4), (2, 1, self.x, 2)):
            self.ln.landed_dp(self.kind, i, self.recv.at[i])
            self.recv[i] = (
                self.recv[i].astype(F32) + self.half(self.src.at[block], h)[...].astype(F32)
            ).astype(BF16)
            self.copy_on(i, h, m).start()

    def copy_on(self, i, h, m):
        return self.ln.over_dp(self.kind, 4 + h, self.recv.at[i], self.recv.at[4 + h], to=m)

    def take(self, h):
        for i in (1 + 2 * h, 4 + h):
            self.ln.landed_dp(self.kind, i, self.recv.at[i])
        own = self.half(self.src.at[self.j], h)[...].astype(F32)
        return own + self.recv[1 + 2 * h].astype(F32) + self.recv[4 + h].astype(F32)

    def end(self):
        for src, m, i in self.plan():
            self.copy(src, m, i).wait_send()
        for i, h, m in ((0, 0, 4), (2, 1, 2)):
            self.copy_on(i, h, m).wait_send()


class CoreSum:
    def __init__(self, ln, kind, src, recv):
        self.ln, self.kind, self.src, self.recv = ln, kind, src, recv
        self.half = recv.shape[1]
        self.core = lax.rem(ln.d, 2)

    def side(self, which):
        return pl.ds(pl.multiple_of(which * self.half, self.half), self.half)

    def copy(self, j):
        ln = self.ln
        return pltpu.make_async_remote_copy(
            src_ref=self.src.at[j, self.side(1 - self.core), :],
            dst_ref=self.recv.at[j],
            send_sem=ln.dsend.at[self.kind, j],
            recv_sem=ln.drecv.at[self.kind, j],
            device_id={"dp": dp_peer(ln.d, 1), "tensor": ln.t},
            device_id_type=MESH,
        )

    def take(self):
        def one(j, carry):
            self.copy(j).wait_recv()
            self.recv[j] = (
                self.recv[j].astype(F32) + self.src[j, self.side(self.core), :].astype(F32)
            ).astype(BF16)
            return carry

        lax.fori_loop(0, 4, one, 0)

    def end(self):
        def one(j, carry):
            self.copy(j).wait_send()
            return carry

        lax.fori_loop(0, 4, one, 0)


def back_kernel(
    gatt, mlp, heads, lse, start, normed, w, hid, gres, resid, gains, arow, low, grads, gain,
    near_cos, near_sin, shift,
    layer_out, gin_out, gain_out, wqkv_out, wo_out, mlpw_out,
    gall, gh, hd, gq, gk, gv, gqkv, nall, wv, mlp_src, mlp_in, gn_src, gn_in,
    ff, ff_in, wo_part, wo_core, wo_in, wo_src, wo_line, wq_part, wq_core, wq_in, wq_src, wq_all,
    rows_in, line_in, layer, gin, gsum, wqkv, wof, ffw,
    tsend, trecv, dsend, drecv, local, store,
):
    ln = Links(tsend, trecv, dsend, drecv)
    t, d = ln.t, ln.d
    rows, width = hid.shape
    span = width // 4
    A, M, B, O, W, R = range(6)
    DF, DR, CO, DO, CW, DW = range(6)

    def ds_of(shard):
        return pl.ds(pl.multiple_of(shard * rows, rows), rows)

    loads = [
        pltpu.make_async_copy(a, b, local.at[i])
        for i, (a, b) in enumerate(
            [
                (grads, ff), (gatt.at[t], gall.at[ds_of(t), :]), (mlp, mlp_src), (heads, hd),
                (w, wv), (normed, nall), (gain, rows_in.at[pl.ds(d, 1)]),
            ]
        )
    ]
    for c in loads:
        c.start()
    ln.barrier((1, 2, 3), (1, 2, 3, 4, 5, 6, 7))
    for m in (3, 2, 1):
        ln.over_tensor(A, m, gatt.at[tensor_peer(t, m)], gall.at[ds_of(t), :]).start()
    ff_sum = PlaneSum(ln, DF, ff, ff_in)
    loads[0].wait()
    ff_sum.start()
    for m in range(1, 8):
        ln.over_dp(DR, m, gain.at[0], rows_in.at[d]).start()
    layer_sum = LineSum(ln, M, mlp_src, mlp_in)
    loads[2].wait()
    layer_sum.start()

    wo_pair = CoreSum(ln, CO, wo_part, wo_core)

    def output_weights(j, carry):
        cols = pl.ds(pl.multiple_of(j * span, 128), span)
        wo_part[j] = mm(arow[:, cols], low[...], TN).astype(BF16)
        wo_pair.copy(j).start()
        return carry

    lax.fori_loop(0, 4, output_weights, 0)

    for c in (loads[1], loads[3]):
        c.wait()
    for m in (1, 2, 3):
        ln.landed_tensor(A, m, gall.at[ds_of(tensor_peer(t, m)), :])
    keep = lax.broadcasted_iota(jnp.int32, (rows, 128), 1) < HEAD

    def split(b, carry):
        u = gall[ds_of(b), :].astype(F32)
        for h in range(4):
            gh[h, ds_of(b), :] = jnp.where(keep, lane_roll(u, -HEAD * h)[:, :128], 0.0).astype(BF16)
        return carry

    lax.fori_loop(0, 4, split, 0)
    gk[...] = jnp.zeros_like(gk)
    gv[...] = jnp.zeros_like(gv)
    scale = 1.0 / math.sqrt(HEAD)

    def attend_back(h, carry):
        c = lax.div(h, 2)
        for b in range(4):
            far = (b + 1) * rows
            here = slice(b * rows, far)
            k, v, q, g = hd[4 + c, :far, :], hd[6 + c, :far, :], hd[h, here, :], gh[h, here, :]
            sc = mm(k, q, NT) * scale
            key = lax.broadcasted_iota(jnp.int32, sc.shape, 0)
            query = lax.broadcasted_iota(jnp.int32, sc.shape, 1) + b * rows
            first = start[:, here].astype(jnp.int32)
            sc = jnp.where((key <= query) & (key >= first), sc, MASKED)
            p = jnp.exp(sc - lse[h, :, here])
            gp = mm(v, g, NT)
            gs = (p * (gp - jnp.sum(p * gp, axis=0, keepdims=True))).astype(BF16)
            gq[h, here, :] = mm(gs, k, TN) * scale
            gk[c, :far, :] += mm(gs, q) * scale
            gv[c, :far, :] += mm(p.astype(BF16), g)
        return carry

    lax.fori_loop(0, 4, attend_back, 0)

    def gather_heads(b, carry):
        at = ds_of(b)
        cosine, sine = turn_tables(near_cos, near_sin, shift, b)
        cosine, sine = cosine[:, :128], sine[:, :128]

        def placed(u, h):
            u = jnp.concatenate(
                [jnp.where(keep, u, 0.0), jnp.zeros((rows, 4 * HEAD - 128), F32)], axis=1
            )
            return lane_roll(u, HEAD * h)

        def turned(u):
            return u * cosine - swap_halves(u) * sine

        left = sum(placed(turned(gq[h, at, :]), h) for h in range(4))
        right = sum(placed(turned(gk[c, at, :]), c) for c in range(2))
        right = right + sum(placed(gv[c, at, :], c + 2) for c in range(2))
        gqkv[at, : 4 * HEAD] = left.astype(BF16)
        gqkv[at, 4 * HEAD :] = right.astype(BF16)
        return carry

    lax.fori_loop(0, 4, gather_heads, 0)
    for c in (loads[4], loads[5]):
        c.wait()
    gn_sum = LineSum(ln, B, gn_src, gn_in)

    def norm_grads(i, carry):
        shard, _ = ln.shard_at(3 - i)
        gn_src[shard] = mm(gqkv[ds_of(shard), :], wv[...], NT).astype(BF16)
        gn_sum.first(i, shard)
        return carry

    layer_sum.hand_on()
    lax.fori_loop(0, 4, norm_grads, 0)
    wo_pair.take()
    wo_sum = PlaneSum(ln, DO, wo_core, wo_in)
    wo_sum.start()
    wq_pair = CoreSum(ln, CW, wq_part, wq_core)

    def head_weights(j, carry):
        cols = pl.ds(pl.multiple_of(j * span, 128), span)
        wq_part[j] = mm(nall[:, cols], gqkv[...], TN).astype(BF16)
        wq_pair.copy(j).start()
        return carry

    lax.fori_loop(0, 4, head_weights, 0)
    ff_sum.hand_on()
    gn_sum.hand_on()
    wq_pair.take()
    wq_sum = PlaneSum(ln, DW, wq_core, wq_in)
    wq_sum.start()
    wo_sum.hand_on()

    loads[6].wait()
    for m in range(1, 8):
        ln.landed_dp(DR, m, rows_in.at[dp_peer(d, m)])
    gsum[0] = sum(rows_in[i] for i in range(8))
    for m in (1, 2, 3):
        ln.over_tensor(R, m, gsum.at[0], line_in.at[m]).start()

    stores = []

    def out(a, b):
        c = pltpu.make_async_copy(a, b, store.at[len(stores)])
        c.start()
        stores.append(c)

    layer[...] = (resid[...] + mlp_src[t].astype(F32) + layer_sum.take()).astype(BF16)
    out(layer, layer_out)
    lanes = ff_sum.lanes
    for h in range(2):
        ffw[:, :, h * lanes : (h + 1) * lanes] = ff_sum.take(h)
    out(ffw, mlpw_out)
    wq_sum.hand_on()
    x = hid[...].astype(F32)
    inv = lax.rsqrt(jnp.mean(x * x, axis=1, keepdims=True) + EPSILON)
    scaled = (gn_src[t].astype(F32) + gn_sum.take()) * gains[0:1, :]
    gin[...] = (
        gres[...]
        + inv * scaled
        - x * (inv * inv * inv) * jnp.mean(scaled * x, axis=1, keepdims=True)
    )
    out(gin, gin_out)
    wrows = wo_src.shape[1]
    lanes = wo_sum.lanes
    for h in range(2):
        u = wo_sum.take(h).astype(BF16)
        for s in range(4):
            wo_src[s, :, h * lanes : (h + 1) * lanes] = u[s * wrows : (s + 1) * wrows, :]
    wo_line_sum = LineSum(ln, O, wo_src, wo_line)
    wo_line_sum.start()
    total = gsum[0]
    for m in (1, 2, 3):
        ln.landed_tensor(R, m, line_in.at[m])
        total = total + line_in[m]
    line_in[0] = total
    out(line_in.at[0], gain_out)
    lanes = wq_sum.lanes
    for h in range(2):
        u = wq_sum.take(h).astype(BF16)
        for s in range(4):
            wq_src[s, :, h * lanes : (h + 1) * lanes] = u[s * wrows : (s + 1) * wrows, :]
    for m in (3, 2, 1):
        ln.over_tensor(W, m, wq_src.at[tensor_peer(t, m)], wq_all.at[m]).start()
    wqkv[pl.ds(t, 1)] = wq_src[pl.ds(t, 1)].astype(F32)
    wo_line_sum.hand_on()
    for m in (1, 2, 3):
        ln.landed_tensor(W, m, wq_all.at[m])
        wqkv[pl.ds(tensor_peer(t, m), 1)] = wq_all[pl.ds(m, 1)].astype(F32)
    out(wqkv, wqkv_out)
    wof[...] = wo_src[t].astype(F32) + wo_line_sum.take()
    out(wof, wo_out)

    for m in (1, 2, 3):
        ln.over_tensor(A, m, gatt.at[tensor_peer(t, m)], gall.at[ds_of(t), :]).wait_send()
        ln.over_tensor(R, m, gsum.at[0], line_in.at[m]).wait_send()
        ln.over_tensor(W, m, wq_src.at[tensor_peer(t, m)], wq_all.at[m]).wait_send()
    for m in range(1, 8):
        ln.over_dp(DR, m, gain.at[0], rows_in.at[d]).wait_send()
    for s in (layer_sum, gn_sum, wo_line_sum, ff_sum, wo_sum, wq_sum, wo_pair, wq_pair):
        s.end()
    for c in stores:
        c.wait()


def back(o, f, hid, tables):
    rows, width = hid.shape
    seq = 4 * rows
    span = width // 4
    wrows = span // 8
    units = f["grads"].shape[-1]
    hbm = pl.BlockSpec(memory_space=pl.ANY)
    vmem = pl.BlockSpec(memory_space=pltpu.VMEM)
    V = pltpu.VMEM
    shapes = dict(
        layer=((rows, width), BF16), gin=((rows, width), F32), gain=((1, width), F32),
        wqkv=((4, wrows, 8 * HEAD), F32), wo=((wrows, width), F32),
        mlp=((3, span // 2, units), F32),
    )
    operands = [
        (f["g_att"], hbm), (f["mlp"], hbm), (o["heads"], hbm), (o["lse"], vmem), (o["start"], vmem),
        (o["normed"], hbm), (o["w"], hbm), (hid, vmem), (f["g_resid"], vmem), (o["resid"], vmem),
        (o["gains"], vmem), (o["rows"], vmem), (f["low"], vmem), (f["grads"], hbm),
        (f["gain"], hbm), (tables[0], vmem), (tables[1], vmem), (tables[2], vmem),
    ]
    half = span // 2
    four = V((4, rows, width), BF16)
    outs = pl.pallas_call(
        back_kernel,
        out_shape=[jax.ShapeDtypeStruct(*v) for v in shapes.values()],
        in_specs=[s for _, s in operands],
        out_specs=[hbm] * len(shapes),
        scratch_shapes=[
            V((seq, span), BF16), V((4, seq, 128), BF16), V((8, seq, 128), BF16),
            V((4, seq, 128), F32), V((2, seq, 128), F32), V((2, seq, 128), F32),
            V((seq, 8 * HEAD), BF16), V((seq, width), BF16), V((width, 8 * HEAD), BF16),
            four, four, four, four,
            V((4, 3, half, units), BF16), V((6, 3, half, units // 2), BF16),
            V((4, span, width), BF16), V((4, half, width), BF16), V((6, half, width // 2), BF16),
            V((4, wrows, width), BF16), V((4, wrows, width), BF16),
            V((4, span, 8 * HEAD), BF16), V((4, half, 8 * HEAD), BF16),
            V((6, half, 4 * HEAD), BF16), V((4, wrows, 8 * HEAD), BF16),
            V((4, wrows, 8 * HEAD), BF16),
            V((8, 1, width), F32), V((4, 1, width), F32),
            V((rows, width), BF16), V((rows, width), F32), V((1, 1, width), F32),
            V((4, wrows, 8 * HEAD), F32), V((wrows, width), F32), V((3, half, units), F32),
            pltpu.SemaphoreType.DMA((6, 4)), pltpu.SemaphoreType.DMA((6, 4)),
            pltpu.SemaphoreType.DMA((6, 8)), pltpu.SemaphoreType.DMA((6, 8)),
            pltpu.SemaphoreType.DMA((7,)), pltpu.SemaphoreType.DMA((6,)),
        ],
        name="back",
        compiler_params=pltpu.CompilerParams(
            collective_id=2, has_side_effects=True, vmem_limit_bytes=VMEM_LIMIT
        ),
    )(*[a for a, _ in operands])
    return dict(zip(shapes, outs))


QUERY_HEADS = 16
KEY_VALUE_HEADS = 8
HEAD_DIMENSION = 96


def angle_tables(pos_rows, head_size):
    half_size = head_size // 2
    freq_rates = ROPE_BASE ** (-(jnp.arange(half_size, dtype=jnp.float32) * 2.0) / head_size)
    turned = pos_rows.astype(jnp.float32)[:, None] * freq_rates[None, :]
    return (jnp.cos(turned)[:, None, :], jnp.sin(turned)[:, None, :])


def apply_rotary(tensor_in, cosine_table, sine_table):
    half_size = tensor_in.shape[-1] // 2
    lo_half = tensor_in[..., :half_size]
    hi_half = tensor_in[..., half_size:]
    return jnp.concatenate(
        [
            lo_half * cosine_table - hi_half * sine_table,
            hi_half * cosine_table + lo_half * sine_table,
        ],
        axis=-1,
    )


def shards(
    hidden_in,
    positions,
    gain_attn,
    w_query,
    key_matrix,
    value_matrix,
    w_output,
    gain_mlp,
    w_gate,
    w_up,
    w_down,
    cotangent,
):
    tok_rows = hidden_in.shape[0]
    model_width = hidden_in.shape[1]
    num_heads = QUERY_HEADS
    key_value_count = KEY_VALUE_HEADS
    head_size = HEAD_DIMENSION
    kv_width = key_value_count * head_size
    queries_per_group = num_heads // key_value_count
    seq_len = tok_rows * lax.axis_size("tensor")
    score_scale = 1.0 / math.sqrt(head_size)
    gathered = (
        lax.all_gather(gain_attn, ("dp", "tensor"), axis=0, tiled=True),
        lax.all_gather(w_query, ("dp", "tensor"), axis=0, tiled=True),
        lax.all_gather(key_matrix, ("dp", "tensor"), axis=0, tiled=True),
        lax.all_gather(value_matrix, ("dp", "tensor"), axis=0, tiled=True),
        lax.all_gather(w_output, ("dp", "tensor"), axis=0, tiled=True),
        lax.all_gather(gain_mlp, ("dp", "tensor"), axis=0, tiled=True),
    )
    gain_one, query_full, key_full, value_full, output_full, gain_two = gathered
    gain_one_f = gain_one.astype(jnp.float32)
    gain_two_f = gain_two.astype(jnp.float32)
    x_float = hidden_in.astype(jnp.float32)
    inv_one = lax.rsqrt(jnp.mean(x_float * x_float, axis=-1, keepdims=True) + EPSILON)
    normed_one = (x_float * inv_one * gain_one_f).astype(jnp.bfloat16)
    queries = jnp.dot(normed_one, query_full, preferred_element_type=jnp.float32)
    key_projected = jnp.dot(normed_one, key_full, preferred_element_type=jnp.float32)
    value_proj = jnp.dot(normed_one, value_full, preferred_element_type=jnp.float32)
    cosine_table, sine_table = angle_tables(positions, head_size)
    rotated_query_rows = apply_rotary(
        queries.reshape(tok_rows, num_heads, head_size), cosine_table, sine_table
    ).astype(jnp.bfloat16)
    rotated_key_rows = (
        apply_rotary(
            key_projected.reshape(tok_rows, key_value_count, head_size), cosine_table, sine_table
        )
        .astype(jnp.bfloat16)
        .reshape(tok_rows, kv_width)
    )
    value_rows_lowered = value_proj.astype(jnp.bfloat16)
    keys_all, values_all = (
        lax.all_gather(rotated_key_rows, "tensor", axis=0, tiled=True),
        lax.all_gather(value_rows_lowered, "tensor", axis=0, tiled=True),
    )
    offset = lax.axis_index("tensor") * tok_rows
    query_index = offset + jnp.arange(tok_rows, dtype=jnp.int32)
    key_index = jnp.arange(seq_len, dtype=jnp.int32)
    visible = (key_index[None, :] <= query_index[:, None]) & (
        key_index[None, :] >= (query_index - positions)[:, None]
    )
    visible = jnp.tile(visible, (queries_per_group, 1))

    def split_queries(tensor_in):
        return (
            tensor_in.reshape(tok_rows, key_value_count, queries_per_group, head_size)
            .transpose(1, 2, 0, 3)
            .reshape(key_value_count, queries_per_group * tok_rows, head_size)
        )

    def split_keys(tensor_in):
        return tensor_in.reshape(seq_len, key_value_count, head_size).transpose(1, 0, 2)

    def merge_heads(tensor_in):
        return (
            tensor_in.reshape(key_value_count, queries_per_group, tok_rows, head_size)
            .transpose(2, 0, 1, 3)
            .reshape(tok_rows, model_width)
        )

    query_heads = split_queries(rotated_query_rows)
    k_heads = split_keys(keys_all)
    value_heads = split_keys(values_all)

    def attend(head_items):
        q_block, k_block, v_block = head_items
        scores = (
            jnp.einsum("qd,kd->qk", q_block, k_block, preferred_element_type=jnp.float32)
            * score_scale
        )
        scores = jnp.where(visible, scores, MASKED)
        peak = jnp.max(scores, axis=-1, keepdims=True)
        exp_vals = jnp.exp(scores - peak)
        total = jnp.sum(exp_vals, axis=-1, keepdims=True)
        probs = exp_vals / total
        out_block = jnp.einsum(
            "qk,kd->qd", probs.astype(jnp.bfloat16), v_block, preferred_element_type=jnp.float32
        )
        return (out_block, peak[:, 0] + jnp.log(total[:, 0]))

    attended_rows, log_total = lax.map(attend, (query_heads, k_heads, value_heads))
    attended_low = merge_heads(attended_rows).astype(jnp.bfloat16)
    resid_sum = x_float + jnp.dot(attended_low, output_full, preferred_element_type=jnp.float32)
    inv_two = lax.rsqrt(jnp.mean(resid_sum * resid_sum, axis=-1, keepdims=True) + EPSILON)
    normed_two = (resid_sum * inv_two * gain_two_f).astype(jnp.bfloat16)
    rows_all = lax.all_gather(normed_two, "tensor", axis=0, tiled=True)
    gate_val = jnp.dot(rows_all, w_gate, preferred_element_type=jnp.float32)
    up_val = jnp.dot(rows_all, w_up, preferred_element_type=jnp.float32)
    sig_gate = jax.nn.sigmoid(gate_val)
    silu_gate = gate_val * sig_gate
    act_low = (silu_gate * up_val).astype(jnp.bfloat16)
    mlp_sum = lax.psum_scatter(
        jnp.dot(act_low, w_down, preferred_element_type=jnp.float32).astype(jnp.bfloat16),
        "tensor",
        scatter_dimension=0,
        tiled=True,
    ).astype(jnp.float32)
    layer_out = (resid_sum + mlp_sum).astype(jnp.bfloat16)
    grad_float = cotangent.astype(jnp.float32)
    grad_all = lax.all_gather(cotangent, "tensor", axis=0, tiled=True)
    grad_down = jnp.einsum("sf,sd->fd", act_low, grad_all, preferred_element_type=jnp.float32)
    g_act = jnp.einsum("sd,fd->sf", grad_all, w_down, preferred_element_type=jnp.float32)
    g_gate = (g_act * up_val * sig_gate * (1.0 + gate_val * (1.0 - sig_gate))).astype(jnp.bfloat16)
    g_up = (g_act * silu_gate).astype(jnp.bfloat16)
    grad_gate = jnp.einsum("sd,sf->df", rows_all, g_gate, preferred_element_type=jnp.float32)
    grad_up = jnp.einsum("sd,sf->df", rows_all, g_up, preferred_element_type=jnp.float32)
    g_norm_two = lax.psum_scatter(
        (
            jnp.einsum("sf,df->sd", g_gate, w_gate, preferred_element_type=jnp.float32)
            + jnp.einsum("sf,df->sd", g_up, w_up, preferred_element_type=jnp.float32)
        ).astype(jnp.bfloat16),
        "tensor",
        scatter_dimension=0,
        tiled=True,
    ).astype(jnp.float32)
    scaled_two = gain_two_f * g_norm_two
    grad_gain_two = jnp.sum(g_norm_two * resid_sum * inv_two, axis=0)
    g_resid = (
        grad_float
        + inv_two * scaled_two
        - resid_sum * inv_two**3 * jnp.mean(scaled_two * resid_sum, axis=-1, keepdims=True)
    )
    g_resid_low = g_resid.astype(jnp.bfloat16)
    grad_output = jnp.einsum(
        "tc,td->cd", attended_low, g_resid_low, preferred_element_type=jnp.float32
    )
    g_att = jnp.einsum(
        "td,cd->tc", g_resid_low, output_full, preferred_element_type=jnp.float32
    ).astype(jnp.bfloat16)
    g_heads = split_queries(g_att)

    def attend_back(head_items):
        q_block, k_block, v_block, log_block, g_block = head_items
        scores = (
            jnp.einsum("qd,kd->qk", q_block, k_block, preferred_element_type=jnp.float32)
            * score_scale
        )
        scores = jnp.where(visible, scores, MASKED)
        probs = jnp.exp(scores - log_block[:, None])
        g_probs = jnp.einsum("qd,kd->qk", g_block, v_block, preferred_element_type=jnp.float32)
        g_scores = (probs * (g_probs - jnp.sum(probs * g_probs, axis=-1, keepdims=True))).astype(
            jnp.bfloat16
        )
        g_rq = (
            jnp.einsum("qk,kd->qd", g_scores, k_block, preferred_element_type=jnp.float32)
            * score_scale
        )
        g_rk = (
            jnp.einsum("qk,qd->kd", g_scores, q_block, preferred_element_type=jnp.float32)
            * score_scale
        )
        g_val = jnp.einsum(
            "qk,qd->kd", probs.astype(jnp.bfloat16), g_block, preferred_element_type=jnp.float32
        )
        return (g_rq, g_rk, g_val)

    g_rq, g_rk, g_val = lax.map(
        attend_back, (query_heads, k_heads, value_heads, log_total, g_heads)
    )
    g_rk_flat = g_rk.transpose(1, 0, 2).reshape(seq_len, kv_width)
    g_val_flat = g_val.transpose(1, 0, 2).reshape(seq_len, kv_width)
    key_part, value_part = (
        lax.psum_scatter(
            g_rk_flat.astype(jnp.bfloat16), "tensor", scatter_dimension=0, tiled=True
        ).astype(jnp.float32),
        lax.psum_scatter(
            g_val_flat.astype(jnp.bfloat16), "tensor", scatter_dimension=0, tiled=True
        ).astype(jnp.float32),
    )
    g_queries = (
        apply_rotary(
            merge_heads(g_rq).reshape(tok_rows, num_heads, head_size), cosine_table, -sine_table
        )
        .reshape(tok_rows, model_width)
        .astype(jnp.bfloat16)
    )
    g_keys = (
        apply_rotary(
            key_part.reshape(tok_rows, key_value_count, head_size), cosine_table, -sine_table
        )
        .reshape(tok_rows, kv_width)
        .astype(jnp.bfloat16)
    )
    g_values = value_part.astype(jnp.bfloat16)
    grad_query = jnp.einsum("tc,td->cd", normed_one, g_queries, preferred_element_type=jnp.float32)
    grad_key = jnp.einsum("tc,td->cd", normed_one, g_keys, preferred_element_type=jnp.float32)
    grad_value = jnp.einsum("tc,td->cd", normed_one, g_values, preferred_element_type=jnp.float32)
    g_norm_one = (
        jnp.einsum("td,cd->tc", g_queries, query_full, preferred_element_type=jnp.float32)
        + jnp.einsum("td,cd->tc", g_keys, key_full, preferred_element_type=jnp.float32)
        + jnp.einsum("td,cd->tc", g_values, value_full, preferred_element_type=jnp.float32)
    )
    scaled_one = gain_one_f * g_norm_one
    grad_gain_one = jnp.sum(g_norm_one * x_float * inv_one, axis=0)
    grad_input = (
        g_resid
        + inv_one * scaled_one
        - x_float * inv_one**3 * jnp.mean(scaled_one * x_float, axis=-1, keepdims=True)
    )
    packed = jnp.concatenate([grad_query, grad_key, grad_value, grad_output], axis=1)
    packed_part = lax.psum_scatter(
        packed.astype(jnp.bfloat16), ("dp", "tensor"), scatter_dimension=0, tiled=True
    ).astype(jnp.float32)
    query_part = packed_part[:, :model_width]
    keyw_part = packed_part[:, model_width : model_width + kv_width]
    valuew_part = packed_part[:, model_width + kv_width : model_width + 2 * kv_width]
    out_part = packed_part[:, model_width + 2 * kv_width :]
    gain_one_part, gain_two_part = (
        lax.psum_scatter(grad_gain_one, ("dp", "tensor"), scatter_dimension=0, tiled=True),
        lax.psum_scatter(grad_gain_two, ("dp", "tensor"), scatter_dimension=0, tiled=True),
    )
    gate_sum, up_sum, down_sum = (
        lax.psum_scatter(
            grad_gate.astype(jnp.bfloat16), "dp", scatter_dimension=0, tiled=True
        ).astype(jnp.float32),
        lax.psum_scatter(
            grad_up.astype(jnp.bfloat16), "dp", scatter_dimension=0, tiled=True
        ).astype(jnp.float32),
        lax.psum_scatter(
            grad_down.astype(jnp.bfloat16), "dp", scatter_dimension=1, tiled=True
        ).astype(jnp.float32),
    )
    return (
        layer_out,
        grad_input,
        gain_one_part,
        query_part,
        keyw_part,
        valuew_part,
        out_part,
        gain_two_part,
        gate_sum,
        up_sum,
        down_sum,
    )


def fast_shards(
    hidden_in, positions, gain_attn, w_query, key_matrix, value_matrix, w_output, gain_mlp,
    w_gate, w_up, w_down, cotangent,
):
    o = front(
        hidden_in, cotangent, positions, gain_attn, gain_mlp, w_query, key_matrix, value_matrix,
        w_output,
    )
    f = feed_forward(o, w_gate, w_up, w_down)
    b = back(o, f, hidden_in, o["tables"])
    wrows = w_query.shape[0]
    parts = b["wqkv"].transpose(1, 0, 2)
    query = parts[:, :, : 4 * HEAD].reshape(wrows, 16 * HEAD)
    key = parts[:, :, 4 * HEAD : 6 * HEAD].reshape(wrows, 8 * HEAD)
    value = parts[:, :, 6 * HEAD :].reshape(wrows, 8 * HEAD)

    def rows_of(w, g):
        return jnp.sum(w.astype(F32) * g, axis=1)

    gain_one = (
        rows_of(w_query, query) + rows_of(key_matrix, key) + rows_of(value_matrix, value)
    ) / gain_attn.astype(F32)
    mine = lax.axis_index("dp") * lax.axis_size("tensor") + lax.axis_index("tensor")
    gain_two = lax.dynamic_slice_in_dim(b["gain"][0], mine * wrows, wrows, 0)
    return (
        b["layer"], b["gin"], gain_one, query, key, value, b["wo"], gain_two,
        b["mlp"][0], b["mlp"][1], b["mlp"][2].T,
    )


def solution(mesh):
    placed = (
        P(("dp", "tensor"), None),
        P(("dp", "tensor")),
        P(("dp", "tensor")),
        P(("dp", "tensor"), None),
        P(("dp", "tensor"), None),
        P(("dp", "tensor"), None),
        P(("dp", "tensor"), None),
        P(("dp", "tensor")),
        P(None, "tensor"),
        P(None, "tensor"),
        P("tensor", None),
        P(("dp", "tensor"), None),
    )
    fits = mesh.shape["dp"] == 8 and mesh.shape["tensor"] == 4
    return jax.shard_map(
        fast_shards if fits else shards,
        mesh=mesh,
        in_specs=placed,
        out_specs=(
            P(("dp", "tensor"), None),
            P(("dp", "tensor"), None),
            P(("dp", "tensor")),
            P(("dp", "tensor"), None),
            P(("dp", "tensor"), None),
            P(("dp", "tensor"), None),
            P(("dp", "tensor"), None),
            P(("dp", "tensor")),
            P("dp", "tensor"),
            P("dp", "tensor"),
            P("tensor", "dp"),
        ),
        check_vma=False,
    )
```

```python
import functools
import math

import jax
import jax.numpy as jnp
import numpy as np
from jax import lax
from jax.experimental import pallas as pl
from jax.experimental.pallas import tpu as pltpu
from jax.sharding import PartitionSpec as P

F32 = jnp.float32
BF16 = jnp.bfloat16
MESH = pl.DeviceIdType.MESH
EPSILON = 1e-05
ROPE_BASE = 100000.0
MASKED = -1e30
HEAD = 96
VMEM_LIMIT = 64 * 2**20 - 65536


def rotary_tables(rows, shards_in_sequence):
    half = HEAD // 2
    lanes = np.arange(4 * HEAD) % half
    rates = ROPE_BASE ** (-(lanes * 2.0) / HEAD)
    near = np.arange(rows)[:, None] * rates[None, :]
    far = (np.arange(shards_in_sequence) * rows)[:, None] * rates[None, :]
    shift = np.concatenate([np.cos(far), np.sin(far)], axis=0)
    return (
        np.cos(near).astype(np.float32),
        np.sin(near).astype(np.float32),
        shift.astype(np.float32),
    )


def tensor_peer(t, m):
    if m == 1:
        return t + 1 - 2 * lax.rem(t, 2)
    if m == 2:
        return lax.rem(t + 2, 4)
    return 3 - t


def dp_peer(d, m):
    if m & 1:
        d = d + 1 - 2 * lax.rem(d, 2)
    if m & 2:
        d = d + 2 - 4 * lax.rem(lax.div(d, 2), 2)
    if m & 4:
        d = lax.rem(d + 4, 8)
    return d


class Links:
    def __init__(self, tsend, trecv, dsend, drecv):
        self.t = lax.axis_index("tensor")
        self.d = lax.axis_index("dp")
        self.mid = lax.rem(lax.div(self.t + 1, 2), 2)
        self.tsend, self.trecv, self.dsend, self.drecv = tsend, trecv, dsend, drecv

    def shard_at(self, i):
        t, mid = self.t, self.mid
        near, two, three = (tensor_peer(t, m) for m in (1, 2, 3))
        if isinstance(i, int):
            if i == 0:
                return t, 0
            if i == 1:
                return near, 1
            if i == 2:
                return two + mid * (three - two), 2 + mid
            return three + mid * (two - three), 3 - mid
        one_if = [1 - jnp.minimum(jnp.abs(i - k), 1) for k in range(4)]
        pairs = [self.shard_at(k) for k in range(4)]
        return (
            sum(f * p[0] for f, p in zip(one_if, pairs)),
            sum(f * p[1] for f, p in zip(one_if, pairs)),
        )

    def over_tensor(self, kind, m, src, dst, recv=None):
        peer = tensor_peer(self.t, m)
        return pltpu.make_async_remote_copy(
            src_ref=src,
            dst_ref=dst,
            send_sem=self.tsend.at[kind, m],
            recv_sem=self.trecv.at[kind, m if recv is None else recv],
            device_id={"dp": self.d, "tensor": peer},
            device_id_type=MESH,
        )

    def over_dp(self, kind, m, src, dst, to=None):
        peer = dp_peer(self.d, m if to is None else to)
        return pltpu.make_async_remote_copy(
            src_ref=src,
            dst_ref=dst,
            send_sem=self.dsend.at[kind, m],
            recv_sem=self.drecv.at[kind, m],
            device_id={"dp": peer, "tensor": self.t},
            device_id_type=MESH,
        )

    def landed_tensor(self, kind, m, ref):
        pltpu.make_async_copy(ref, ref, self.trecv.at[kind, m]).wait()

    def landed_dp(self, kind, m, ref):
        pltpu.make_async_copy(ref, ref, self.drecv.at[kind, m]).wait()

    def gather_start(self, kind, src, at):
        own = at(self.t)
        self.over_tensor(kind, 1, src, own).start()

        @pl.when(self.mid == 0)
        def _():
            self.over_tensor(kind, 2, src, own).start()

        @pl.when(self.mid == 1)
        def _():
            self.over_tensor(kind, 3, src, own).start()

    def gather_take(self, kind, i, at):
        shard, m = self.shard_at(i)
        block = at(shard)
        self.landed_tensor(kind, m, block)

        def hand_on():
            pltpu.make_async_remote_copy(
                src_ref=block,
                dst_ref=block,
                send_sem=self.tsend.at[kind, 2 + i],
                recv_sem=self.trecv.at[kind, 5 - m],
                device_id={"dp": self.d, "tensor": tensor_peer(self.t, 1)},
                device_id_type=MESH,
            ).start()

        if isinstance(i, int):
            if i >= 2:
                pl.when(self.mid == 1)(hand_on)
        else:
            pl.when((self.mid == 1) & (i >= 2))(hand_on)

    def gather_end(self, kind, src, at):
        own = at(self.t)
        self.over_tensor(kind, 1, src, own).wait_send()

        @pl.when(self.mid == 0)
        def _():
            self.over_tensor(kind, 2, src, own).wait_send()

        @pl.when(self.mid == 1)
        def _():
            self.over_tensor(kind, 3, src, own).wait_send()
            for i in (2, 3):
                shard, m = self.shard_at(i)
                pltpu.make_async_copy(at(shard), at(shard), self.tsend.at[kind, 2 + i]).wait()

    def barrier(self, tensor_peers, dp_peers):
        sem = pltpu.get_barrier_semaphore()
        for m in tensor_peers:
            pl.semaphore_signal(
                sem,
                inc=1,
                device_id={"dp": self.d, "tensor": tensor_peer(self.t, m)},
                device_id_type=MESH,
            )
        for m in dp_peers:
            pl.semaphore_signal(
                sem,
                inc=1,
                device_id={"dp": dp_peer(self.d, m), "tensor": self.t},
                device_id_type=MESH,
            )
        pl.semaphore_wait(sem, len(tensor_peers) + len(dp_peers))


def mm(a, b, dims=((1,), (0,))):
    return lax.dot_general(a, b, (dims, ((), ())), preferred_element_type=F32)


NN = ((1,), (0,))
NT = ((1,), (1,))
TN = ((0,), (0,))


def lane_roll(u, by):
    return pltpu.roll(u, by % u.shape[-1], u.ndim - 1)


def swap_halves(u):
    lane = lax.broadcasted_iota(jnp.int32, u.shape, 1)
    low = lax.rem(lane, HEAD) < HEAD // 2
    return jnp.where(low, -lane_roll(u, -(HEAD // 2)), lane_roll(u, HEAD // 2))


def turn_tables(near_cos, near_sin, shift, shard):
    c = shift[pl.ds(shard, 1), :]
    s = shift[pl.ds(shard + 4, 1), :]
    a, b = near_cos[...], near_sin[...]
    return a * c - b * s, b * c + a * s


class LineSum:
    def __init__(self, ln, kind, src, recv):
        self.ln, self.kind, self.src, self.recv = ln, kind, src, recv
        t = ln.t
        self.near, self.two, self.three = (tensor_peer(t, m) for m in (1, 2, 3))

    def copy(self, src, to, slot, sem):
        ln, kind = self.ln, self.kind
        return pltpu.make_async_remote_copy(
            src_ref=src,
            dst_ref=self.recv.at[slot],
            send_sem=ln.tsend.at[kind, sem],
            recv_sem=ln.trecv.at[kind, slot],
            device_id={"dp": ln.d, "tensor": to},
            device_id_type=MESH,
        )

    def first(self, i, shard):
        c = self.copy(self.src.at[shard], self.near, i, i)
        if isinstance(i, int):
            if i == 2:
                c.start()
            else:
                pl.when(self.ln.mid == 0)(c.start)
        else:
            pl.when((i == 2) | ((self.ln.mid == 0) & (i < 2)))(c.start)

    def start(self):
        for i, shard in enumerate((self.three, self.two, self.near)):
            self.first(i, shard)

    def hand_on(self):
        @pl.when(self.ln.mid == 1)
        def _():
            for i, shard in enumerate((self.two, self.three)):
                self.ln.landed_tensor(self.kind, i, self.recv.at[i])
                self.recv[i] = (
                    self.recv[i].astype(F32) + self.src[shard].astype(F32)
                ).astype(BF16)
                self.copy(self.recv.at[i], shard, 3, i).start()

    def take(self):
        for i in (2, 3):
            self.ln.landed_tensor(self.kind, i, self.recv.at[i])
        return self.recv[2].astype(F32) + self.recv[3].astype(F32)

    def end(self):
        for i in range(3):
            pltpu.make_async_copy(
                self.src.at[0], self.src.at[0], self.ln.tsend.at[self.kind, i]
            ).wait()


class PlaneSum:
    def __init__(self, ln, kind, src, recv):
        self.ln, self.kind, self.src, self.recv = ln, kind, src, recv
        j = lax.div(ln.d, 2)
        self.j = j
        self.x = j + 1 - 2 * lax.rem(j, 2)
        self.y = lax.rem(j + 2, 4)
        self.diag = lax.rem(self.x + 2, 4)
        self.lanes = src.shape[-1] // 2

    def half(self, ref, h):
        spot = [slice(None)] * (len(ref.shape) - 1) + [pl.ds(h * self.lanes, self.lanes)]
        return ref.at[tuple(spot)]

    def copy(self, src, m, i):
        return self.ln.over_dp(self.kind, i, src, self.recv.at[i], to=m)

    def plan(self):
        return (
            (self.half(self.src.at[self.diag], 0), 2, 0),
            (self.half(self.src.at[self.diag], 1), 4, 2),
            (self.half(self.src.at[self.x], 0), 2, 1),
            (self.half(self.src.at[self.y], 1), 4, 3),
        )

    def start(self):
        for src, m, i in self.plan():
            self.copy(src, m, i).start()

    def hand_on(self):
        for i, h, block, m in ((0, 0, self.y, 4), (2, 1, self.x, 2)):
            self.ln.landed_dp(self.kind, i, self.recv.at[i])
            self.recv[i] = (
                self.recv[i].astype(F32) + self.half(self.src.at[block], h)[...].astype(F32)
            ).astype(BF16)
            self.copy_on(i, h, m).start()

    def copy_on(self, i, h, m):
        return self.ln.over_dp(self.kind, 4 + h, self.recv.at[i], self.recv.at[4 + h], to=m)

    def take(self, h):
        for i in (1 + 2 * h, 4 + h):
            self.ln.landed_dp(self.kind, i, self.recv.at[i])
        own = self.half(self.src.at[self.j], h)[...].astype(F32)
        return own + self.recv[1 + 2 * h].astype(F32) + self.recv[4 + h].astype(F32)

    def end(self):
        for src, m, i in self.plan():
            self.copy(src, m, i).wait_send()
        for i, h, m in ((0, 0, 4), (2, 1, 2)):
            self.copy_on(i, h, m).wait_send()


class CoreSum:
    def __init__(self, ln, kind, src, recv):
        self.ln, self.kind, self.src, self.recv = ln, kind, src, recv
        self.half = recv.shape[1]
        self.core = lax.rem(ln.d, 2)

    def side(self, which):
        return pl.ds(pl.multiple_of(which * self.half, self.half), self.half)

    def copy(self, j):
        ln = self.ln
        return pltpu.make_async_remote_copy(
            src_ref=self.src.at[j, self.side(1 - self.core), :],
            dst_ref=self.recv.at[j],
            send_sem=ln.dsend.at[self.kind, j],
            recv_sem=ln.drecv.at[self.kind, j],
            device_id={"dp": dp_peer(ln.d, 1), "tensor": ln.t},
            device_id_type=MESH,
        )

    def take(self):
        def one(j, carry):
            self.copy(j).wait_recv()
            self.recv[j] = (
                self.recv[j].astype(F32) + self.src[j, self.side(self.core), :].astype(F32)
            ).astype(BF16)
            return carry

        lax.fori_loop(0, 4, one, 0)

    def end(self):
        def one(j, carry):
            self.copy(j).wait_send()
            return carry

        lax.fori_loop(0, 4, one, 0)


def layer_kernel(
    hid, cot, tile, wpack, wo, wg, wu, wd, near_cos, near_sin, shift,
    layer_out, gin_out, gain_out, wqkv_out, wo_out, mlpw_out,
    xall, nall, call, w, wof, tiles, qh, kh, vh, att, arow, lse, start, gains, resid, normed2,
    grecv, ff, msend, gatt, gres, low, gain,
    gall, mlp_in, ff_in, wo_core, wo_in, wo_src, wo_line, wq_core, wq_in, wq_src, wq_all,
    rows_in, line_in, gsum,
    tsend, trecv, dsend, drecv, local, store,
):
    ln = Links(tsend, trecv, dsend, drecv)
    t, d = ln.t, ln.d
    rows, width = hid.shape
    units = wg.shape[1]
    seq = 4 * rows
    span = width // 4
    half = span // 2
    core = lax.rem(d, 2)
    wrows = wo.shape[0]
    srows = 4 * wrows
    TILE, W, X, O, C, A, N, G, GA, M, B, OL, WL, R = range(14)
    DT, DW, FW, DO, FO, DF, DR, CO, DOS, CW, DWS, CK = range(12)
    V = pltpu.VMEM

    def ds_of(shard):
        return pl.ds(pl.multiple_of(shard * rows, rows), rows)

    def rows_at(ref, shard):
        return ref.at[ds_of(shard), :]

    def w_at(ref, dd, tt=None):
        if tt is None:
            return ref.at[pl.ds(pl.multiple_of(dd * srows, 16), srows), :]
        return ref.at[pl.ds(pl.multiple_of(dd * srows + tt * wrows, 16), wrows), :]

    x_of = functools.partial(rows_at, xall)
    c_of = functools.partial(rows_at, call)

    def wo_of(tt):
        return w_at(wof, d, tt)

    def columns(tt):
        return arow.at[:, pl.ds(pl.multiple_of(tt * span, 128), span)]

    at_own = ds_of(t)
    scale = 1.0 / math.sqrt(HEAD)
    layer_sum = LineSum(ln, M, msend, mlp_in)
    ff_sum = PlaneSum(ln, DF, ff, ff_in)

    def visible(shape, b):
        key = lax.broadcasted_iota(jnp.int32, shape, 0)
        query = lax.broadcasted_iota(jnp.int32, shape, 1) + b * rows
        first = start[:, b * rows : (b + 1) * rows].astype(jnp.int32)
        return (key <= query) & (key >= first)

    def front(outh):
        mine = [
            pltpu.make_async_copy(a, b, local.at[i])
            for i, (a, b) in enumerate(
                [(tile, tiles.at[d, t]), (wpack.at[t], w_at(w, d, t)), (wo, wo_of(t)),
                 (hid, x_of(t)), (cot, c_of(t))]
            )
        ]
        for c in mine:
            c.start()
        ln.barrier((1, 2, 3), (1, 2, 3, 4, 5, 6, 7))
        for m in (1, 2, 3):
            ln.over_tensor(TILE, m, tile, tiles.at[d, t]).start()
        for m in (1, 2, 3):
            ln.over_tensor(W, m, wpack.at[tensor_peer(t, m)], w_at(w, d, t)).start()
        ln.gather_start(O, wo, wo_of)
        ln.gather_start(X, hid, x_of)
        mine[0].wait()
        for m in (1, 2, 3):
            ln.landed_tensor(TILE, m, tiles.at[d, tensor_peer(t, m)])
        for m in range(1, 8):
            ln.over_dp(DT, m, tiles.at[d], tiles.at[d]).start()
        mine[1].wait()
        for m in (1, 2, 3):
            ln.landed_tensor(W, m, w_at(w, d, tensor_peer(t, m)))
        for m in (2, 4, 6, 1):
            ln.over_dp(DW, m, w_at(w, d), w_at(w, d)).start()
        mine[2].wait()
        for i in (1, 2, 3):
            ln.gather_take(O, i, wo_of)
        for m in (2, 4, 6, 1):
            ln.over_dp(DO, m, w_at(wof, d), w_at(wof, d)).start()
        for m in range(1, 8):
            ln.landed_dp(DT, m, tiles.at[dp_peer(d, m)])
        for m in (2, 4, 6):
            dd = dp_peer(d, m)
            ln.landed_dp(DW, m, w_at(w, dd))
            ln.over_dp(FW, m, w_at(w, dd), w_at(w, dd), to=1).start()
        for g in range(4):
            acc = jnp.zeros((8, 8 * wrows), F32)
            for j in range(8):
                r = 8 * g + j
                piece = jnp.concatenate(
                    [tiles[r // 4, r % 4], jnp.zeros((8, 8 * wrows - 128), F32)], axis=1
                )
                acc = acc + lane_roll(piece, wrows * j)
            gains[:, g * 8 * wrows : (g + 1) * 8 * wrows] = acc
        for s in range(4):
            start[:, s * rows : (s + 1) * rows] = tiles[d, s, 2:3, :]
        mine[3].wait()
        for i in (1, 2, 3):
            ln.gather_take(X, i, x_of)
        mine[4].wait()
        ln.gather_start(C, cot, c_of)
        ln.landed_dp(DW, 1, w_at(w, dp_peer(d, 1)))
        for m in (2, 4, 6):
            ln.landed_dp(FW, m, w_at(w, dp_peer(d, m ^ 1)))

        def project(s, carry):
            at = ds_of(s)
            x = xall[at, :].astype(F32)
            inv = lax.rsqrt(jnp.mean(x * x, axis=1, keepdims=True) + EPSILON)
            normed = (x * inv * gains[0:1, :]).astype(BF16)
            nall[at, :] = normed
            cosine, sine = turn_tables(near_cos, near_sin, shift, s)
            q = mm(normed, w[:, : 4 * HEAD])
            q = q * cosine + swap_halves(q) * sine
            kv = mm(normed, w[:, 4 * HEAD :])
            lane = lax.broadcasted_iota(jnp.int32, kv.shape, 1)
            kv = jnp.where(lane < 2 * HEAD, kv * cosine + swap_halves(kv) * sine, kv)
            keep = lax.broadcasted_iota(jnp.int32, (rows, 128), 1) < HEAD

            def head(u, h):
                return jnp.where(keep, lane_roll(u, -HEAD * h)[:, :128], 0.0).astype(BF16)

            for h in range(4):
                qh[h, at, :] = head(q, h)
            for c in range(2):
                kh[c, at, :] = head(kv, c)
                vh[c, at, :] = head(kv, c + 2)
            return carry

        lax.fori_loop(0, 4, project, 0)

        def attend(h, carry):
            @pl.when((h == 1) | (h == 3))
            def _():
                ln.gather_take(C, lax.div(h + 1, 2), c_of)

            c = lax.div(h, 2)
            for b in range(4):
                far = (b + 1) * rows
                here = slice(b * rows, far)
                sc = mm(kh[c, :far, :], qh[h, here, :], NT) * scale
                sc = jnp.where(visible(sc.shape, b), sc, MASKED)
                peak = jnp.max(sc, axis=0, keepdims=True)
                e = jnp.exp(sc - peak)
                total = jnp.sum(e, axis=0, keepdims=True)
                p = (e * (1.0 / total)).astype(BF16)
                outh[h, here, :] = mm(p, vh[c, :far, :], TN)
                lse[h, :, here] = peak + jnp.log(total)
            return carry

        lax.fori_loop(0, 4, attend, 0)

        def pack(b, carry):
            acc = jnp.zeros((rows, 4 * HEAD), F32)
            for h in range(4):
                piece = jnp.concatenate(
                    [outh[h, ds_of(b), :], jnp.zeros((rows, 4 * HEAD - 128), F32)], axis=1
                )
                acc = acc + lane_roll(piece, HEAD * h)
            att[b] = acc.astype(BF16)
            return carry

        lax.fori_loop(0, 4, pack, 0)
        ln.gather_end(X, hid, x_of)
        for m in (3, 2, 1):
            ln.over_tensor(A, m, att.at[tensor_peer(t, m)], columns(t)).start()
        own = pltpu.make_async_copy(att.at[t], columns(t), local.at[0])
        own.start()
        ln.gather_take(C, 3, c_of)
        for m in (2, 4, 6):
            dd = dp_peer(d, m)
            ln.landed_dp(DO, m, w_at(wof, dd))
            ln.over_dp(FO, m, w_at(wof, dd), w_at(wof, dd), to=1).start()
        ln.landed_dp(DO, 1, w_at(wof, dp_peer(d, 1)))
        for m in (2, 4, 6):
            ln.landed_dp(FO, m, w_at(wof, dp_peer(d, m ^ 1)))
        own.wait()
        for m in (1, 2, 3):
            ln.landed_tensor(A, m, columns(tensor_peer(t, m)))
        third = width // 3

        def project_out(n, carry):
            cols = pl.ds(pl.multiple_of(n * third, 128), third)
            resid[:, cols] = xall[at_own, cols].astype(F32) + mm(arow[...], wof[:, cols])
            return carry

        lax.fori_loop(0, 3, project_out, 0)
        r = resid[...]
        inv = lax.rsqrt(jnp.mean(r * r, axis=1, keepdims=True) + EPSILON)
        normed2[...] = (r * inv * gains[1:2, :]).astype(BF16)
        ln.gather_start(N, normed2, x_of)
        xall[at_own, :] = normed2[...]

    def feed(loads, gate_w, up_w, down_w, act, gg, gu, gsend, gown, part):
        for c in loads:
            c.wait()

        def to_owner(shard, m):
            return pltpu.make_async_remote_copy(
                src_ref=gsend.at[shard],
                dst_ref=grecv.at[m - 1],
                send_sem=tsend.at[G, m],
                recv_sem=trecv.at[G, m],
                device_id={"dp": d, "tensor": shard},
                device_id_type=MESH,
            )

        def one_shard(i, carry):
            shard, m = ln.shard_at(i)

            @pl.when(i > 0)
            def _():
                ln.gather_take(N, i, x_of)

            at = ds_of(shard)
            r = xall[at, :]
            gate = mm(r, gate_w[...])
            up = mm(r, up_w[...])
            sig = 1.0 / (1.0 + jnp.exp(-gate))
            silu = gate * sig
            act[at, :] = (silu * up).astype(BF16)
            g_act = mm(call[at, :], down_w[...], NT)
            gg[at, :] = (g_act * up * sig * (1.0 + gate * (1.0 - sig))).astype(BF16)
            gu[at, :] = (g_act * silu).astype(BF16)
            g = mm(gg[at, :], gate_w[...], NT) + mm(gu[at, :], up_w[...], NT)

            @pl.when(i == 0)
            def _():
                gown[...] = g

            @pl.when(i > 0)
            def _():
                gsend[shard] = g.astype(BF16)
                to_owner(shard, m).start()

            msend[shard] = mm(act[at, :], down_w[...]).astype(BF16)
            return carry

        lax.fori_loop(0, 4, one_shard, 0)
        layer_sum.first(0, layer_sum.three)
        layer_sum.first(1, layer_sum.two)

        def side(which):
            return pl.ds(pl.multiple_of(which * half, half), half)

        def to_core(k, j):
            return pltpu.make_async_remote_copy(
                src_ref=part.at[lax.rem(j, 2), k, side(1 - core), :],
                dst_ref=ff.at[j, k],
                send_sem=dsend.at[CK + k, j],
                recv_sem=drecv.at[CK + k, j],
                device_id={"dp": dp_peer(d, 1), "tensor": t},
                device_id_type=MESH,
            )

        def chip_sum(j):
            for k in range(3):
                to_core(k, j).wait_recv()
                ff[j, k] = (
                    part[lax.rem(j, 2), k, side(core), :].astype(F32) + ff[j, k].astype(F32)
                ).astype(BF16)
                to_core(k, j).wait_send()

        def weights(j, carry):
            cols = pl.ds(pl.multiple_of(j * span, 128), span)
            for k, (a, b) in enumerate(((xall, gg), (xall, gu), (call, act))):
                part[lax.rem(j, 2), k] = mm(a[:, cols], b[...], TN).astype(BF16)
                to_core(k, j).start()

            @pl.when(j > 0)
            def _():
                chip_sum(j - 1)

            return carry

        lax.fori_loop(0, 4, weights, 0)
        chip_sum(3)
        ff_sum.start()
        for m in (1, 2, 3):
            ln.landed_tensor(G, m, grecv.at[m - 1])
        g = gown[...]
        for m in (1, 2, 3):
            g = g + grecv[m - 1].astype(F32)
        r = resid[...]
        inv = lax.rsqrt(jnp.mean(r * r, axis=1, keepdims=True) + EPSILON)
        gain[0] = jnp.sum(g * r * inv, axis=0, keepdims=True)
        scaled = g * gains[1:2, :]
        gr = (
            call[at_own, :].astype(F32)
            + inv * scaled
            - r * (inv * inv * inv) * jnp.mean(scaled * r, axis=1, keepdims=True)
        )
        gres[...] = gr
        low[...] = gr.astype(BF16)
        for s in range(4):
            gatt[s] = mm(low[...], wof[s * span : (s + 1) * span, :], NT).astype(BF16)
        for m in (1, 2, 3):
            to_owner(tensor_peer(t, m), m).wait_send()

    def forward(gate_w, up_w, down_w):
        loads = [
            pltpu.make_async_copy(a, b, local.at[5 + i])
            for i, (a, b) in enumerate(((wg, gate_w), (wu, up_w), (wd, down_w)))
        ]
        for c in loads:
            c.start()
        pl.run_scoped(front, V((4, seq, 128), F32))
        hidden = V((seq, units), BF16)
        pl.run_scoped(
            functools.partial(feed, loads, gate_w, up_w, down_w),
            hidden, hidden, hidden, V((4, rows, width), BF16), V((rows, width), F32),
            V((2, 3, span, units), BF16),
        )

    pl.run_scoped(
        forward, V((width, units), BF16), V((width, units), BF16), V((units, width), BF16)
    )

    def backward(gh, gq, gk, gv, gqkv, gn_src, wo_part, wq_part, layer, gin, wqkv, wo_full, ffw):
        for m in (3, 2, 1):
            ln.over_tensor(GA, m, gatt.at[tensor_peer(t, m)], rows_at(gall, t)).start()
        own = [
            pltpu.make_async_copy(gatt.at[t], rows_at(gall, t), local.at[0]),
            pltpu.make_async_copy(gain, rows_in.at[pl.ds(d, 1)], local.at[1]),
        ]
        for c in own:
            c.start()
        for m in range(1, 8):
            ln.over_dp(DR, m, gain.at[0], rows_in.at[d]).start()
        layer_sum.first(2, layer_sum.near)
        wo_pair = CoreSum(ln, CO, wo_part, wo_core)

        def output_weights(j, carry):
            cols = pl.ds(pl.multiple_of(j * span, 128), span)
            wo_part[j] = mm(arow[:, cols], low[...], TN).astype(BF16)
            wo_pair.copy(j).start()
            return carry

        lax.fori_loop(0, 4, output_weights, 0)
        layer_sum.hand_on()
        own[0].wait()
        for m in (1, 2, 3):
            ln.landed_tensor(GA, m, rows_at(gall, tensor_peer(t, m)))
        keep = lax.broadcasted_iota(jnp.int32, (rows, 128), 1) < HEAD

        def split(b, carry):
            u = gall[ds_of(b), :].astype(F32)
            for h in range(4):
                gh[h, ds_of(b), :] = jnp.where(
                    keep, lane_roll(u, -HEAD * h)[:, :128], 0.0
                ).astype(BF16)
            return carry

        lax.fori_loop(0, 4, split, 0)
        gk[...] = jnp.zeros_like(gk)
        gv[...] = jnp.zeros_like(gv)
        wo_pair.take()
        wo_sum = PlaneSum(ln, DOS, wo_core, wo_in)
        wo_sum.start()

        def attend_back(h, carry):
            c = lax.div(h, 2)
            for b in range(4):
                far = (b + 1) * rows
                here = slice(b * rows, far)
                k, v, q, g = kh[c, :far, :], vh[c, :far, :], qh[h, here, :], gh[h, here, :]
                sc = mm(k, q, NT) * scale
                sc = jnp.where(visible(sc.shape, b), sc, MASKED)
                p = jnp.exp(sc - lse[h, :, here])
                gp = mm(v, g, NT)
                gs = (p * (gp - jnp.sum(p * gp, axis=0, keepdims=True))).astype(BF16)
                gq[h, here, :] = mm(gs, k, TN) * scale
                gk[c, :far, :] += mm(gs, q) * scale
                gv[c, :far, :] += mm(p.astype(BF16), g)
            return carry

        lax.fori_loop(0, 4, attend_back, 0)

        def gather_heads(b, carry):
            at = ds_of(b)
            cosine, sine = turn_tables(near_cos, near_sin, shift, b)
            cosine, sine = cosine[:, :128], sine[:, :128]

            def placed(u, h):
                u = jnp.concatenate(
                    [jnp.where(keep, u, 0.0), jnp.zeros((rows, 4 * HEAD - 128), F32)], axis=1
                )
                return lane_roll(u, HEAD * h)

            def turned(u):
                return u * cosine - swap_halves(u) * sine

            left = sum(placed(turned(gq[h, at, :]), h) for h in range(4))
            right = sum(placed(turned(gk[c, at, :]), c) for c in range(2))
            right = right + sum(placed(gv[c, at, :], c + 2) for c in range(2))
            gqkv[at, : 4 * HEAD] = left.astype(BF16)
            gqkv[at, 4 * HEAD :] = right.astype(BF16)
            return carry

        lax.fori_loop(0, 4, gather_heads, 0)
        gn_sum = LineSum(ln, B, gn_src, grecv)

        def norm_grads(i, carry):
            shard, _ = ln.shard_at(3 - i)
            gn_src[shard] = mm(gqkv[ds_of(shard), :], w[...], NT).astype(BF16)
            gn_sum.first(i, shard)
            return carry

        lax.fori_loop(0, 4, norm_grads, 0)
        wq_pair = CoreSum(ln, CW, wq_part, wq_core)

        def head_weights(j, carry):
            cols = pl.ds(pl.multiple_of(j * span, 128), span)
            wq_part[j] = mm(nall[:, cols], gqkv[...], TN).astype(BF16)
            wq_pair.copy(j).start()
            return carry

        ff_sum.hand_on()
        lax.fori_loop(0, 4, head_weights, 0)
        wq_pair.take()
        wq_sum = PlaneSum(ln, DWS, wq_core, wq_in)
        wq_sum.start()
        gn_sum.hand_on()
        wo_sum.hand_on()

        own[1].wait()
        for m in range(1, 8):
            ln.landed_dp(DR, m, rows_in.at[dp_peer(d, m)])
        gsum[0] = sum(rows_in[i] for i in range(8))
        for m in (1, 2, 3):
            ln.over_tensor(R, m, gsum.at[0], line_in.at[m]).start()

        stores = []

        def out(a, b):
            c = pltpu.make_async_copy(a, b, store.at[len(stores)])
            c.start()
            stores.append(c)

        layer[...] = (resid[...] + msend[t].astype(F32) + layer_sum.take()).astype(BF16)
        out(layer, layer_out)
        lanes = ff_sum.lanes
        for h in range(2):
            ffw[:, :, h * lanes : (h + 1) * lanes] = ff_sum.take(h)
        out(ffw, mlpw_out)
        wq_sum.hand_on()
        x = hid[...].astype(F32)
        inv = lax.rsqrt(jnp.mean(x * x, axis=1, keepdims=True) + EPSILON)
        scaled = (gn_src[t].astype(F32) + gn_sum.take()) * gains[0:1, :]
        gin[...] = (
            gres[...]
            + inv * scaled
            - x * (inv * inv * inv) * jnp.mean(scaled * x, axis=1, keepdims=True)
        )
        out(gin, gin_out)
        lanes = wo_sum.lanes
        for h in range(2):
            u = wo_sum.take(h).astype(BF16)
            for s in range(4):
                wo_src[s, :, h * lanes : (h + 1) * lanes] = u[s * wrows : (s + 1) * wrows, :]
        wo_line_sum = LineSum(ln, OL, wo_src, wo_line)
        wo_line_sum.start()
        total = gsum[0]
        for m in (1, 2, 3):
            ln.landed_tensor(R, m, line_in.at[m])
            total = total + line_in[m]
        line_in[0] = total
        out(line_in.at[0], gain_out)
        lanes = wq_sum.lanes
        for h in range(2):
            u = wq_sum.take(h).astype(BF16)
            for s in range(4):
                wq_src[s, :, h * lanes : (h + 1) * lanes] = u[s * wrows : (s + 1) * wrows, :]
        for m in (3, 2, 1):
            ln.over_tensor(WL, m, wq_src.at[tensor_peer(t, m)], wq_all.at[m]).start()
        wqkv[pl.ds(t, 1)] = wq_src[pl.ds(t, 1)].astype(F32)
        wo_line_sum.hand_on()
        for m in (1, 2, 3):
            ln.landed_tensor(WL, m, wq_all.at[m])
            wqkv[pl.ds(tensor_peer(t, m), 1)] = wq_all[pl.ds(m, 1)].astype(F32)
        out(wqkv, wqkv_out)
        wo_full[...] = wo_src[t].astype(F32) + wo_line_sum.take()
        out(wo_full, wo_out)

        for m in (1, 2, 3):
            ln.over_tensor(TILE, m, tile, tiles.at[d, t]).wait_send()
            ln.over_tensor(W, m, wpack.at[tensor_peer(t, m)], w_at(w, d, t)).wait_send()
            ln.over_tensor(A, m, att.at[tensor_peer(t, m)], columns(t)).wait_send()
            ln.over_tensor(GA, m, gatt.at[tensor_peer(t, m)], rows_at(gall, t)).wait_send()
            ln.over_tensor(R, m, gsum.at[0], line_in.at[m]).wait_send()
            ln.over_tensor(WL, m, wq_src.at[tensor_peer(t, m)], wq_all.at[m]).wait_send()
        ln.gather_end(O, wo, wo_of)
        ln.gather_end(C, cot, c_of)
        ln.gather_end(N, normed2, x_of)
        for m in range(1, 8):
            ln.over_dp(DT, m, tiles.at[d], tiles.at[d]).wait_send()
            ln.over_dp(DR, m, gain.at[0], rows_in.at[d]).wait_send()
        for m in (2, 4, 6, 1):
            ln.over_dp(DW, m, w_at(w, d), w_at(w, d)).wait_send()
            ln.over_dp(DO, m, w_at(wof, d), w_at(wof, d)).wait_send()
        for m in (2, 4, 6):
            dd = dp_peer(d, m)
            ln.over_dp(FW, m, w_at(w, dd), w_at(w, dd), to=1).wait_send()
            ln.over_dp(FO, m, w_at(wof, dd), w_at(wof, dd), to=1).wait_send()
        for s in (layer_sum, gn_sum, wo_line_sum, ff_sum, wo_sum, wq_sum, wo_pair, wq_pair):
            s.end()
        for c in stores:
            c.wait()

    pl.run_scoped(
        backward,
        V((4, seq, 128), BF16), V((4, seq, 128), F32), V((2, seq, 128), F32),
        V((2, seq, 128), F32), V((seq, 8 * HEAD), BF16), V((4, rows, width), BF16),
        V((4, span, width), BF16), V((4, span, 8 * HEAD), BF16),
        V((rows, width), BF16), V((rows, width), F32), V((4, wrows, 8 * HEAD), F32),
        V((wrows, width), F32), V((3, half, units), F32),
    )


def layer(hid, cot, positions, gain_attn, gain_mlp, wq, wk, wv, wo, wg, wu, wd):
    rows, width = hid.shape
    wrows = wq.shape[0]
    units = wg.shape[1]
    seq = 4 * rows
    span = width // 4
    half = span // 2
    t = lax.axis_index("tensor")
    index = t * rows + jnp.arange(rows, dtype=jnp.int32)
    pad = (0, 128 - wrows)
    tile = jnp.stack(
        [
            jnp.pad(gain_attn.astype(F32), pad),
            jnp.pad(gain_mlp.astype(F32), pad),
            (index - positions).astype(F32),
        ]
        + [jnp.zeros((128,), F32)] * 5
    )
    wpack = jnp.concatenate(
        [a.reshape(wrows, 4, a.shape[1] // 4).transpose(1, 0, 2) for a in (wq, wk, wv)], axis=2
    )
    near_cos, near_sin, shift = rotary_tables(rows, 4)
    hbm = pl.BlockSpec(memory_space=pl.ANY)
    vmem = pl.BlockSpec(memory_space=pltpu.VMEM)
    V = pltpu.VMEM
    shapes = dict(
        layer=((rows, width), BF16), gin=((rows, width), F32), gain=((1, width), F32),
        wqkv=((4, wrows, 8 * HEAD), F32), wo=((wrows, width), F32),
        mlp=((3, half, units), F32),
    )
    wide = V((seq, width), BF16)
    thin, thin_f = V((rows, width), BF16), V((rows, width), F32)
    four = V((4, rows, width), BF16)
    pair = V((2, seq, 128), BF16)
    outs = pl.pallas_call(
        layer_kernel,
        out_shape=[jax.ShapeDtypeStruct(*v) for v in shapes.values()],
        in_specs=[vmem] + [hbm] * 7 + [vmem] * 3,
        out_specs=[hbm] * len(shapes),
        scratch_shapes=[
            wide, wide, wide, V((width, 8 * HEAD), BF16), V((width, width), BF16),
            V((8, 4, 8, 128), F32), V((4, seq, 128), BF16), pair, pair,
            V((4, rows, span), BF16), thin, V((4, 1, seq), F32), V((1, seq), F32),
            V((8, width), F32), thin_f, thin,
            four, V((4, 3, half, units), BF16), four, V((4, rows, span), BF16), thin_f, thin,
            V((1, 1, width), F32),
            V((seq, span), BF16), four, V((6, 3, half, units // 2), BF16),
            V((4, half, width), BF16), V((6, half, width // 2), BF16),
            V((4, wrows, width), BF16), V((4, wrows, width), BF16),
            V((4, half, 8 * HEAD), BF16), V((6, half, 4 * HEAD), BF16),
            V((4, wrows, 8 * HEAD), BF16), V((4, wrows, 8 * HEAD), BF16),
            V((8, 1, width), F32), V((4, 1, width), F32), V((1, 1, width), F32),
            pltpu.SemaphoreType.DMA((14, 6)), pltpu.SemaphoreType.DMA((14, 4)),
            pltpu.SemaphoreType.DMA((14, 8)), pltpu.SemaphoreType.DMA((14, 8)),
            pltpu.SemaphoreType.DMA((8,)), pltpu.SemaphoreType.DMA((6,)),
        ],
        name="layer",
        compiler_params=pltpu.CompilerParams(
            collective_id=0, has_side_effects=True, vmem_limit_bytes=VMEM_LIMIT
        ),
    )(hid, cot, tile, wpack, wo, wg, wu, wd, near_cos, near_sin, shift)
    return dict(zip(shapes, outs))


QUERY_HEADS = 16
KEY_VALUE_HEADS = 8
HEAD_DIMENSION = 96


def angle_tables(pos_rows, head_size):
    half_size = head_size // 2
    freq_rates = ROPE_BASE ** (-(jnp.arange(half_size, dtype=jnp.float32) * 2.0) / head_size)
    turned = pos_rows.astype(jnp.float32)[:, None] * freq_rates[None, :]
    return (jnp.cos(turned)[:, None, :], jnp.sin(turned)[:, None, :])


def apply_rotary(tensor_in, cosine_table, sine_table):
    half_size = tensor_in.shape[-1] // 2
    lo_half = tensor_in[..., :half_size]
    hi_half = tensor_in[..., half_size:]
    return jnp.concatenate(
        [
            lo_half * cosine_table - hi_half * sine_table,
            hi_half * cosine_table + lo_half * sine_table,
        ],
        axis=-1,
    )


def shards(
    hidden_in,
    positions,
    gain_attn,
    w_query,
    key_matrix,
    value_matrix,
    w_output,
    gain_mlp,
    w_gate,
    w_up,
    w_down,
    cotangent,
):
    tok_rows = hidden_in.shape[0]
    model_width = hidden_in.shape[1]
    num_heads = QUERY_HEADS
    key_value_count = KEY_VALUE_HEADS
    head_size = HEAD_DIMENSION
    kv_width = key_value_count * head_size
    queries_per_group = num_heads // key_value_count
    seq_len = tok_rows * lax.axis_size("tensor")
    score_scale = 1.0 / math.sqrt(head_size)
    gathered = (
        lax.all_gather(gain_attn, ("dp", "tensor"), axis=0, tiled=True),
        lax.all_gather(w_query, ("dp", "tensor"), axis=0, tiled=True),
        lax.all_gather(key_matrix, ("dp", "tensor"), axis=0, tiled=True),
        lax.all_gather(value_matrix, ("dp", "tensor"), axis=0, tiled=True),
        lax.all_gather(w_output, ("dp", "tensor"), axis=0, tiled=True),
        lax.all_gather(gain_mlp, ("dp", "tensor"), axis=0, tiled=True),
    )
    gain_one, query_full, key_full, value_full, output_full, gain_two = gathered
    gain_one_f = gain_one.astype(jnp.float32)
    gain_two_f = gain_two.astype(jnp.float32)
    x_float = hidden_in.astype(jnp.float32)
    inv_one = lax.rsqrt(jnp.mean(x_float * x_float, axis=-1, keepdims=True) + EPSILON)
    normed_one = (x_float * inv_one * gain_one_f).astype(jnp.bfloat16)
    queries = jnp.dot(normed_one, query_full, preferred_element_type=jnp.float32)
    key_projected = jnp.dot(normed_one, key_full, preferred_element_type=jnp.float32)
    value_proj = jnp.dot(normed_one, value_full, preferred_element_type=jnp.float32)
    cosine_table, sine_table = angle_tables(positions, head_size)
    rotated_query_rows = apply_rotary(
        queries.reshape(tok_rows, num_heads, head_size), cosine_table, sine_table
    ).astype(jnp.bfloat16)
    rotated_key_rows = (
        apply_rotary(
            key_projected.reshape(tok_rows, key_value_count, head_size), cosine_table, sine_table
        )
        .astype(jnp.bfloat16)
        .reshape(tok_rows, kv_width)
    )
    value_rows_lowered = value_proj.astype(jnp.bfloat16)
    keys_all, values_all = (
        lax.all_gather(rotated_key_rows, "tensor", axis=0, tiled=True),
        lax.all_gather(value_rows_lowered, "tensor", axis=0, tiled=True),
    )
    offset = lax.axis_index("tensor") * tok_rows
    query_index = offset + jnp.arange(tok_rows, dtype=jnp.int32)
    key_index = jnp.arange(seq_len, dtype=jnp.int32)
    visible = (key_index[None, :] <= query_index[:, None]) & (
        key_index[None, :] >= (query_index - positions)[:, None]
    )
    visible = jnp.tile(visible, (queries_per_group, 1))

    def split_queries(tensor_in):
        return (
            tensor_in.reshape(tok_rows, key_value_count, queries_per_group, head_size)
            .transpose(1, 2, 0, 3)
            .reshape(key_value_count, queries_per_group * tok_rows, head_size)
        )

    def split_keys(tensor_in):
        return tensor_in.reshape(seq_len, key_value_count, head_size).transpose(1, 0, 2)

    def merge_heads(tensor_in):
        return (
            tensor_in.reshape(key_value_count, queries_per_group, tok_rows, head_size)
            .transpose(2, 0, 1, 3)
            .reshape(tok_rows, model_width)
        )

    query_heads = split_queries(rotated_query_rows)
    k_heads = split_keys(keys_all)
    value_heads = split_keys(values_all)

    def attend(head_items):
        q_block, k_block, v_block = head_items
        scores = (
            jnp.einsum("qd,kd->qk", q_block, k_block, preferred_element_type=jnp.float32)
            * score_scale
        )
        scores = jnp.where(visible, scores, MASKED)
        peak = jnp.max(scores, axis=-1, keepdims=True)
        exp_vals = jnp.exp(scores - peak)
        total = jnp.sum(exp_vals, axis=-1, keepdims=True)
        probs = exp_vals / total
        out_block = jnp.einsum(
            "qk,kd->qd", probs.astype(jnp.bfloat16), v_block, preferred_element_type=jnp.float32
        )
        return (out_block, peak[:, 0] + jnp.log(total[:, 0]))

    attended_rows, log_total = lax.map(attend, (query_heads, k_heads, value_heads))
    attended_low = merge_heads(attended_rows).astype(jnp.bfloat16)
    resid_sum = x_float + jnp.dot(attended_low, output_full, preferred_element_type=jnp.float32)
    inv_two = lax.rsqrt(jnp.mean(resid_sum * resid_sum, axis=-1, keepdims=True) + EPSILON)
    normed_two = (resid_sum * inv_two * gain_two_f).astype(jnp.bfloat16)
    rows_all = lax.all_gather(normed_two, "tensor", axis=0, tiled=True)
    gate_val = jnp.dot(rows_all, w_gate, preferred_element_type=jnp.float32)
    up_val = jnp.dot(rows_all, w_up, preferred_element_type=jnp.float32)
    sig_gate = jax.nn.sigmoid(gate_val)
    silu_gate = gate_val * sig_gate
    act_low = (silu_gate * up_val).astype(jnp.bfloat16)
    mlp_sum = lax.psum_scatter(
        jnp.dot(act_low, w_down, preferred_element_type=jnp.float32).astype(jnp.bfloat16),
        "tensor",
        scatter_dimension=0,
        tiled=True,
    ).astype(jnp.float32)
    layer_out = (resid_sum + mlp_sum).astype(jnp.bfloat16)
    grad_float = cotangent.astype(jnp.float32)
    grad_all = lax.all_gather(cotangent, "tensor", axis=0, tiled=True)
    grad_down = jnp.einsum("sf,sd->fd", act_low, grad_all, preferred_element_type=jnp.float32)
    g_act = jnp.einsum("sd,fd->sf", grad_all, w_down, preferred_element_type=jnp.float32)
    g_gate = (g_act * up_val * sig_gate * (1.0 + gate_val * (1.0 - sig_gate))).astype(jnp.bfloat16)
    g_up = (g_act * silu_gate).astype(jnp.bfloat16)
    grad_gate = jnp.einsum("sd,sf->df", rows_all, g_gate, preferred_element_type=jnp.float32)
    grad_up = jnp.einsum("sd,sf->df", rows_all, g_up, preferred_element_type=jnp.float32)
    g_norm_two = lax.psum_scatter(
        (
            jnp.einsum("sf,df->sd", g_gate, w_gate, preferred_element_type=jnp.float32)
            + jnp.einsum("sf,df->sd", g_up, w_up, preferred_element_type=jnp.float32)
        ).astype(jnp.bfloat16),
        "tensor",
        scatter_dimension=0,
        tiled=True,
    ).astype(jnp.float32)
    scaled_two = gain_two_f * g_norm_two
    grad_gain_two = jnp.sum(g_norm_two * resid_sum * inv_two, axis=0)
    g_resid = (
        grad_float
        + inv_two * scaled_two
        - resid_sum * inv_two**3 * jnp.mean(scaled_two * resid_sum, axis=-1, keepdims=True)
    )
    g_resid_low = g_resid.astype(jnp.bfloat16)
    grad_output = jnp.einsum(
        "tc,td->cd", attended_low, g_resid_low, preferred_element_type=jnp.float32
    )
    g_att = jnp.einsum(
        "td,cd->tc", g_resid_low, output_full, preferred_element_type=jnp.float32
    ).astype(jnp.bfloat16)
    g_heads = split_queries(g_att)

    def attend_back(head_items):
        q_block, k_block, v_block, log_block, g_block = head_items
        scores = (
            jnp.einsum("qd,kd->qk", q_block, k_block, preferred_element_type=jnp.float32)
            * score_scale
        )
        scores = jnp.where(visible, scores, MASKED)
        probs = jnp.exp(scores - log_block[:, None])
        g_probs = jnp.einsum("qd,kd->qk", g_block, v_block, preferred_element_type=jnp.float32)
        g_scores = (probs * (g_probs - jnp.sum(probs * g_probs, axis=-1, keepdims=True))).astype(
            jnp.bfloat16
        )
        g_rq = (
            jnp.einsum("qk,kd->qd", g_scores, k_block, preferred_element_type=jnp.float32)
            * score_scale
        )
        g_rk = (
            jnp.einsum("qk,qd->kd", g_scores, q_block, preferred_element_type=jnp.float32)
            * score_scale
        )
        g_val = jnp.einsum(
            "qk,qd->kd", probs.astype(jnp.bfloat16), g_block, preferred_element_type=jnp.float32
        )
        return (g_rq, g_rk, g_val)

    g_rq, g_rk, g_val = lax.map(
        attend_back, (query_heads, k_heads, value_heads, log_total, g_heads)
    )
    g_rk_flat = g_rk.transpose(1, 0, 2).reshape(seq_len, kv_width)
    g_val_flat = g_val.transpose(1, 0, 2).reshape(seq_len, kv_width)
    key_part, value_part = (
        lax.psum_scatter(
            g_rk_flat.astype(jnp.bfloat16), "tensor", scatter_dimension=0, tiled=True
        ).astype(jnp.float32),
        lax.psum_scatter(
            g_val_flat.astype(jnp.bfloat16), "tensor", scatter_dimension=0, tiled=True
        ).astype(jnp.float32),
    )
    g_queries = (
        apply_rotary(
            merge_heads(g_rq).reshape(tok_rows, num_heads, head_size), cosine_table, -sine_table
        )
        .reshape(tok_rows, model_width)
        .astype(jnp.bfloat16)
    )
    g_keys = (
        apply_rotary(
            key_part.reshape(tok_rows, key_value_count, head_size), cosine_table, -sine_table
        )
        .reshape(tok_rows, kv_width)
        .astype(jnp.bfloat16)
    )
    g_values = value_part.astype(jnp.bfloat16)
    grad_query = jnp.einsum("tc,td->cd", normed_one, g_queries, preferred_element_type=jnp.float32)
    grad_key = jnp.einsum("tc,td->cd", normed_one, g_keys, preferred_element_type=jnp.float32)
    grad_value = jnp.einsum("tc,td->cd", normed_one, g_values, preferred_element_type=jnp.float32)
    g_norm_one = (
        jnp.einsum("td,cd->tc", g_queries, query_full, preferred_element_type=jnp.float32)
        + jnp.einsum("td,cd->tc", g_keys, key_full, preferred_element_type=jnp.float32)
        + jnp.einsum("td,cd->tc", g_values, value_full, preferred_element_type=jnp.float32)
    )
    scaled_one = gain_one_f * g_norm_one
    grad_gain_one = jnp.sum(g_norm_one * x_float * inv_one, axis=0)
    grad_input = (
        g_resid
        + inv_one * scaled_one
        - x_float * inv_one**3 * jnp.mean(scaled_one * x_float, axis=-1, keepdims=True)
    )
    packed = jnp.concatenate([grad_query, grad_key, grad_value, grad_output], axis=1)
    packed_part = lax.psum_scatter(
        packed.astype(jnp.bfloat16), ("dp", "tensor"), scatter_dimension=0, tiled=True
    ).astype(jnp.float32)
    query_part = packed_part[:, :model_width]
    keyw_part = packed_part[:, model_width : model_width + kv_width]
    valuew_part = packed_part[:, model_width + kv_width : model_width + 2 * kv_width]
    out_part = packed_part[:, model_width + 2 * kv_width :]
    gain_one_part, gain_two_part = (
        lax.psum_scatter(grad_gain_one, ("dp", "tensor"), scatter_dimension=0, tiled=True),
        lax.psum_scatter(grad_gain_two, ("dp", "tensor"), scatter_dimension=0, tiled=True),
    )
    gate_sum, up_sum, down_sum = (
        lax.psum_scatter(
            grad_gate.astype(jnp.bfloat16), "dp", scatter_dimension=0, tiled=True
        ).astype(jnp.float32),
        lax.psum_scatter(
            grad_up.astype(jnp.bfloat16), "dp", scatter_dimension=0, tiled=True
        ).astype(jnp.float32),
        lax.psum_scatter(
            grad_down.astype(jnp.bfloat16), "dp", scatter_dimension=1, tiled=True
        ).astype(jnp.float32),
    )
    return (
        layer_out,
        grad_input,
        gain_one_part,
        query_part,
        keyw_part,
        valuew_part,
        out_part,
        gain_two_part,
        gate_sum,
        up_sum,
        down_sum,
    )


def fast_shards(
    hidden_in, positions, gain_attn, w_query, key_matrix, value_matrix, w_output, gain_mlp,
    w_gate, w_up, w_down, cotangent,
):
    b = layer(
        hidden_in, cotangent, positions, gain_attn, gain_mlp, w_query, key_matrix, value_matrix,
        w_output, w_gate, w_up, w_down,
    )
    wrows = w_query.shape[0]
    parts = b["wqkv"].transpose(1, 0, 2)
    query = parts[:, :, : 4 * HEAD].reshape(wrows, 16 * HEAD)
    key = parts[:, :, 4 * HEAD : 6 * HEAD].reshape(wrows, 8 * HEAD)
    value = parts[:, :, 6 * HEAD :].reshape(wrows, 8 * HEAD)

    def rows_of(w, g):
        return jnp.sum(w.astype(F32) * g, axis=1)

    gain_one = (
        rows_of(w_query, query) + rows_of(key_matrix, key) + rows_of(value_matrix, value)
    ) / gain_attn.astype(F32)
    mine = lax.axis_index("dp") * lax.axis_size("tensor") + lax.axis_index("tensor")
    gain_two = lax.dynamic_slice_in_dim(b["gain"][0], mine * wrows, wrows, 0)
    return (
        b["layer"], b["gin"], gain_one, query, key, value, b["wo"], gain_two,
        b["mlp"][0], b["mlp"][1], b["mlp"][2].T,
    )


def solution(mesh):
    placed = (
        P(("dp", "tensor"), None),
        P(("dp", "tensor")),
        P(("dp", "tensor")),
        P(("dp", "tensor"), None),
        P(("dp", "tensor"), None),
        P(("dp", "tensor"), None),
        P(("dp", "tensor"), None),
        P(("dp", "tensor")),
        P(None, "tensor"),
        P(None, "tensor"),
        P("tensor", None),
        P(("dp", "tensor"), None),
    )
    fits = mesh.shape["dp"] == 8 and mesh.shape["tensor"] == 4
    return jax.shard_map(
        fast_shards if fits else shards,
        mesh=mesh,
        in_specs=placed,
        out_specs=(
            P(("dp", "tensor"), None),
            P(("dp", "tensor"), None),
            P(("dp", "tensor")),
            P(("dp", "tensor"), None),
            P(("dp", "tensor"), None),
            P(("dp", "tensor"), None),
            P(("dp", "tensor"), None),
            P(("dp", "tensor")),
            P("dp", "tensor"),
            P("dp", "tensor"),
            P("tensor", "dp"),
        ),
        check_vma=False,
    )
```

```python
import functools
import math

import jax
import jax.numpy as jnp
import numpy as np
from jax import lax
from jax.experimental import pallas as pl
from jax.experimental.pallas import tpu as pltpu
from jax.sharding import PartitionSpec as P

F32 = jnp.float32
BF16 = jnp.bfloat16
MESH = pl.DeviceIdType.MESH
EPSILON = 1e-05
ROPE_BASE = 100000.0
MASKED = -1e30
HEAD = 96
VMEM_LIMIT = 64 * 2**20 - 65536


def rotary_tables(rows, shards_in_sequence):
    half = HEAD // 2
    lanes = np.arange(4 * HEAD) % half
    rates = ROPE_BASE ** (-(lanes * 2.0) / HEAD)
    near = np.arange(rows)[:, None] * rates[None, :]
    far = (np.arange(shards_in_sequence) * rows)[:, None] * rates[None, :]
    shift = np.concatenate([np.cos(far), np.sin(far)], axis=0)
    return (
        np.cos(near).astype(np.float32),
        np.sin(near).astype(np.float32),
        shift.astype(np.float32),
    )


def tensor_peer(t, m):
    if m == 1:
        return t + 1 - 2 * lax.rem(t, 2)
    if m == 2:
        return lax.rem(t + 2, 4)
    return 3 - t


def dp_peer(d, m):
    if m & 1:
        d = d + 1 - 2 * lax.rem(d, 2)
    if m & 2:
        d = d + 2 - 4 * lax.rem(lax.div(d, 2), 2)
    if m & 4:
        d = lax.rem(d + 4, 8)
    return d


class Links:
    def __init__(self, tsend, trecv, dsend, drecv):
        self.t = lax.axis_index("tensor")
        self.d = lax.axis_index("dp")
        self.mid = lax.rem(lax.div(self.t + 1, 2), 2)
        self.tsend, self.trecv, self.dsend, self.drecv = tsend, trecv, dsend, drecv

    def shard_at(self, i):
        t, mid = self.t, self.mid
        near, two, three = (tensor_peer(t, m) for m in (1, 2, 3))
        if isinstance(i, int):
            if i == 0:
                return t, 0
            if i == 1:
                return near, 1
            if i == 2:
                return two + mid * (three - two), 2 + mid
            return three + mid * (two - three), 3 - mid
        one_if = [1 - jnp.minimum(jnp.abs(i - k), 1) for k in range(4)]
        pairs = [self.shard_at(k) for k in range(4)]
        return (
            sum(f * p[0] for f, p in zip(one_if, pairs)),
            sum(f * p[1] for f, p in zip(one_if, pairs)),
        )

    def over_tensor(self, kind, m, src, dst, recv=None):
        peer = tensor_peer(self.t, m)
        return pltpu.make_async_remote_copy(
            src_ref=src,
            dst_ref=dst,
            send_sem=self.tsend.at[kind, m],
            recv_sem=self.trecv.at[kind, m if recv is None else recv],
            device_id={"dp": self.d, "tensor": peer},
            device_id_type=MESH,
        )

    def over_dp(self, kind, m, src, dst, to=None):
        peer = dp_peer(self.d, m if to is None else to)
        return pltpu.make_async_remote_copy(
            src_ref=src,
            dst_ref=dst,
            send_sem=self.dsend.at[kind, m],
            recv_sem=self.drecv.at[kind, m],
            device_id={"dp": peer, "tensor": self.t},
            device_id_type=MESH,
        )

    def landed_tensor(self, kind, m, ref):
        pltpu.make_async_copy(ref, ref, self.trecv.at[kind, m]).wait()

    def landed_dp(self, kind, m, ref):
        pltpu.make_async_copy(ref, ref, self.drecv.at[kind, m]).wait()

    def gather_start(self, kind, src, at):
        own = at(self.t)
        self.over_tensor(kind, 1, src, own).start()

        @pl.when(self.mid == 0)
        def _():
            self.over_tensor(kind, 2, src, own).start()

        @pl.when(self.mid == 1)
        def _():
            self.over_tensor(kind, 3, src, own).start()

    def gather_take(self, kind, i, at):
        shard, m = self.shard_at(i)
        block = at(shard)
        self.landed_tensor(kind, m, block)

        def hand_on():
            pltpu.make_async_remote_copy(
                src_ref=block,
                dst_ref=block,
                send_sem=self.tsend.at[kind, 2 + i],
                recv_sem=self.trecv.at[kind, 5 - m],
                device_id={"dp": self.d, "tensor": tensor_peer(self.t, 1)},
                device_id_type=MESH,
            ).start()

        if isinstance(i, int):
            if i >= 2:
                pl.when(self.mid == 1)(hand_on)
        else:
            pl.when((self.mid == 1) & (i >= 2))(hand_on)

    def gather_end(self, kind, src, at):
        own = at(self.t)
        self.over_tensor(kind, 1, src, own).wait_send()

        @pl.when(self.mid == 0)
        def _():
            self.over_tensor(kind, 2, src, own).wait_send()

        @pl.when(self.mid == 1)
        def _():
            self.over_tensor(kind, 3, src, own).wait_send()
            for i in (2, 3):
                shard, m = self.shard_at(i)
                pltpu.make_async_copy(at(shard), at(shard), self.tsend.at[kind, 2 + i]).wait()

    def barrier(self, tensor_peers, dp_peers):
        sem = pltpu.get_barrier_semaphore()
        for m in tensor_peers:
            pl.semaphore_signal(
                sem,
                inc=1,
                device_id={"dp": self.d, "tensor": tensor_peer(self.t, m)},
                device_id_type=MESH,
            )
        for m in dp_peers:
            pl.semaphore_signal(
                sem,
                inc=1,
                device_id={"dp": dp_peer(self.d, m), "tensor": self.t},
                device_id_type=MESH,
            )
        pl.semaphore_wait(sem, len(tensor_peers) + len(dp_peers))


def mm(a, b, dims=((1,), (0,))):
    return lax.dot_general(a, b, (dims, ((), ())), preferred_element_type=F32)


NN = ((1,), (0,))
NT = ((1,), (1,))
TN = ((0,), (0,))


def lane_roll(u, by):
    return pltpu.roll(u, by % u.shape[-1], u.ndim - 1)


def swap_halves(u):
    lane = lax.broadcasted_iota(jnp.int32, u.shape, 1)
    low = lax.rem(lane, HEAD) < HEAD // 2
    return jnp.where(low, -lane_roll(u, -(HEAD // 2)), lane_roll(u, HEAD // 2))


def turn_tables(near_cos, near_sin, shift, shard):
    c = shift[pl.ds(shard, 1), :]
    s = shift[pl.ds(shard + 4, 1), :]
    a, b = near_cos[...], near_sin[...]
    return a * c - b * s, b * c + a * s


class LineSum:
    def __init__(self, ln, kind, src, recv):
        self.ln, self.kind, self.src, self.recv = ln, kind, src, recv
        t = ln.t
        self.near, self.two, self.three = (tensor_peer(t, m) for m in (1, 2, 3))

    def copy(self, src, to, slot, sem):
        ln, kind = self.ln, self.kind
        return pltpu.make_async_remote_copy(
            src_ref=src,
            dst_ref=self.recv.at[slot],
            send_sem=ln.tsend.at[kind, sem],
            recv_sem=ln.trecv.at[kind, slot],
            device_id={"dp": ln.d, "tensor": to},
            device_id_type=MESH,
        )

    def first(self, i, shard):
        c = self.copy(self.src.at[shard], self.near, i, i)
        if isinstance(i, int):
            if i == 2:
                c.start()
            else:
                pl.when(self.ln.mid == 0)(c.start)
        else:
            pl.when((i == 2) | ((self.ln.mid == 0) & (i < 2)))(c.start)

    def start(self):
        for i, shard in enumerate((self.three, self.two, self.near)):
            self.first(i, shard)

    def hand_on(self):
        @pl.when(self.ln.mid == 1)
        def _():
            for i, shard in enumerate((self.two, self.three)):
                self.ln.landed_tensor(self.kind, i, self.recv.at[i])
                self.recv[i] = (
                    self.recv[i].astype(F32) + self.src[shard].astype(F32)
                ).astype(BF16)
                self.copy(self.recv.at[i], shard, 3, i).start()

    def take(self):
        for i in (2, 3):
            self.ln.landed_tensor(self.kind, i, self.recv.at[i])
        return self.recv[2].astype(F32) + self.recv[3].astype(F32)

    def end(self):
        for i in range(3):
            pltpu.make_async_copy(
                self.src.at[0], self.src.at[0], self.ln.tsend.at[self.kind, i]
            ).wait()


class PlaneSum:
    def __init__(self, ln, kind, src, recv):
        self.ln, self.kind, self.src, self.recv = ln, kind, src, recv
        j = lax.div(ln.d, 2)
        self.j = j
        self.x = j + 1 - 2 * lax.rem(j, 2)
        self.y = lax.rem(j + 2, 4)
        self.diag = lax.rem(self.x + 2, 4)
        self.lanes = src.shape[-1] // 2

    def half(self, ref, h):
        spot = [slice(None)] * (len(ref.shape) - 1) + [pl.ds(h * self.lanes, self.lanes)]
        return ref.at[tuple(spot)]

    def copy(self, src, m, i):
        return self.ln.over_dp(self.kind, i, src, self.recv.at[i], to=m)

    def plan(self):
        return (
            (self.half(self.src.at[self.diag], 0), 2, 0),
            (self.half(self.src.at[self.diag], 1), 4, 2),
            (self.half(self.src.at[self.x], 0), 2, 1),
            (self.half(self.src.at[self.y], 1), 4, 3),
        )

    def start(self):
        for src, m, i in self.plan():
            self.copy(src, m, i).start()

    def hand_on(self):
        for i, h, block, m in ((0, 0, self.y, 4), (2, 1, self.x, 2)):
            self.ln.landed_dp(self.kind, i, self.recv.at[i])
            self.recv[i] = (
                self.recv[i].astype(F32) + self.half(self.src.at[block], h)[...].astype(F32)
            ).astype(BF16)
            self.copy_on(i, h, m).start()

    def copy_on(self, i, h, m):
        return self.ln.over_dp(self.kind, 4 + h, self.recv.at[i], self.recv.at[4 + h], to=m)

    def take(self, h):
        for i in (1 + 2 * h, 4 + h):
            self.ln.landed_dp(self.kind, i, self.recv.at[i])
        own = self.half(self.src.at[self.j], h)[...].astype(F32)
        return own + self.recv[1 + 2 * h].astype(F32) + self.recv[4 + h].astype(F32)

    def end(self):
        for src, m, i in self.plan():
            self.copy(src, m, i).wait_send()
        for i, h, m in ((0, 0, 4), (2, 1, 2)):
            self.copy_on(i, h, m).wait_send()


class CoreSum:
    def __init__(self, ln, kind, src, recv):
        self.ln, self.kind, self.src, self.recv = ln, kind, src, recv
        self.half = recv.shape[1]
        self.core = lax.rem(ln.d, 2)

    def side(self, which):
        return pl.ds(pl.multiple_of(which * self.half, self.half), self.half)

    def copy(self, j):
        ln = self.ln
        return pltpu.make_async_remote_copy(
            src_ref=self.src.at[j, self.side(1 - self.core), :],
            dst_ref=self.recv.at[j],
            send_sem=ln.dsend.at[self.kind, j],
            recv_sem=ln.drecv.at[self.kind, j],
            device_id={"dp": dp_peer(ln.d, 1), "tensor": ln.t},
            device_id_type=MESH,
        )

    def take(self):
        def one(j, carry):
            self.copy(j).wait_recv()
            self.recv[j] = (
                self.recv[j].astype(F32) + self.src[j, self.side(self.core), :].astype(F32)
            ).astype(BF16)
            return carry

        lax.fori_loop(0, 4, one, 0)

    def end(self):
        def one(j, carry):
            self.copy(j).wait_send()
            return carry

        lax.fori_loop(0, 4, one, 0)


def layer_kernel(
    hid, cot, pos, gain_one, gain_two, wq, wk, wv, wo, wg, wu, wd, near_cos, near_sin, shift,
    layer_out, gin_out, gain_out, wqkv_out, wo_out, mlpw_out,
    xall, nall, call, w, wof, tiles, qh, kh, vh, att, arow, lse, start, gains, resid, normed2,
    grecv, ff, msend, gatt, gres, low, gain,
    gall, mlp_in, ff_in, wo_core, wo_in, wo_src, wo_line, wq_core, wq_in, wq_src, wq_all,
    rows_in, line_in, gsum, tile, wpack, gown_row,
    tsend, trecv, dsend, drecv, local, store,
):
    ln = Links(tsend, trecv, dsend, drecv)
    t, d = ln.t, ln.d
    rows, width = hid.shape
    units = wg.shape[1]
    seq = 4 * rows
    span = width // 4
    half = span // 2
    core = lax.rem(d, 2)
    wrows = wo.shape[0]
    srows = 4 * wrows
    TILE, W, X, O, C, A, N, G, GA, M, B, OL, WL, R = range(14)
    DT, DW, FW, DO, FO, DR, CO, DOS, CW, DWS, CK, DF = (*range(11), 13)
    V = pltpu.VMEM

    def ds_of(shard):
        return pl.ds(pl.multiple_of(shard * rows, rows), rows)

    def rows_at(ref, shard):
        return ref.at[ds_of(shard), :]

    def w_at(ref, dd, tt=None):
        if tt is None:
            return ref.at[pl.ds(pl.multiple_of(dd * srows, 16), srows), :]
        return ref.at[pl.ds(pl.multiple_of(dd * srows + tt * wrows, 16), wrows), :]

    x_of = functools.partial(rows_at, xall)
    c_of = functools.partial(rows_at, call)

    def wo_of(tt):
        return w_at(wof, d, tt)

    def columns(tt):
        return arow.at[:, pl.ds(pl.multiple_of(tt * span, 128), span)]

    at_own = ds_of(t)
    scale = 1.0 / math.sqrt(HEAD)
    layer_sum = LineSum(ln, M, msend, mlp_in)
    ff_sums = [
        PlaneSum(ln, DF + k, ff.at[:, k], ff_in.at[:, k]) for k in range(3)
    ]

    def visible(shape, b):
        key = lax.broadcasted_iota(jnp.int32, shape, 0)
        query = lax.broadcasted_iota(jnp.int32, shape, 1) + b * rows
        first = start[:, b * rows : (b + 1) * rows].astype(jnp.int32)
        return (key <= query) & (key >= first)

    def front(outh):
        tile[...] = jnp.zeros_like(tile)
        tile[0:1, :wrows] = gain_one[...].astype(F32)
        tile[1:2, :wrows] = gain_two[...].astype(F32)
        index = t * rows + lax.broadcasted_iota(jnp.int32, (1, rows), 1)
        tile[2:3, :] = (index - pos[...]).astype(F32)
        keys, values = wk[...].astype(F32), wv[...].astype(F32)
        pair = 2 * HEAD
        lane = lax.broadcasted_iota(jnp.int32, (wrows, span), 1)
        for s in range(4):
            wpack[s, :, :span] = wq[:, s * span : (s + 1) * span]
            wpack[s, :, span:] = jnp.where(
                lane < pair,
                lane_roll(keys, -pair * s)[:, :span],
                lane_roll(values, pair - pair * s)[:, :span],
            ).astype(BF16)
        mine = [
            pltpu.make_async_copy(a, b, local.at[i])
            for i, (a, b) in enumerate(
                [(tile, tiles.at[d, t]), (wpack.at[t], w_at(w, d, t)), (wo, wo_of(t)),
                 (hid, x_of(t)), (cot, c_of(t))]
            )
        ]
        for c in mine:
            c.start()
        ln.barrier((1, 2, 3), (1, 2, 3, 4, 5, 6, 7))
        for m in (1, 2, 3):
            ln.over_tensor(TILE, m, tile, tiles.at[d, t]).start()
        for m in (1, 2, 3):
            ln.over_tensor(W, m, wpack.at[tensor_peer(t, m)], w_at(w, d, t)).start()
        ln.gather_start(O, wo, wo_of)
        ln.gather_start(X, hid, x_of)
        mine[0].wait()
        for m in (1, 2, 3):
            ln.landed_tensor(TILE, m, tiles.at[d, tensor_peer(t, m)])
        for m in range(1, 8):
            ln.over_dp(DT, m, tiles.at[d], tiles.at[d]).start()
        mine[1].wait()
        for m in (1, 2, 3):
            ln.landed_tensor(W, m, w_at(w, d, tensor_peer(t, m)))
        for m in (2, 4, 6, 1):
            ln.over_dp(DW, m, w_at(w, d), w_at(w, d)).start()
        mine[2].wait()
        for i in (1, 2, 3):
            ln.gather_take(O, i, wo_of)
        for m in (2, 4, 6, 1):
            ln.over_dp(DO, m, w_at(wof, d), w_at(wof, d)).start()
        for m in range(1, 8):
            ln.landed_dp(DT, m, tiles.at[dp_peer(d, m)])
        for m in (2, 4, 6):
            dd = dp_peer(d, m)
            ln.landed_dp(DW, m, w_at(w, dd))
            ln.over_dp(FW, m, w_at(w, dd), w_at(w, dd), to=1).start()
        for g in range(4):
            acc = jnp.zeros((8, 8 * wrows), F32)
            for j in range(8):
                r = 8 * g + j
                piece = jnp.concatenate(
                    [tiles[r // 4, r % 4], jnp.zeros((8, 8 * wrows - 128), F32)], axis=1
                )
                acc = acc + lane_roll(piece, wrows * j)
            gains[:, g * 8 * wrows : (g + 1) * 8 * wrows] = acc
        for s in range(4):
            start[:, s * rows : (s + 1) * rows] = tiles[d, s, 2:3, :]
        mine[3].wait()
        for i in (1, 2, 3):
            ln.gather_take(X, i, x_of)
        mine[4].wait()
        ln.gather_start(C, cot, c_of)
        ln.landed_dp(DW, 1, w_at(w, dp_peer(d, 1)))
        for m in (2, 4, 6):
            ln.landed_dp(FW, m, w_at(w, dp_peer(d, m ^ 1)))

        def project(s, carry):
            at = ds_of(s)
            x = xall[at, :].astype(F32)
            inv = lax.rsqrt(jnp.mean(x * x, axis=1, keepdims=True) + EPSILON)
            normed = (x * inv * gains[0:1, :]).astype(BF16)
            nall[at, :] = normed
            cosine, sine = turn_tables(near_cos, near_sin, shift, s)
            q = mm(normed, w[:, : 4 * HEAD])
            q = q * cosine + swap_halves(q) * sine
            kv = mm(normed, w[:, 4 * HEAD :])
            lane = lax.broadcasted_iota(jnp.int32, kv.shape, 1)
            kv = jnp.where(lane < 2 * HEAD, kv * cosine + swap_halves(kv) * sine, kv)
            keep = lax.broadcasted_iota(jnp.int32, (rows, 128), 1) < HEAD

            def head(u, h):
                return jnp.where(keep, lane_roll(u, -HEAD * h)[:, :128], 0.0).astype(BF16)

            for h in range(4):
                qh[h, at, :] = head(q, h)
            for c in range(2):
                kh[c, at, :] = head(kv, c)
                vh[c, at, :] = head(kv, c + 2)
            return carry

        lax.fori_loop(0, 4, project, 0)

        def attend(h, carry):
            c = lax.div(h, 2)
            for b in range(4):
                far = (b + 1) * rows
                here = slice(b * rows, far)
                sc = mm(kh[c, :far, :], qh[h, here, :], NT) * scale
                sc = jnp.where(visible(sc.shape, b), sc, MASKED)
                peak = jnp.max(sc, axis=0, keepdims=True)
                e = jnp.exp(sc - peak)
                total = jnp.sum(e, axis=0, keepdims=True)
                p = (e * (1.0 / total)).astype(BF16)
                outh[h, here, :] = mm(p, vh[c, :far, :], TN)
                lse[h, :, here] = peak + jnp.log(total)
            return carry

        lax.fori_loop(0, 4, attend, 0)

        def pack(b, carry):
            acc = jnp.zeros((rows, 4 * HEAD), F32)
            for h in range(4):
                piece = jnp.concatenate(
                    [outh[h, ds_of(b), :], jnp.zeros((rows, 4 * HEAD - 128), F32)], axis=1
                )
                acc = acc + lane_roll(piece, HEAD * h)
            att[b] = acc.astype(BF16)
            return carry

        lax.fori_loop(0, 4, pack, 0)
        ln.gather_end(X, hid, x_of)
        for m in (3, 2, 1):
            ln.over_tensor(A, m, att.at[tensor_peer(t, m)], columns(t)).start()
        own = pltpu.make_async_copy(att.at[t], columns(t), local.at[0])
        own.start()

        @pl.when(ln.mid == 1)
        def _():
            for i in (1, 2, 3):
                ln.gather_take(C, i, c_of)

        for m in (2, 4, 6):
            dd = dp_peer(d, m)
            ln.landed_dp(DO, m, w_at(wof, dd))
            ln.over_dp(FO, m, w_at(wof, dd), w_at(wof, dd), to=1).start()
        ln.landed_dp(DO, 1, w_at(wof, dp_peer(d, 1)))
        for m in (2, 4, 6):
            ln.landed_dp(FO, m, w_at(wof, dp_peer(d, m ^ 1)))
        own.wait()
        for m in (1, 2, 3):
            ln.landed_tensor(A, m, columns(tensor_peer(t, m)))
        third = width // 3

        def project_out(n, carry):
            cols = pl.ds(pl.multiple_of(n * third, 128), third)
            resid[:, cols] = xall[at_own, cols].astype(F32) + mm(arow[...], wof[:, cols])
            return carry

        lax.fori_loop(0, 3, project_out, 0)
        r = resid[...]
        inv = lax.rsqrt(jnp.mean(r * r, axis=1, keepdims=True) + EPSILON)
        normed2[...] = (r * inv * gains[1:2, :]).astype(BF16)
        ln.gather_start(N, normed2, x_of)
        xall[at_own, :] = normed2[...]

    def feed(loads, gate_w, up_w, down_w, act, gg, gu, gsend, gown, part, gact):
        for c in loads:
            c.wait()

        def to_owner(shard, m):
            return pltpu.make_async_remote_copy(
                src_ref=gsend.at[shard],
                dst_ref=grecv.at[m - 1],
                send_sem=tsend.at[G, m],
                recv_sem=trecv.at[G, m],
                device_id={"dp": d, "tensor": shard},
                device_id_type=MESH,
            )

        @pl.when(ln.mid == 0)
        def _():
            for i in (1, 2, 3):
                ln.gather_take(C, i, c_of)

        piece = units // 4

        def act_grads(c, carry):
            cols = pl.ds(pl.multiple_of(c * piece, 128), piece)
            gact[:, cols] = mm(call[...], down_w[cols, :], NT)
            return carry

        lax.fori_loop(0, 4, act_grads, 0)

        def one_shard(i, carry):
            shard, m = ln.shard_at(i)

            @pl.when(i > 0)
            def _():
                ln.gather_take(N, i, x_of)

            at = ds_of(shard)
            r = xall[at, :]
            for c in range(4):
                cols = slice(c * piece, (c + 1) * piece)
                gate = mm(r, gate_w[:, cols])
                up = mm(r, up_w[:, cols])
                sig = 1.0 / (1.0 + jnp.exp(-gate))
                silu = gate * sig
                act[at, cols] = (silu * up).astype(BF16)
                g_act = gact[at, cols]
                gg[at, cols] = (g_act * up * sig * (1.0 + gate * (1.0 - sig))).astype(BF16)
                gu[at, cols] = (g_act * silu).astype(BF16)
            g = mm(gg[at, :], gate_w[...], NT) + mm(gu[at, :], up_w[...], NT)

            @pl.when(i == 0)
            def _():
                gown[...] = g

            @pl.when(i > 0)
            def _():
                gsend[shard] = g.astype(BF16)
                to_owner(shard, m).start()

            return carry

        lax.fori_loop(0, 4, one_shard, 0)

        def side(which):
            return pl.ds(pl.multiple_of(which * half, half), half)

        def to_core(k, j):
            return pltpu.make_async_remote_copy(
                src_ref=part.at[j, side(1 - core), :],
                dst_ref=ff.at[j, k],
                send_sem=dsend.at[CK + k, j],
                recv_sem=drecv.at[CK + k, j],
                device_id={"dp": dp_peer(d, 1), "tensor": t},
                device_id_type=MESH,
            )

        def chip_sum(k, j):
            to_core(k, j).wait_recv()
            ff[j, k] = (
                part[j, side(core), :].astype(F32) + ff[j, k].astype(F32)
            ).astype(BF16)
            to_core(k, j).wait_send()

        for k, (a, b) in enumerate(((xall, gg), (xall, gu), (call, act))):

            def weights(j, carry, k=k, a=a, b=b):
                cols = pl.ds(pl.multiple_of(j * span, 128), span)
                if k > 0:

                    @pl.when(j == 2)
                    def _():
                        chip_sum(k - 1, 3)
                        ff_sums[k - 1].start()

                part[j] = mm(a[:, cols], b[...], TN).astype(BF16)
                to_core(k, j).start()

                @pl.when(j > 0)
                def _():
                    chip_sum(k, j - 1)

                return carry

            lax.fori_loop(0, 4, weights, 0)
        chip_sum(2, 3)
        ff_sums[2].start()

        def feed_sums(n, carry):
            third = width // 3
            cols = pl.ds(pl.multiple_of(n * third, 128), third)
            msend[:, :, cols] = mm(act[...], down_w[:, cols]).astype(BF16).reshape(4, rows, third)
            return carry

        lax.fori_loop(0, 3, feed_sums, 0)
        for m in (1, 2, 3):
            ln.landed_tensor(G, m, grecv.at[m - 1])
        g = gown[...]
        for m in (1, 2, 3):
            g = g + grecv[m - 1].astype(F32)
        r = resid[...]
        inv = lax.rsqrt(jnp.mean(r * r, axis=1, keepdims=True) + EPSILON)
        gain[0] = jnp.sum(g * r * inv, axis=0, keepdims=True)
        scaled = g * gains[1:2, :]
        gr = (
            call[at_own, :].astype(F32)
            + inv * scaled
            - r * (inv * inv * inv) * jnp.mean(scaled * r, axis=1, keepdims=True)
        )
        gres[...] = gr
        low[...] = gr.astype(BF16)
        for s in range(4):
            gatt[s] = mm(low[...], wof[s * span : (s + 1) * span, :], NT).astype(BF16)
        for m in (1, 2, 3):
            to_owner(tensor_peer(t, m), m).wait_send()

    def forward(gate_w, up_w, down_w):
        loads = [
            pltpu.make_async_copy(a, b, local.at[5 + i])
            for i, (a, b) in enumerate(((wg, gate_w), (wu, up_w), (wd, down_w)))
        ]
        for c in loads:
            c.start()
        pl.run_scoped(front, V((4, seq, 128), F32))
        hidden = V((seq, units), BF16)
        pl.run_scoped(
            functools.partial(feed, loads, gate_w, up_w, down_w),
            hidden, hidden, hidden, V((4, rows, width), BF16), V((rows, width), F32),
            V((4, span, units), BF16), V((seq, units), F32),
        )

    pl.run_scoped(
        forward, V((width, units), BF16), V((width, units), BF16), V((units, width), BF16)
    )

    def backward(gh, gq, gk, gv, gqkv, gn_src, wo_part, wq_part, layer, gin, wqkv, wo_full, ffw):
        for m in (3, 2, 1):
            ln.over_tensor(GA, m, gatt.at[tensor_peer(t, m)], rows_at(gall, t)).start()
        own = [
            pltpu.make_async_copy(gatt.at[t], rows_at(gall, t), local.at[0]),
            pltpu.make_async_copy(gain, rows_in.at[pl.ds(d, 1)], local.at[1]),
        ]
        for c in own:
            c.start()
        for m in range(1, 8):
            ln.over_dp(DR, m, gain.at[0], rows_in.at[d]).start()
        layer_sum.start()
        wo_pair = CoreSum(ln, CO, wo_part, wo_core)

        def output_weights(j, carry):
            cols = pl.ds(pl.multiple_of(j * span, 128), span)
            wo_part[j] = mm(arow[:, cols], low[...], TN).astype(BF16)
            wo_pair.copy(j).start()
            return carry

        lax.fori_loop(0, 4, output_weights, 0)
        for k in range(2):
            ff_sums[k].hand_on()
        own[0].wait()
        for m in (1, 2, 3):
            ln.landed_tensor(GA, m, rows_at(gall, tensor_peer(t, m)))
        keep = lax.broadcasted_iota(jnp.int32, (rows, 128), 1) < HEAD

        def split(b, carry):
            u = gall[ds_of(b), :].astype(F32)
            for h in range(4):
                gh[h, ds_of(b), :] = jnp.where(
                    keep, lane_roll(u, -HEAD * h)[:, :128], 0.0
                ).astype(BF16)
            return carry

        lax.fori_loop(0, 4, split, 0)
        gk[...] = jnp.zeros_like(gk)
        gv[...] = jnp.zeros_like(gv)
        wo_pair.take()
        wo_sum = PlaneSum(ln, DOS, wo_core, wo_in)
        wo_sum.start()

        def attend_back(h, carry):
            c = lax.div(h, 2)
            for b in range(4):
                far = (b + 1) * rows
                here = slice(b * rows, far)
                k, v, q, g = kh[c, :far, :], vh[c, :far, :], qh[h, here, :], gh[h, here, :]
                sc = mm(k, q, NT) * scale
                sc = jnp.where(visible(sc.shape, b), sc, MASKED)
                p = jnp.exp(sc - lse[h, :, here])
                gp = mm(v, g, NT)
                gs = (p * (gp - jnp.sum(p * gp, axis=0, keepdims=True))).astype(BF16)
                gq[h, here, :] = mm(gs, k, TN) * scale
                gk[c, :far, :] += mm(gs, q) * scale
                gv[c, :far, :] += mm(p.astype(BF16), g)
            return carry

        lax.fori_loop(0, 4, attend_back, 0)

        def gather_heads(b, carry):
            at = ds_of(b)
            cosine, sine = turn_tables(near_cos, near_sin, shift, b)
            cosine, sine = cosine[:, :128], sine[:, :128]

            def placed(u, h):
                u = jnp.concatenate(
                    [jnp.where(keep, u, 0.0), jnp.zeros((rows, 4 * HEAD - 128), F32)], axis=1
                )
                return lane_roll(u, HEAD * h)

            def turned(u):
                return u * cosine - swap_halves(u) * sine

            left = sum(placed(turned(gq[h, at, :]), h) for h in range(4))
            right = sum(placed(turned(gk[c, at, :]), c) for c in range(2))
            right = right + sum(placed(gv[c, at, :], c + 2) for c in range(2))
            gqkv[at, : 4 * HEAD] = left.astype(BF16)
            gqkv[at, 4 * HEAD :] = right.astype(BF16)
            return carry

        lax.fori_loop(0, 4, gather_heads, 0)
        gn_sum = LineSum(ln, B, gn_src, grecv)

        def norm_grads(i, carry):
            shard, _ = ln.shard_at(3 - i)
            gn_src[shard] = mm(gqkv[ds_of(shard), :], w[...], NT).astype(BF16)
            gn_sum.first(i, shard)
            return carry

        lax.fori_loop(0, 4, norm_grads, 0)
        wq_pair = CoreSum(ln, CW, wq_part, wq_core)

        def head_weights(j, carry):
            cols = pl.ds(pl.multiple_of(j * span, 128), span)
            wq_part[j] = mm(nall[:, cols], gqkv[...], TN).astype(BF16)
            wq_pair.copy(j).start()
            return carry

        ff_sums[2].hand_on()
        wo_sum.hand_on()
        lax.fori_loop(0, 4, head_weights, 0)
        wq_pair.take()
        wq_sum = PlaneSum(ln, DWS, wq_core, wq_in)
        wq_sum.start()

        own[1].wait()
        for m in range(1, 8):
            ln.landed_dp(DR, m, rows_in.at[dp_peer(d, m)])
        gsum[0] = sum(rows_in[i] for i in range(8))
        for m in (1, 2, 3):
            ln.over_tensor(R, m, gsum.at[0], line_in.at[m]).start()
        layer_sum.hand_on()
        stores = []

        def out(a, b):
            c = pltpu.make_async_copy(a, b, store.at[len(stores)])
            c.start()
            stores.append(c)

        def to_rows(total, dst):
            lanes = total.lanes
            for h in range(2):
                u = total.take(h).astype(BF16)
                for s in range(4):
                    dst[s, :, h * lanes : (h + 1) * lanes] = u[s * wrows : (s + 1) * wrows, :]

        def feed_weights(k):
            lanes = units // 2
            for h in range(2):
                ffw[k, :, h * lanes : (h + 1) * lanes] = ff_sums[k].take(h)
            out(ffw.at[k], mlpw_out.at[k])

        to_rows(wo_sum, wo_src)
        wo_line_sum = LineSum(ln, OL, wo_src, wo_line)
        wo_line_sum.start()
        gn_sum.hand_on()
        wq_sum.hand_on()
        layer[...] = (resid[...] + msend[t].astype(F32) + layer_sum.take()).astype(BF16)
        out(layer, layer_out)
        for k in range(3):
            feed_weights(k)
        to_rows(wq_sum, wq_src)
        for m in (3, 2, 1):
            ln.over_tensor(WL, m, wq_src.at[tensor_peer(t, m)], wq_all.at[m]).start()
        wqkv[pl.ds(t, 1)] = wq_src[pl.ds(t, 1)].astype(F32)
        wo_line_sum.hand_on()
        total = gsum[0]
        for m in (1, 2, 3):
            ln.landed_tensor(R, m, line_in.at[m])
            total = total + line_in[m]
        mine = (d * 4 + t) * wrows
        turned = pltpu.roll(jnp.broadcast_to(total, (8, width)), lax.rem(width - mine, width), 1)
        gown_row[...] = turned[:, :128]
        out(gown_row, gain_out)
        x = hid[...].astype(F32)
        inv = lax.rsqrt(jnp.mean(x * x, axis=1, keepdims=True) + EPSILON)
        scaled = (gn_src[t].astype(F32) + gn_sum.take()) * gains[0:1, :]
        gin[...] = (
            gres[...]
            + inv * scaled
            - x * (inv * inv * inv) * jnp.mean(scaled * x, axis=1, keepdims=True)
        )
        out(gin, gin_out)
        wo_full[...] = wo_src[t].astype(F32) + wo_line_sum.take()
        out(wo_full, wo_out)
        for m in (1, 2, 3):
            ln.landed_tensor(WL, m, wq_all.at[m])
            wqkv[pl.ds(tensor_peer(t, m), 1)] = wq_all[pl.ds(m, 1)].astype(F32)
        out(wqkv, wqkv_out)

        for m in (1, 2, 3):
            ln.over_tensor(TILE, m, tile, tiles.at[d, t]).wait_send()
            ln.over_tensor(W, m, wpack.at[tensor_peer(t, m)], w_at(w, d, t)).wait_send()
            ln.over_tensor(A, m, att.at[tensor_peer(t, m)], columns(t)).wait_send()
            ln.over_tensor(GA, m, gatt.at[tensor_peer(t, m)], rows_at(gall, t)).wait_send()
            ln.over_tensor(R, m, gsum.at[0], line_in.at[m]).wait_send()
            ln.over_tensor(WL, m, wq_src.at[tensor_peer(t, m)], wq_all.at[m]).wait_send()
        ln.gather_end(O, wo, wo_of)
        ln.gather_end(C, cot, c_of)
        ln.gather_end(N, normed2, x_of)
        for m in range(1, 8):
            ln.over_dp(DT, m, tiles.at[d], tiles.at[d]).wait_send()
            ln.over_dp(DR, m, gain.at[0], rows_in.at[d]).wait_send()
        for m in (2, 4, 6, 1):
            ln.over_dp(DW, m, w_at(w, d), w_at(w, d)).wait_send()
            ln.over_dp(DO, m, w_at(wof, d), w_at(wof, d)).wait_send()
        for m in (2, 4, 6):
            dd = dp_peer(d, m)
            ln.over_dp(FW, m, w_at(w, dd), w_at(w, dd), to=1).wait_send()
            ln.over_dp(FO, m, w_at(wof, dd), w_at(wof, dd), to=1).wait_send()
        for s in (layer_sum, gn_sum, wo_line_sum, *ff_sums, wo_sum, wq_sum, wo_pair, wq_pair):
            s.end()
        for c in stores:
            c.wait()

    pl.run_scoped(
        backward,
        V((4, seq, 128), BF16), V((4, seq, 128), F32), V((2, seq, 128), F32),
        V((2, seq, 128), F32), V((seq, 8 * HEAD), BF16), V((4, rows, width), BF16),
        V((4, span, width), BF16), V((4, span, 8 * HEAD), BF16),
        V((rows, width), BF16), V((rows, width), F32), V((4, wrows, 8 * HEAD), F32),
        V((wrows, width), F32), V((3, half, units), F32),
    )


def layer(hid, cot, positions, gain_attn, gain_mlp, wq, wk, wv, wo, wg, wu, wd):
    rows, width = hid.shape
    wrows = wq.shape[0]
    units = wg.shape[1]
    seq = 4 * rows
    span = width // 4
    half = span // 2
    near_cos, near_sin, shift = rotary_tables(rows, 4)
    hbm = pl.BlockSpec(memory_space=pl.ANY)
    vmem = pl.BlockSpec(memory_space=pltpu.VMEM)
    V = pltpu.VMEM
    shapes = dict(
        layer=((rows, width), BF16), gin=((rows, width), F32), gain=((8, 128), F32),
        wqkv=((4, wrows, 8 * HEAD), F32), wo=((wrows, width), F32),
        mlp=((3, half, units), F32),
    )
    wide = V((seq, width), BF16)
    thin, thin_f = V((rows, width), BF16), V((rows, width), F32)
    four = V((4, rows, width), BF16)
    pair = V((2, seq, 128), BF16)
    outs = pl.pallas_call(
        layer_kernel,
        out_shape=[jax.ShapeDtypeStruct(*v) for v in shapes.values()],
        in_specs=[vmem, hbm] + [vmem] * 6 + [hbm] * 4 + [vmem] * 3,
        out_specs=[hbm] * len(shapes),
        scratch_shapes=[
            wide, wide, wide, V((width, 8 * HEAD), BF16), V((width, width), BF16),
            V((8, 4, 8, 128), F32), V((4, seq, 128), BF16), pair, pair,
            V((4, rows, span), BF16), thin, V((4, 1, seq), F32), V((1, seq), F32),
            V((8, width), F32), thin_f, thin,
            four, V((4, 3, half, units), BF16), four, V((4, rows, span), BF16), thin_f, thin,
            V((1, 1, width), F32),
            V((seq, span), BF16), four, V((6, 3, half, units // 2), BF16),
            V((4, half, width), BF16), V((6, half, width // 2), BF16),
            V((4, wrows, width), BF16), V((4, wrows, width), BF16),
            V((4, half, 8 * HEAD), BF16), V((6, half, 4 * HEAD), BF16),
            V((4, wrows, 8 * HEAD), BF16), V((4, wrows, 8 * HEAD), BF16),
            V((8, 1, width), F32), V((4, 1, width), F32), V((1, 1, width), F32),
            V((8, 128), F32), V((4, wrows, 8 * HEAD), BF16), V((8, 128), F32),
            pltpu.SemaphoreType.DMA((14, 6)), pltpu.SemaphoreType.DMA((14, 4)),
            pltpu.SemaphoreType.DMA((16, 8)), pltpu.SemaphoreType.DMA((16, 8)),
            pltpu.SemaphoreType.DMA((8,)), pltpu.SemaphoreType.DMA((8,)),
        ],
        name="layer",
        compiler_params=pltpu.CompilerParams(
            collective_id=0, has_side_effects=True, vmem_limit_bytes=VMEM_LIMIT
        ),
    )(
        hid, cot, positions.reshape(1, rows), gain_attn.reshape(1, wrows),
        gain_mlp.reshape(1, wrows), wq, wk, wv, wo, wg, wu, wd, near_cos, near_sin, shift,
    )
    return dict(zip(shapes, outs))


def finish_kernel(
    layer, gin, gain, wqkv, wo, mlp, wq, wk, wv, gain_one,
    layer_out, gin_out, gain_one_out, query_out, key_out, value_out, wo_out, gain_two_out,
    gate_out, up_out, down_out,
    lay, gi, ga, w4, wof, ff, one, query, key, value, two, load, store,
):
    moves = [
        (layer, lay, layer_out), (gin, gi, gin_out), (wo, wof, wo_out),
        (mlp.at[0], ff.at[0], gate_out), (mlp.at[1], ff.at[1], up_out),
        (mlp.at[2], ff.at[2], down_out), (wqkv, w4, None), (gain, ga, None),
    ]
    loads = [pltpu.make_async_copy(a, b, load.at[i]) for i, (a, b, _) in enumerate(moves)]
    for i in (6, 7, 0, 1, 2, 3, 4, 5):
        loads[i].start()
    stores = []

    def out(a, b):
        c = pltpu.make_async_copy(a, b, store.at[len(stores)])
        c.start()
        stores.append(c)

    wrows, span = query.shape[0], query.shape[1] // 4
    pair = 2 * HEAD
    loads[6].wait()
    lane = lax.broadcasted_iota(jnp.int32, (wrows, 8 * HEAD), 1)
    keys = jnp.zeros((wrows, 8 * HEAD), F32)
    values = jnp.zeros((wrows, 8 * HEAD), F32)
    for s in range(4):
        query[:, s * span : (s + 1) * span] = w4[s, :, :span]
        u = jnp.concatenate([w4[s, :, span:], jnp.zeros((wrows, span), F32)], axis=1)
        here = (lane >= pair * s) & (lane < pair * (s + 1))
        keys = jnp.where(here, lane_roll(u, pair * s), keys)
        values = jnp.where(here, lane_roll(u, pair * s - pair), values)
    key[...] = keys
    value[...] = values
    out(query, query_out)
    out(key, key_out)
    out(value, value_out)
    total = (
        jnp.sum(wq[...].astype(F32) * query[...], axis=1, keepdims=True)
        + jnp.sum(wk[...].astype(F32) * keys, axis=1, keepdims=True)
        + jnp.sum(wv[...].astype(F32) * values, axis=1, keepdims=True)
    )
    tall = jnp.concatenate(
        [jnp.broadcast_to(total, (wrows, 128)), jnp.zeros((128 - wrows, 128), F32)], axis=0
    )
    one[...] = tall.T[0:1, :wrows] / gain_one[...].astype(F32)
    out(one, gain_one_out)
    loads[7].wait()
    two[...] = ga[0:1, :wrows]
    out(two, gain_two_out)
    for i in range(6):
        loads[i].wait()
        out(moves[i][1], moves[i][2])
    for c in stores:
        c.wait()


def finish(b, wq, wk, wv, gain_attn):
    rows, width = b["layer"].shape
    wrows, kv = wk.shape
    half, units = b["mlp"].shape[1:]
    hbm = pl.BlockSpec(memory_space=pl.ANY)
    vmem = pl.BlockSpec(memory_space=pltpu.VMEM)
    V = pltpu.VMEM
    thin = ((rows, width), F32)
    row = ((1, wrows), F32)
    weight, narrow = ((wrows, width), F32), ((wrows, kv), F32)
    shapes = [
        ((rows, width), BF16), thin, row, weight, narrow, narrow, weight, row,
        ((half, units), F32), ((half, units), F32), ((half, units), F32),
    ]
    return pl.pallas_call(
        finish_kernel,
        out_shape=[jax.ShapeDtypeStruct(*v) for v in shapes],
        in_specs=[hbm] * 6 + [vmem] * 4,
        out_specs=[hbm] * len(shapes),
        scratch_shapes=[
            V((rows, width), BF16), V(*thin), V((8, 128), F32), V((4, wrows, 8 * HEAD), F32),
            V(*weight), V((3, half, units), F32), V(*row), V(*weight), V(*narrow), V(*narrow),
            V(*row),
            pltpu.SemaphoreType.DMA((8,)), pltpu.SemaphoreType.DMA((11,)),
        ],
        name="finish",
        compiler_params=pltpu.CompilerParams(vmem_limit_bytes=VMEM_LIMIT),
    )(
        b["layer"], b["gin"], b["gain"], b["wqkv"], b["wo"], b["mlp"], wq, wk, wv,
        gain_attn.reshape(1, wrows),
    )


QUERY_HEADS = 16
KEY_VALUE_HEADS = 8
HEAD_DIMENSION = 96


def angle_tables(pos_rows, head_size):
    half_size = head_size // 2
    freq_rates = ROPE_BASE ** (-(jnp.arange(half_size, dtype=jnp.float32) * 2.0) / head_size)
    turned = pos_rows.astype(jnp.float32)[:, None] * freq_rates[None, :]
    return (jnp.cos(turned)[:, None, :], jnp.sin(turned)[:, None, :])


def apply_rotary(tensor_in, cosine_table, sine_table):
    half_size = tensor_in.shape[-1] // 2
    lo_half = tensor_in[..., :half_size]
    hi_half = tensor_in[..., half_size:]
    return jnp.concatenate(
        [
            lo_half * cosine_table - hi_half * sine_table,
            hi_half * cosine_table + lo_half * sine_table,
        ],
        axis=-1,
    )


def shards(
    hidden_in,
    positions,
    gain_attn,
    w_query,
    key_matrix,
    value_matrix,
    w_output,
    gain_mlp,
    w_gate,
    w_up,
    w_down,
    cotangent,
):
    tok_rows = hidden_in.shape[0]
    model_width = hidden_in.shape[1]
    num_heads = QUERY_HEADS
    key_value_count = KEY_VALUE_HEADS
    head_size = HEAD_DIMENSION
    kv_width = key_value_count * head_size
    queries_per_group = num_heads // key_value_count
    seq_len = tok_rows * lax.axis_size("tensor")
    score_scale = 1.0 / math.sqrt(head_size)
    gathered = (
        lax.all_gather(gain_attn, ("dp", "tensor"), axis=0, tiled=True),
        lax.all_gather(w_query, ("dp", "tensor"), axis=0, tiled=True),
        lax.all_gather(key_matrix, ("dp", "tensor"), axis=0, tiled=True),
        lax.all_gather(value_matrix, ("dp", "tensor"), axis=0, tiled=True),
        lax.all_gather(w_output, ("dp", "tensor"), axis=0, tiled=True),
        lax.all_gather(gain_mlp, ("dp", "tensor"), axis=0, tiled=True),
    )
    gain_one, query_full, key_full, value_full, output_full, gain_two = gathered
    gain_one_f = gain_one.astype(jnp.float32)
    gain_two_f = gain_two.astype(jnp.float32)
    x_float = hidden_in.astype(jnp.float32)
    inv_one = lax.rsqrt(jnp.mean(x_float * x_float, axis=-1, keepdims=True) + EPSILON)
    normed_one = (x_float * inv_one * gain_one_f).astype(jnp.bfloat16)
    queries = jnp.dot(normed_one, query_full, preferred_element_type=jnp.float32)
    key_projected = jnp.dot(normed_one, key_full, preferred_element_type=jnp.float32)
    value_proj = jnp.dot(normed_one, value_full, preferred_element_type=jnp.float32)
    cosine_table, sine_table = angle_tables(positions, head_size)
    rotated_query_rows = apply_rotary(
        queries.reshape(tok_rows, num_heads, head_size), cosine_table, sine_table
    ).astype(jnp.bfloat16)
    rotated_key_rows = (
        apply_rotary(
            key_projected.reshape(tok_rows, key_value_count, head_size), cosine_table, sine_table
        )
        .astype(jnp.bfloat16)
        .reshape(tok_rows, kv_width)
    )
    value_rows_lowered = value_proj.astype(jnp.bfloat16)
    keys_all, values_all = (
        lax.all_gather(rotated_key_rows, "tensor", axis=0, tiled=True),
        lax.all_gather(value_rows_lowered, "tensor", axis=0, tiled=True),
    )
    offset = lax.axis_index("tensor") * tok_rows
    query_index = offset + jnp.arange(tok_rows, dtype=jnp.int32)
    key_index = jnp.arange(seq_len, dtype=jnp.int32)
    visible = (key_index[None, :] <= query_index[:, None]) & (
        key_index[None, :] >= (query_index - positions)[:, None]
    )
    visible = jnp.tile(visible, (queries_per_group, 1))

    def split_queries(tensor_in):
        return (
            tensor_in.reshape(tok_rows, key_value_count, queries_per_group, head_size)
            .transpose(1, 2, 0, 3)
            .reshape(key_value_count, queries_per_group * tok_rows, head_size)
        )

    def split_keys(tensor_in):
        return tensor_in.reshape(seq_len, key_value_count, head_size).transpose(1, 0, 2)

    def merge_heads(tensor_in):
        return (
            tensor_in.reshape(key_value_count, queries_per_group, tok_rows, head_size)
            .transpose(2, 0, 1, 3)
            .reshape(tok_rows, model_width)
        )

    query_heads = split_queries(rotated_query_rows)
    k_heads = split_keys(keys_all)
    value_heads = split_keys(values_all)

    def attend(head_items):
        q_block, k_block, v_block = head_items
        scores = (
            jnp.einsum("qd,kd->qk", q_block, k_block, preferred_element_type=jnp.float32)
            * score_scale
        )
        scores = jnp.where(visible, scores, MASKED)
        peak = jnp.max(scores, axis=-1, keepdims=True)
        exp_vals = jnp.exp(scores - peak)
        total = jnp.sum(exp_vals, axis=-1, keepdims=True)
        probs = exp_vals / total
        out_block = jnp.einsum(
            "qk,kd->qd", probs.astype(jnp.bfloat16), v_block, preferred_element_type=jnp.float32
        )
        return (out_block, peak[:, 0] + jnp.log(total[:, 0]))

    attended_rows, log_total = lax.map(attend, (query_heads, k_heads, value_heads))
    attended_low = merge_heads(attended_rows).astype(jnp.bfloat16)
    resid_sum = x_float + jnp.dot(attended_low, output_full, preferred_element_type=jnp.float32)
    inv_two = lax.rsqrt(jnp.mean(resid_sum * resid_sum, axis=-1, keepdims=True) + EPSILON)
    normed_two = (resid_sum * inv_two * gain_two_f).astype(jnp.bfloat16)
    rows_all = lax.all_gather(normed_two, "tensor", axis=0, tiled=True)
    gate_val = jnp.dot(rows_all, w_gate, preferred_element_type=jnp.float32)
    up_val = jnp.dot(rows_all, w_up, preferred_element_type=jnp.float32)
    sig_gate = jax.nn.sigmoid(gate_val)
    silu_gate = gate_val * sig_gate
    act_low = (silu_gate * up_val).astype(jnp.bfloat16)
    mlp_sum = lax.psum_scatter(
        jnp.dot(act_low, w_down, preferred_element_type=jnp.float32).astype(jnp.bfloat16),
        "tensor",
        scatter_dimension=0,
        tiled=True,
    ).astype(jnp.float32)
    layer_out = (resid_sum + mlp_sum).astype(jnp.bfloat16)
    grad_float = cotangent.astype(jnp.float32)
    grad_all = lax.all_gather(cotangent, "tensor", axis=0, tiled=True)
    grad_down = jnp.einsum("sf,sd->fd", act_low, grad_all, preferred_element_type=jnp.float32)
    g_act = jnp.einsum("sd,fd->sf", grad_all, w_down, preferred_element_type=jnp.float32)
    g_gate = (g_act * up_val * sig_gate * (1.0 + gate_val * (1.0 - sig_gate))).astype(jnp.bfloat16)
    g_up = (g_act * silu_gate).astype(jnp.bfloat16)
    grad_gate = jnp.einsum("sd,sf->df", rows_all, g_gate, preferred_element_type=jnp.float32)
    grad_up = jnp.einsum("sd,sf->df", rows_all, g_up, preferred_element_type=jnp.float32)
    g_norm_two = lax.psum_scatter(
        (
            jnp.einsum("sf,df->sd", g_gate, w_gate, preferred_element_type=jnp.float32)
            + jnp.einsum("sf,df->sd", g_up, w_up, preferred_element_type=jnp.float32)
        ).astype(jnp.bfloat16),
        "tensor",
        scatter_dimension=0,
        tiled=True,
    ).astype(jnp.float32)
    scaled_two = gain_two_f * g_norm_two
    grad_gain_two = jnp.sum(g_norm_two * resid_sum * inv_two, axis=0)
    g_resid = (
        grad_float
        + inv_two * scaled_two
        - resid_sum * inv_two**3 * jnp.mean(scaled_two * resid_sum, axis=-1, keepdims=True)
    )
    g_resid_low = g_resid.astype(jnp.bfloat16)
    grad_output = jnp.einsum(
        "tc,td->cd", attended_low, g_resid_low, preferred_element_type=jnp.float32
    )
    g_att = jnp.einsum(
        "td,cd->tc", g_resid_low, output_full, preferred_element_type=jnp.float32
    ).astype(jnp.bfloat16)
    g_heads = split_queries(g_att)

    def attend_back(head_items):
        q_block, k_block, v_block, log_block, g_block = head_items
        scores = (
            jnp.einsum("qd,kd->qk", q_block, k_block, preferred_element_type=jnp.float32)
            * score_scale
        )
        scores = jnp.where(visible, scores, MASKED)
        probs = jnp.exp(scores - log_block[:, None])
        g_probs = jnp.einsum("qd,kd->qk", g_block, v_block, preferred_element_type=jnp.float32)
        g_scores = (probs * (g_probs - jnp.sum(probs * g_probs, axis=-1, keepdims=True))).astype(
            jnp.bfloat16
        )
        g_rq = (
            jnp.einsum("qk,kd->qd", g_scores, k_block, preferred_element_type=jnp.float32)
            * score_scale
        )
        g_rk = (
            jnp.einsum("qk,qd->kd", g_scores, q_block, preferred_element_type=jnp.float32)
            * score_scale
        )
        g_val = jnp.einsum(
            "qk,qd->kd", probs.astype(jnp.bfloat16), g_block, preferred_element_type=jnp.float32
        )
        return (g_rq, g_rk, g_val)

    g_rq, g_rk, g_val = lax.map(
        attend_back, (query_heads, k_heads, value_heads, log_total, g_heads)
    )
    g_rk_flat = g_rk.transpose(1, 0, 2).reshape(seq_len, kv_width)
    g_val_flat = g_val.transpose(1, 0, 2).reshape(seq_len, kv_width)
    key_part, value_part = (
        lax.psum_scatter(
            g_rk_flat.astype(jnp.bfloat16), "tensor", scatter_dimension=0, tiled=True
        ).astype(jnp.float32),
        lax.psum_scatter(
            g_val_flat.astype(jnp.bfloat16), "tensor", scatter_dimension=0, tiled=True
        ).astype(jnp.float32),
    )
    g_queries = (
        apply_rotary(
            merge_heads(g_rq).reshape(tok_rows, num_heads, head_size), cosine_table, -sine_table
        )
        .reshape(tok_rows, model_width)
        .astype(jnp.bfloat16)
    )
    g_keys = (
        apply_rotary(
            key_part.reshape(tok_rows, key_value_count, head_size), cosine_table, -sine_table
        )
        .reshape(tok_rows, kv_width)
        .astype(jnp.bfloat16)
    )
    g_values = value_part.astype(jnp.bfloat16)
    grad_query = jnp.einsum("tc,td->cd", normed_one, g_queries, preferred_element_type=jnp.float32)
    grad_key = jnp.einsum("tc,td->cd", normed_one, g_keys, preferred_element_type=jnp.float32)
    grad_value = jnp.einsum("tc,td->cd", normed_one, g_values, preferred_element_type=jnp.float32)
    g_norm_one = (
        jnp.einsum("td,cd->tc", g_queries, query_full, preferred_element_type=jnp.float32)
        + jnp.einsum("td,cd->tc", g_keys, key_full, preferred_element_type=jnp.float32)
        + jnp.einsum("td,cd->tc", g_values, value_full, preferred_element_type=jnp.float32)
    )
    scaled_one = gain_one_f * g_norm_one
    grad_gain_one = jnp.sum(g_norm_one * x_float * inv_one, axis=0)
    grad_input = (
        g_resid
        + inv_one * scaled_one
        - x_float * inv_one**3 * jnp.mean(scaled_one * x_float, axis=-1, keepdims=True)
    )
    packed = jnp.concatenate([grad_query, grad_key, grad_value, grad_output], axis=1)
    packed_part = lax.psum_scatter(
        packed.astype(jnp.bfloat16), ("dp", "tensor"), scatter_dimension=0, tiled=True
    ).astype(jnp.float32)
    query_part = packed_part[:, :model_width]
    keyw_part = packed_part[:, model_width : model_width + kv_width]
    valuew_part = packed_part[:, model_width + kv_width : model_width + 2 * kv_width]
    out_part = packed_part[:, model_width + 2 * kv_width :]
    gain_one_part, gain_two_part = (
        lax.psum_scatter(grad_gain_one, ("dp", "tensor"), scatter_dimension=0, tiled=True),
        lax.psum_scatter(grad_gain_two, ("dp", "tensor"), scatter_dimension=0, tiled=True),
    )
    gate_sum, up_sum, down_sum = (
        lax.psum_scatter(
            grad_gate.astype(jnp.bfloat16), "dp", scatter_dimension=0, tiled=True
        ).astype(jnp.float32),
        lax.psum_scatter(
            grad_up.astype(jnp.bfloat16), "dp", scatter_dimension=0, tiled=True
        ).astype(jnp.float32),
        lax.psum_scatter(
            grad_down.astype(jnp.bfloat16), "dp", scatter_dimension=1, tiled=True
        ).astype(jnp.float32),
    )
    return (
        layer_out,
        grad_input,
        gain_one_part,
        query_part,
        keyw_part,
        valuew_part,
        out_part,
        gain_two_part,
        gate_sum,
        up_sum,
        down_sum,
    )


def fast_shards(
    hidden_in, positions, gain_attn, w_query, key_matrix, value_matrix, w_output, gain_mlp,
    w_gate, w_up, w_down, cotangent,
):
    b = layer(
        hidden_in, cotangent, positions, gain_attn, gain_mlp, w_query, key_matrix, value_matrix,
        w_output, w_gate, w_up, w_down,
    )
    o = finish(b, w_query, key_matrix, value_matrix, gain_attn)
    wrows = w_query.shape[0]
    return (
        o[0], o[1], o[2].reshape(wrows), o[3], o[4], o[5], o[6], o[7].reshape(wrows), o[8], o[9], o[10].T,
    )


def solution(mesh):
    placed = (
        P(("dp", "tensor"), None),
        P(("dp", "tensor")),
        P(("dp", "tensor")),
        P(("dp", "tensor"), None),
        P(("dp", "tensor"), None),
        P(("dp", "tensor"), None),
        P(("dp", "tensor"), None),
        P(("dp", "tensor")),
        P(None, "tensor"),
        P(None, "tensor"),
        P("tensor", None),
        P(("dp", "tensor"), None),
    )
    fits = mesh.shape["dp"] == 8 and mesh.shape["tensor"] == 4
    return jax.shard_map(
        fast_shards if fits else shards,
        mesh=mesh,
        in_specs=placed,
        out_specs=(
            P(("dp", "tensor"), None),
            P(("dp", "tensor"), None),
            P(("dp", "tensor")),
            P(("dp", "tensor"), None),
            P(("dp", "tensor"), None),
            P(("dp", "tensor"), None),
            P(("dp", "tensor"), None),
            P(("dp", "tensor")),
            P("dp", "tensor"),
            P("dp", "tensor"),
            P("tensor", "dp"),
        ),
        check_vma=False,
    )
```

```python
import functools
import math

import jax
import jax.numpy as jnp
import numpy as np
from jax import lax
from jax.experimental import pallas as pl
from jax.experimental.pallas import tpu as pltpu
from jax.sharding import PartitionSpec as P

F32 = jnp.float32
BF16 = jnp.bfloat16
MESH = pl.DeviceIdType.MESH
EPSILON = 1e-05
ROPE_BASE = 100000.0
MASKED = -1e30
HEAD = 96
VMEM_LIMIT = 64 * 2**20 - 65536


def rotary_tables(rows, shards_in_sequence):
    half = HEAD // 2
    lanes = np.arange(4 * HEAD) % half
    rates = ROPE_BASE ** (-(lanes * 2.0) / HEAD)
    near = np.arange(rows)[:, None] * rates[None, :]
    far = (np.arange(shards_in_sequence) * rows)[:, None] * rates[None, :]
    shift = np.concatenate([np.cos(far), np.sin(far)], axis=0)
    return (
        np.cos(near).astype(np.float32),
        np.sin(near).astype(np.float32),
        shift.astype(np.float32),
    )


def tensor_peer(t, m):
    if m == 1:
        return t + 1 - 2 * lax.rem(t, 2)
    if m == 2:
        return lax.rem(t + 2, 4)
    return 3 - t


def dp_peer(d, m):
    if m & 1:
        d = d + 1 - 2 * lax.rem(d, 2)
    if m & 2:
        d = d + 2 - 4 * lax.rem(lax.div(d, 2), 2)
    if m & 4:
        d = lax.rem(d + 4, 8)
    return d


class Links:
    def __init__(self, tsend, trecv, dsend, drecv):
        self.t = lax.axis_index("tensor")
        self.d = lax.axis_index("dp")
        self.mid = lax.rem(lax.div(self.t + 1, 2), 2)
        self.tsend, self.trecv, self.dsend, self.drecv = tsend, trecv, dsend, drecv

    def shard_at(self, i):
        t, mid = self.t, self.mid
        near, two, three = (tensor_peer(t, m) for m in (1, 2, 3))
        if isinstance(i, int):
            if i == 0:
                return t, 0
            if i == 1:
                return near, 1
            if i == 2:
                return two + mid * (three - two), 2 + mid
            return three + mid * (two - three), 3 - mid
        one_if = [1 - jnp.minimum(jnp.abs(i - k), 1) for k in range(4)]
        pairs = [self.shard_at(k) for k in range(4)]
        return (
            sum(f * p[0] for f, p in zip(one_if, pairs)),
            sum(f * p[1] for f, p in zip(one_if, pairs)),
        )

    def over_tensor(self, kind, m, src, dst, recv=None):
        peer = tensor_peer(self.t, m)
        return pltpu.make_async_remote_copy(
            src_ref=src,
            dst_ref=dst,
            send_sem=self.tsend.at[kind, m],
            recv_sem=self.trecv.at[kind, m if recv is None else recv],
            device_id={"dp": self.d, "tensor": peer},
            device_id_type=MESH,
        )

    def over_dp(self, kind, m, src, dst, to=None):
        peer = dp_peer(self.d, m if to is None else to)
        return pltpu.make_async_remote_copy(
            src_ref=src,
            dst_ref=dst,
            send_sem=self.dsend.at[kind, m],
            recv_sem=self.drecv.at[kind, m],
            device_id={"dp": peer, "tensor": self.t},
            device_id_type=MESH,
        )

    def landed_tensor(self, kind, m, ref):
        pltpu.make_async_copy(ref, ref, self.trecv.at[kind, m]).wait()

    def landed_dp(self, kind, m, ref):
        pltpu.make_async_copy(ref, ref, self.drecv.at[kind, m]).wait()

    def gather_start(self, kind, src, at):
        own = at(self.t)
        self.over_tensor(kind, 1, src, own).start()

        @pl.when(self.mid == 0)
        def _():
            self.over_tensor(kind, 2, src, own).start()

        @pl.when(self.mid == 1)
        def _():
            self.over_tensor(kind, 3, src, own).start()

    def gather_take(self, kind, i, at):
        shard, m = self.shard_at(i)
        block = at(shard)
        self.landed_tensor(kind, m, block)

        def hand_on():
            pltpu.make_async_remote_copy(
                src_ref=block,
                dst_ref=block,
                send_sem=self.tsend.at[kind, 2 + i],
                recv_sem=self.trecv.at[kind, 5 - m],
                device_id={"dp": self.d, "tensor": tensor_peer(self.t, 1)},
                device_id_type=MESH,
            ).start()

        if isinstance(i, int):
            if i >= 2:
                pl.when(self.mid == 1)(hand_on)
        else:
            pl.when((self.mid == 1) & (i >= 2))(hand_on)

    def gather_end(self, kind, src, at):
        own = at(self.t)
        self.over_tensor(kind, 1, src, own).wait_send()

        @pl.when(self.mid == 0)
        def _():
            self.over_tensor(kind, 2, src, own).wait_send()

        @pl.when(self.mid == 1)
        def _():
            self.over_tensor(kind, 3, src, own).wait_send()
            for i in (2, 3):
                shard, m = self.shard_at(i)
                pltpu.make_async_copy(at(shard), at(shard), self.tsend.at[kind, 2 + i]).wait()

    def greet(self, tensor_peers, dp_peers):
        sem = pltpu.get_barrier_semaphore()
        for m in tensor_peers:
            pl.semaphore_signal(
                sem,
                inc=1,
                device_id={"dp": self.d, "tensor": tensor_peer(self.t, m)},
                device_id_type=MESH,
            )
        for m in dp_peers:
            pl.semaphore_signal(
                sem,
                inc=1,
                device_id={"dp": dp_peer(self.d, m), "tensor": self.t},
                device_id_type=MESH,
            )
        return len(tensor_peers) + len(dp_peers)


def mm(a, b, dims=((1,), (0,))):
    return lax.dot_general(a, b, (dims, ((), ())), preferred_element_type=F32)


NN = ((1,), (0,))
NT = ((1,), (1,))
TN = ((0,), (0,))


def lane_roll(u, by):
    return pltpu.roll(u, by % u.shape[-1], u.ndim - 1)


def swap_halves(u):
    lane = lax.broadcasted_iota(jnp.int32, u.shape, 1)
    low = lax.rem(lane, HEAD) < HEAD // 2
    return jnp.where(low, -lane_roll(u, -(HEAD // 2)), lane_roll(u, HEAD // 2))


def turn_tables(near_cos, near_sin, shift, shard):
    c = shift[pl.ds(shard, 1), :]
    s = shift[pl.ds(shard + 4, 1), :]
    a, b = near_cos[...], near_sin[...]
    return a * c - b * s, b * c + a * s


class LineSum:
    def __init__(self, ln, kind, src, recv):
        self.ln, self.kind, self.src, self.recv = ln, kind, src, recv
        t = ln.t
        self.near, self.two, self.three = (tensor_peer(t, m) for m in (1, 2, 3))

    def copy(self, src, to, slot, sem):
        ln, kind = self.ln, self.kind
        return pltpu.make_async_remote_copy(
            src_ref=src,
            dst_ref=self.recv.at[slot],
            send_sem=ln.tsend.at[kind, sem],
            recv_sem=ln.trecv.at[kind, slot],
            device_id={"dp": ln.d, "tensor": to},
            device_id_type=MESH,
        )

    def first(self, i, shard):
        c = self.copy(self.src.at[shard], self.near, i, i)
        if isinstance(i, int):
            if i == 2:
                c.start()
            else:
                pl.when(self.ln.mid == 0)(c.start)
        else:
            pl.when((i == 2) | ((self.ln.mid == 0) & (i < 2)))(c.start)

    def start(self):
        for i, shard in enumerate((self.three, self.two, self.near)):
            self.first(i, shard)

    def hand_on(self):
        @pl.when(self.ln.mid == 1)
        def _():
            for i, shard in enumerate((self.two, self.three)):
                self.ln.landed_tensor(self.kind, i, self.recv.at[i])
                self.recv[i] = (
                    self.recv[i].astype(F32) + self.src[shard].astype(F32)
                ).astype(BF16)
                self.copy(self.recv.at[i], shard, 3, i).start()

    def take(self):
        for i in (2, 3):
            self.ln.landed_tensor(self.kind, i, self.recv.at[i])
        return self.recv[2].astype(F32) + self.recv[3].astype(F32)

    def end(self):
        for i in range(3):
            pltpu.make_async_copy(
                self.src.at[0], self.src.at[0], self.ln.tsend.at[self.kind, i]
            ).wait()


class PlaneSum:
    def __init__(self, ln, kind, src, slot, width):
        self.ln, self.kind, self.src, self.slot = ln, kind, src, slot
        j = lax.div(ln.d, 2)
        self.j = j
        self.x = j + 1 - 2 * lax.rem(j, 2)
        self.y = lax.rem(j + 2, 4)
        self.diag = lax.rem(self.x + 2, 4)
        self.lanes = width // 2

    def half(self, ref, h):
        spot = [slice(None)] * (len(ref.shape) - 1) + [pl.ds(h * self.lanes, self.lanes)]
        return ref.at[tuple(spot)]

    def copy(self, src, m, i):
        return self.ln.over_dp(self.kind, i, src, self.slot(i), to=m)

    def plan(self):
        return (
            (self.half(self.src(self.diag), 0), 2, 0),
            (self.half(self.src(self.diag), 1), 4, 2),
            (self.half(self.src(self.x), 0), 2, 1),
            (self.half(self.src(self.y), 1), 4, 3),
        )

    def start(self):
        for src, m, i in self.plan():
            self.copy(src, m, i).start()

    def hand_on(self):
        for i, h, block, m in ((0, 0, self.y, 4), (2, 1, self.x, 2)):
            self.ln.landed_dp(self.kind, i, self.slot(i))
            self.slot(i)[...] = (
                self.slot(i)[...].astype(F32) + self.half(self.src(block), h)[...].astype(F32)
            ).astype(BF16)
            self.copy_on(i, h, m).start()

    def copy_on(self, i, h, m):
        return self.ln.over_dp(self.kind, 4 + h, self.slot(i), self.slot(4 + h), to=m)

    def take(self, h):
        for i in (1 + 2 * h, 4 + h):
            self.ln.landed_dp(self.kind, i, self.slot(i))
        own = self.half(self.src(self.j), h)[...].astype(F32)
        return own + self.slot(1 + 2 * h)[...].astype(F32) + self.slot(4 + h)[...].astype(F32)

    def end(self):
        for src, m, i in self.plan():
            self.copy(src, m, i).wait_send()
        for i, h, m in ((0, 0, 4), (2, 1, 2)):
            self.copy_on(i, h, m).wait_send()


class PlaneGather:
    def __init__(self, ln, kind, hand, block, part):
        self.ln, self.kind, self.hand, self.block, self.part = ln, kind, hand, block, part

    def own(self, m):
        here = self.block(self.ln.d)
        return self.ln.over_dp(self.kind, m, here, here)

    def on(self, m):
        h, to, i = (0, 4, 3) if m == 2 else (1, 2, 5)
        piece = self.part(dp_peer(self.ln.d, m), h)
        return self.ln.over_dp(self.kind, i, piece, piece, to=to)

    def core(self, m):
        block = self.block(dp_peer(self.ln.d, m))
        return self.ln.over_dp(self.hand, m, block, block, to=1)

    def start(self):
        for m in (2, 4, 1):
            self.own(m).start()

    def hand_on(self):
        for m in (2, 4):
            self.ln.landed_dp(self.kind, m, self.block(dp_peer(self.ln.d, m)))
            self.on(m).start()
            self.core(m).start()

    def take(self):
        far = dp_peer(self.ln.d, 6)
        for h, i in ((0, 3), (1, 5)):
            self.ln.landed_dp(self.kind, i, self.part(far, h))
        self.core(6).start()
        self.ln.landed_dp(self.kind, 1, self.block(dp_peer(self.ln.d, 1)))
        for m in (2, 4, 6):
            self.ln.landed_dp(self.hand, m, self.block(dp_peer(self.ln.d, m ^ 1)))

    def end(self):
        for m in (2, 4, 1):
            self.own(m).wait_send()
        for m in (2, 4):
            self.on(m).wait_send()
        for m in (2, 4, 6):
            self.core(m).wait_send()


class CoreSum:
    def __init__(self, ln, kind, src, slot):
        self.ln, self.kind, self.src, self.slot = ln, kind, src, slot
        self.half = src.shape[1] // 2
        self.core = lax.rem(ln.d, 2)

    def side(self, which):
        return pl.ds(pl.multiple_of(which * self.half, self.half), self.half)

    def copy(self, j):
        ln = self.ln
        return pltpu.make_async_remote_copy(
            src_ref=self.src.at[j, self.side(1 - self.core), :],
            dst_ref=self.slot(j),
            send_sem=ln.dsend.at[self.kind, j],
            recv_sem=ln.drecv.at[self.kind, j],
            device_id={"dp": dp_peer(ln.d, 1), "tensor": ln.t},
            device_id_type=MESH,
        )

    def take(self):
        def one(j, carry):
            self.copy(j).wait_recv()
            self.slot(j)[...] = (
                self.slot(j)[...].astype(F32) + self.src[j, self.side(self.core), :].astype(F32)
            ).astype(BF16)
            return carry

        lax.fori_loop(0, 4, one, 0)

    def end(self):
        def one(j, carry):
            self.copy(j).wait_send()
            return carry

        lax.fori_loop(0, 4, one, 0)


def layer_kernel(
    hid, cot, pos, gain_one, gain_two, wq, wk, wv, wo, wg, wu, wd, near_cos, near_sin, shift,
    layer_out, gin_out, gain_out, wqkv_out, wo_out, mlpw_out,
    xall, nall, call, w, wof, tiles, qh, kh, vh, att, arow, lse, start, gains, resid, normed2,
    grecv, ff, msend, gatt, gres, low, gain,
    gall, mlp_in, ff_in, wo_core, wo_in, wo_src, wo_line, wq_src, wq_all,
    rows_in, line_in, gsum, tile, wpack, gown_row, bias,
    tsend, trecv, dsend, drecv, local, store,
):
    ln = Links(tsend, trecv, dsend, drecv)
    t, d = ln.t, ln.d
    rows, width = hid.shape
    units = wg.shape[1]
    seq = 4 * rows
    span = width // 4
    half = span // 2
    wide = 2 * span
    core = lax.rem(d, 2)
    wrows = wo.shape[0]
    srows = 4 * wrows
    TILE, W, X, O, C, A, N, G, GA, M, B, OL, WL, R = range(14)
    DT, DW, FW, DO, FO, DR, CO, DOS, CW, DWS, CK, DF = (*range(11), 13)
    V = pltpu.VMEM

    def ds_of(shard):
        return pl.ds(pl.multiple_of(shard * rows, rows), rows)

    def rows_at(ref, shard):
        return ref.at[ds_of(shard), :]

    def w_at(ref, dd, tt=None):
        if tt is None:
            return ref.at[pl.ds(pl.multiple_of(dd * srows, 16), srows), :]
        return ref.at[pl.ds(pl.multiple_of(dd * srows + tt * wrows, 16), wrows), :]

    x_of = functools.partial(rows_at, xall)
    c_of = functools.partial(rows_at, call)

    def wo_of(tt):
        return w_at(wof, d, tt)

    def columns(tt):
        return arow.at[:, pl.ds(pl.multiple_of((tt - 1) * wide, 128), wide)]

    at_own = ds_of(t)
    near, two, three = (tensor_peer(t, m) for m in (1, 2, 3))
    inner, outer = pl.when(ln.mid == 1), pl.when(ln.mid == 0)

    def to_inner(kind, src, dst, act):
        @outer
        def _():
            act(ln.over_tensor(kind, 1, src(near - 1), dst))
            act(ln.over_tensor(kind, 2, src(two - 1), dst))

        @inner
        def _():
            act(ln.over_tensor(kind, 3, src(three - 1), dst))

    def go(c):
        c.start()

    def gone(c):
        c.wait_send()

    def from_inner(kind, take):
        def one(m):
            take(kind, m, tensor_peer(t, m))

        @outer
        def _():
            one(1)
            one(2)

        @inner
        def _():
            one(3)

    def part_rows(ref, dd, h):
        return ref.at[pl.ds(pl.multiple_of(dd * srows + h * (srows // 2), 16), srows // 2), :]

    w_plane = PlaneGather(ln, DW, FW, lambda dd: w_at(w, dd), functools.partial(part_rows, w))
    o_plane = PlaneGather(ln, DO, FO, lambda dd: w_at(wof, dd), functools.partial(part_rows, wof))
    scale = 1.0 / math.sqrt(HEAD)
    layer_sum = LineSum(ln, M, msend, mlp_in)
    ff_sums = [
        PlaneSum(
            ln, DF + k, lambda j, k=k: ff.at[j, k], lambda i, k=k: ff_in.at[i, k], units
        )
        for k in range(3)
    ]

    def visible(shape, b):
        key = lax.broadcasted_iota(jnp.int32, shape, 0)
        query = lax.broadcasted_iota(jnp.int32, shape, 1) + b * rows
        first = start[:, b * rows : (b + 1) * rows].astype(jnp.int32)
        return (key <= query) & (key >= first)

    def front(outh):
        greeted = ln.greet((1, 2, 3), (1, 2, 3, 4, 5, 6, 7))
        tile[...] = jnp.zeros_like(tile)
        tile[0:1, :wrows] = gain_one[...].astype(F32)
        tile[1:2, :wrows] = gain_two[...].astype(F32)
        index = t * rows + lax.broadcasted_iota(jnp.int32, (1, rows), 1)
        tile[2:3, :] = (index - pos[...]).astype(F32)
        for g in range(2):
            wpack[g, :, :wide] = wq[:, g * wide : (g + 1) * wide]
            wpack[g, :, wide : wide + span] = wk[:, g * span : (g + 1) * span]
            wpack[g, :, wide + span :] = wv[:, g * span : (g + 1) * span]
        mine = [
            pltpu.make_async_copy(a, b, local.at[i])
            for i, (a, b) in enumerate(
                [(tile, tiles.at[d, t]), (wo, wo_of(t)), (hid, x_of(t)), (cot, c_of(t))]
            )
        ]
        for c in mine:
            c.start()
        own_w = pltpu.make_async_copy(wpack.at[t - 1], w_at(w, d, t), local.at[4])
        inner(own_w.start)
        pl.semaphore_wait(pltpu.get_barrier_semaphore(), greeted)
        for m in (1, 2, 3):
            ln.over_tensor(TILE, m, tile, tiles.at[d, t]).start()
        to_inner(W, lambda g: wpack.at[g], w_at(w, d, t), go)
        ln.gather_start(O, wo, wo_of)
        inner(ln.over_tensor(C, 1, cot, c_of(t)).start)
        to_inner(X, lambda g: hid, x_of(t), go)
        mine[0].wait()
        for m in (1, 2, 3):
            ln.landed_tensor(TILE, m, tiles.at[d, tensor_peer(t, m)])
        for m in range(1, 8):
            ln.over_dp(DT, m, tiles.at[d], tiles.at[d]).start()

        @inner
        def _():
            own_w.wait()
            for m in (1, 2, 3):
                ln.landed_tensor(W, m, w_at(w, d, tensor_peer(t, m)))
            w_plane.start()

        mine[1].wait()
        for i in (1, 2, 3):
            ln.gather_take(O, i, wo_of)
        o_plane.start()
        mine[3].wait()
        inner(ln.over_tensor(C, 3, cot, c_of(t)).start)
        outer(lambda: ln.gather_start(C, cot, c_of))
        for m in range(1, 8):
            ln.landed_dp(DT, m, tiles.at[dp_peer(d, m)])
        for g in range(4):
            acc = jnp.zeros((8, 8 * wrows), F32)
            for j in range(8):
                r = 8 * g + j
                piece = jnp.concatenate(
                    [tiles[r // 4, r % 4], jnp.zeros((8, 8 * wrows - 128), F32)], axis=1
                )
                acc = acc + lane_roll(piece, wrows * j)
            gains[:, g * 8 * wrows : (g + 1) * 8 * wrows] = acc
        for s in range(4):
            start[:, s * rows : (s + 1) * rows] = tiles[d, s, 2:3, :]
        mine[2].wait()

        def project(s, carry):
            at = ds_of(s)
            x = xall[at, :].astype(F32)
            inv = lax.rsqrt(jnp.mean(x * x, axis=1, keepdims=True) + EPSILON)
            normed = (x * inv * gains[0:1, :]).astype(BF16)
            nall[at, :] = normed
            cosine, sine = turn_tables(near_cos, near_sin, shift, s)
            keep = lax.broadcasted_iota(jnp.int32, (rows, 128), 1) < HEAD

            def head(u, h):
                return jnp.where(keep, lane_roll(u, -HEAD * h)[:, :128], 0.0).astype(BF16)

            for g in range(4):
                u = mm(normed, w[:, g * span : (g + 1) * span])
                if g < 3:
                    u = u * cosine + swap_halves(u) * sine
                for h in range(4):
                    if g < 2:
                        qh[4 * g + h, at, :] = head(u, h)
                    elif g == 2:
                        kh[h, at, :] = head(u, h)
                    else:
                        vh[h, at, :] = head(u, h)
            return carry

        def attend(h, carry):
            @pl.when(h == 0)
            def _():
                for i in (1, 2):
                    ln.gather_take(C, i, c_of)

            c = lax.div(h, 2)
            for b in range(4):
                far = (b + 1) * rows
                here = slice(b * rows, far)
                sc = mm(kh[c, :far, :], qh[h, here, :], NT) * scale + bias[:far, here]
                peak = jnp.max(sc, axis=0, keepdims=True)
                e = jnp.exp(sc - peak)
                total = jnp.sum(e, axis=0, keepdims=True)
                p = (e * (1.0 / total)).astype(BF16)
                outh[h, here, :] = mm(p, vh[c, :far, :], TN)
                lse[h, :, here] = peak + jnp.log(total)
            return carry


        def pack(b, carry):
            for g in range(2):
                acc = jnp.zeros((rows, span), F32)
                for h in range(4):
                    piece = jnp.concatenate(
                        [outh[4 * g + h, ds_of(b), :], jnp.zeros((rows, span - 128), F32)], axis=1
                    )
                    acc = acc + lane_roll(piece, HEAD * h)
                att[b, :, g * span : (g + 1) * span] = acc.astype(BF16)
            return carry

        own = pltpu.make_async_copy(att.at[t], columns(t), local.at[0])

        @inner
        def _():
            for b in range(4):
                far = (b + 1) * rows
                bias[:far, b * rows : far] = jnp.where(visible((far, rows), b), 0.0, MASKED)
            w_plane.hand_on()
            w_plane.take()
            for m in (1, 2, 3):
                ln.landed_tensor(X, m, x_of(tensor_peer(t, m)))
            lax.fori_loop(0, 4, project, 0)

        o_plane.hand_on()

        @inner
        def _():
            lax.fori_loop(0, 8, attend, 0)
            lax.fori_loop(0, 4, pack, 0)
            for m in (2, 1, 3):
                ln.over_tensor(A, m, att.at[tensor_peer(t, m)], columns(t)).start()
            own.start()
            ln.gather_take(C, 3, c_of)
            own.wait()

        o_plane.take()
        from_inner(A, lambda kind, m, p: ln.landed_tensor(kind, m, columns(p)))
        third = width // 3

        def project_out(n, carry):
            cols = pl.ds(pl.multiple_of(n * third, 128), third)
            resid[:, cols] = xall[at_own, cols].astype(F32) + mm(arow[...], wof[:, cols])
            return carry

        lax.fori_loop(0, 3, project_out, 0)
        r = resid[...]
        inv = lax.rsqrt(jnp.mean(r * r, axis=1, keepdims=True) + EPSILON)
        normed2[...] = (r * inv * gains[1:2, :]).astype(BF16)
        ln.gather_start(N, normed2, x_of)
        xall[at_own, :] = normed2[...]

    def feed(loads, gate_w, up_w, down_w, act, gg, gu, gsend, gown, part, gact):
        for c in loads:
            c.wait()

        def to_owner(shard, m):
            return pltpu.make_async_remote_copy(
                src_ref=gsend.at[shard],
                dst_ref=grecv.at[m - 1],
                send_sem=tsend.at[G, m],
                recv_sem=trecv.at[G, m],
                device_id={"dp": d, "tensor": shard},
                device_id_type=MESH,
            )

        @pl.when(ln.mid == 0)
        def _():
            for i in (1, 2, 3):
                ln.gather_take(C, i, c_of)

        piece = units // 4

        def one_shard(i, carry):
            shard, m = ln.shard_at(i)
            at = ds_of(shard)
            gact[...] = mm(call[at, :], down_w[...], NT)

            @pl.when(i > 0)
            def _():
                ln.gather_take(N, i, x_of)

            r = xall[at, :]
            for c in range(4):
                cols = slice(c * piece, (c + 1) * piece)
                gate = mm(r, gate_w[:, cols])
                up = mm(r, up_w[:, cols])
                sig = 1.0 / (1.0 + jnp.exp(-gate))
                silu = gate * sig
                act[at, cols] = (silu * up).astype(BF16)
                g_act = gact[:, cols]
                gg[at, cols] = (g_act * up * sig * (1.0 + gate * (1.0 - sig))).astype(BF16)
                gu[at, cols] = (g_act * silu).astype(BF16)
            g = mm(gg[at, :], gate_w[...], NT) + mm(gu[at, :], up_w[...], NT)

            @pl.when(i == 0)
            def _():
                gown[...] = g

            @pl.when(i > 0)
            def _():
                gsend[shard] = g.astype(BF16)
                to_owner(shard, m).start()

            return carry

        lax.fori_loop(0, 4, one_shard, 0)

        def side(which):
            return pl.ds(pl.multiple_of(which * half, half), half)

        def to_core(k, j):
            return pltpu.make_async_remote_copy(
                src_ref=part.at[j, side(1 - core), :],
                dst_ref=ff.at[j, k],
                send_sem=dsend.at[CK + k, j],
                recv_sem=drecv.at[CK + k, j],
                device_id={"dp": dp_peer(d, 1), "tensor": t},
                device_id_type=MESH,
            )

        def chip_sum(k, j):
            to_core(k, j).wait_recv()
            ff[j, k] = (
                part[j, side(core), :].astype(F32) + ff[j, k].astype(F32)
            ).astype(BF16)
            to_core(k, j).wait_send()

        for k, (a, b) in enumerate(((xall, gg), (xall, gu), (call, act))):

            def weights(j, carry, k=k, a=a, b=b):
                cols = pl.ds(pl.multiple_of(j * span, 128), span)
                if k > 0:

                    @pl.when(j == 2)
                    def _():
                        chip_sum(k - 1, 3)
                        ff_sums[k - 1].start()

                part[j] = mm(a[:, cols], b[...], TN).astype(BF16)
                to_core(k, j).start()

                @pl.when(j > 0)
                def _():
                    chip_sum(k, j - 1)

                return carry

            lax.fori_loop(0, 4, weights, 0)
        chip_sum(2, 3)
        ff_sums[2].start()

        def feed_sums(n, carry):
            third = width // 3
            cols = pl.ds(pl.multiple_of(n * third, 128), third)
            msend[:, :, cols] = mm(act[...], down_w[:, cols]).astype(BF16).reshape(4, rows, third)
            return carry

        lax.fori_loop(0, 3, feed_sums, 0)
        for m in (1, 2, 3):
            ln.landed_tensor(G, m, grecv.at[m - 1])
        g = gown[...]
        for m in (1, 2, 3):
            g = g + grecv[m - 1].astype(F32)
        r = resid[...]
        inv = lax.rsqrt(jnp.mean(r * r, axis=1, keepdims=True) + EPSILON)
        gain[0] = jnp.sum(g * r * inv, axis=0, keepdims=True)
        scaled = g * gains[1:2, :]
        gr = (
            call[at_own, :].astype(F32)
            + inv * scaled
            - r * (inv * inv * inv) * jnp.mean(scaled * r, axis=1, keepdims=True)
        )
        gres[...] = gr
        low[...] = gr.astype(BF16)
        for g in range(2):
            gatt[g] = mm(low[...], wof[g * wide : (g + 1) * wide, :], NT).astype(BF16)
        for m in (1, 2, 3):
            to_owner(tensor_peer(t, m), m).wait_send()

    def forward(gate_w, up_w, down_w):
        loads = [
            pltpu.make_async_copy(a, b, local.at[5 + i])
            for i, (a, b) in enumerate(((wg, gate_w), (wu, up_w), (wd, down_w)))
        ]
        for c in loads:
            c.start()
        pl.run_scoped(front, V((8, seq, 128), F32))
        hidden = V((seq, units), BF16)
        pl.run_scoped(
            functools.partial(feed, loads, gate_w, up_w, down_w),
            hidden, hidden, hidden, V((4, rows, width), BF16), V((rows, width), F32),
            V((4, span, units), BF16), V((rows, units), F32),
        )

    pl.run_scoped(
        forward, V((width, units), BF16), V((width, units), BF16), V((units, width), BF16)
    )

    def backward(gh, gq, gk, gv, gqkv, gn_src, wo_part, layer, gin, wqkv, wo_full, ffw):
        to_inner(GA, lambda g: gatt.at[g], rows_at(gall, t), go)
        own = [
            pltpu.make_async_copy(gatt.at[t - 1], rows_at(gall, t), local.at[0]),
            pltpu.make_async_copy(gain, rows_in.at[pl.ds(d, 1)], local.at[1]),
        ]
        inner(own[0].start)
        own[1].start()
        for m in range(1, 8):
            ln.over_dp(DR, m, gain.at[0], rows_in.at[d]).start()
        layer_sum.start()
        ln.gather_end(O, wo, wo_of)
        o_plane.end()
        wo_pair = CoreSum(ln, CO, wo_part, lambda j: wo_core.at[j])

        def output_weights(j, carry):
            cols = pl.ds(pl.multiple_of(j * span, 128), span)
            wo_part[j] = mm(arow[:, cols], low[...], TN).astype(BF16)
            wo_pair.copy(j).start()
            return carry

        lax.fori_loop(0, 4, output_weights, 0)
        for k in range(2):
            ff_sums[k].hand_on()
        keep = lax.broadcasted_iota(jnp.int32, (rows, 128), 1) < HEAD
        wo_pair.take()
        wo_sum = PlaneSum(ln, DOS, lambda j: wo_core.at[j], lambda i: wo_in.at[i], width)
        wo_sum.start()

        def split(b, carry):
            for g in range(2):
                u = gall[ds_of(b), g * span : (g + 1) * span].astype(F32)
                for h in range(4):
                    gh[4 * g + h, ds_of(b), :] = jnp.where(
                        keep, lane_roll(u, -HEAD * h)[:, :128], 0.0
                    ).astype(BF16)
            return carry

        def attend_back(h, carry):
            c = lax.div(h, 2)
            for b in range(4):
                far = (b + 1) * rows
                here = slice(b * rows, far)
                k, v, q, g = kh[c, :far, :], vh[c, :far, :], qh[h, here, :], gh[h, here, :]
                sc = mm(k, q, NT) * scale + bias[:far, here]
                p = jnp.exp(sc - lse[h, :, here])
                gp = mm(v, g, NT)
                gs = (p * (gp - jnp.sum(p * gp, axis=0, keepdims=True))).astype(BF16)
                gq[h, here, :] = mm(gs, k, TN) * scale
                gk[c, :far, :] += mm(gs, q) * scale
                gv[c, :far, :] += mm(p.astype(BF16), g)
            return carry


        def gather_heads(b, carry):
            at = ds_of(b)
            cosine, sine = turn_tables(near_cos, near_sin, shift, b)
            cosine, sine = cosine[:, :128], sine[:, :128]

            def placed(u, h):
                u = jnp.concatenate(
                    [jnp.where(keep, u, 0.0), jnp.zeros((rows, 4 * HEAD - 128), F32)], axis=1
                )
                return lane_roll(u, HEAD * h)

            def turned(u):
                return u * cosine - swap_halves(u) * sine

            parts = [
                [turned(gq[h, at, :]) for h in range(4)],
                [turned(gq[4 + h, at, :]) for h in range(4)],
                [turned(gk[c, at, :]) for c in range(4)],
                [gv[c, at, :] for c in range(4)],
            ]
            for g, heads in enumerate(parts):
                u = sum(placed(v, h) for h, v in enumerate(heads))
                gqkv[at, g * span : (g + 1) * span] = u.astype(BF16)
            return carry

        def to_row_owner(shard, m):
            return pltpu.make_async_remote_copy(
                src_ref=gn_src.at[shard],
                dst_ref=grecv.at[m - 1],
                send_sem=tsend.at[B, m],
                recv_sem=trecv.at[B, m],
                device_id={"dp": d, "tensor": shard},
                device_id_type=MESH,
            )

        def norm_grads(i, carry):
            shard, m = ln.shard_at(3 - i)
            gn_src[shard] = mm(gqkv[ds_of(shard), :], w[...], NT).astype(BF16)

            @pl.when(i < 3)
            def _():
                to_row_owner(shard, m).start()

            return carry

        @inner
        def _():
            own[0].wait()
            for m in (1, 2, 3):
                ln.landed_tensor(GA, m, rows_at(gall, tensor_peer(t, m)))
            lax.fori_loop(0, 4, split, 0)
            gk[...] = jnp.zeros_like(gk)
            gv[...] = jnp.zeros_like(gv)
            lax.fori_loop(0, 8, attend_back, 0)
            lax.fori_loop(0, 4, gather_heads, 0)
            wo_sum.hand_on()
            lax.fori_loop(0, 4, norm_grads, 0)

        outer(wo_sum.hand_on)
        ff_sums[2].hand_on()

        def in_wo(j):
            return wof.at[pl.ds(pl.multiple_of(j * half, half), half), :]

        def in_wo_half(i):
            return wof.at[(4 + i // 2) * half : (5 + i // 2) * half, (i % 2) * wide : (i % 2 + 1) * wide]

        wo_pair.end()
        wq_pair = CoreSum(ln, CW, wo_part, in_wo)
        wq_sum = PlaneSum(ln, DWS, in_wo, in_wo_half, width)

        def head_weights(j, carry):
            cols = pl.ds(pl.multiple_of(j * span, 128), span)
            wo_part[j] = mm(nall[:, cols], gqkv[...], TN).astype(BF16)
            wq_pair.copy(j).start()
            return carry

        @inner
        def _():
            lax.fori_loop(0, 4, head_weights, 0)
            wq_pair.take()
            wq_sum.start()

        own[1].wait()
        for m in range(1, 8):
            ln.landed_dp(DR, m, rows_in.at[dp_peer(d, m)])
        gsum[0] = sum(rows_in[i] for i in range(8))
        for m in (1, 2, 3):
            ln.over_tensor(R, m, gsum.at[0], line_in.at[m]).start()
        layer_sum.hand_on()
        stores = []

        def out(a, b):
            c = pltpu.make_async_copy(a, b, store.at[len(stores)])
            c.start()
            stores.append(c)

        def to_rows(total, dst):
            lanes = total.lanes
            for h in range(2):
                u = total.take(h).astype(BF16)
                for s in range(4):
                    dst[s, :, h * lanes : (h + 1) * lanes] = u[s * wrows : (s + 1) * wrows, :]

        def feed_weights(k):
            lanes = units // 2
            for h in range(2):
                ffw[k, :, h * lanes : (h + 1) * lanes] = ff_sums[k].take(h)
            out(ffw.at[k], mlpw_out.at[k])

        to_rows(wo_sum, wo_src)
        wo_line_sum = LineSum(ln, OL, wo_src, wo_line)
        wo_line_sum.start()
        inner(wq_sum.hand_on)
        layer[...] = (resid[...] + msend[t].astype(F32) + layer_sum.take()).astype(BF16)
        out(layer, layer_out)
        for k in range(3):
            feed_weights(k)

        @inner
        def _():
            to_rows(wq_sum, wq_src)
            for m in (2, 1, 3):
                ln.over_tensor(WL, m, wq_src.at[tensor_peer(t, m)], wq_all.at[m]).start()
            wqkv[pl.ds(t - 1, 1)] = wq_src[pl.ds(t, 1)].astype(F32)

        wo_line_sum.hand_on()
        total = gsum[0]
        for m in (1, 2, 3):
            ln.landed_tensor(R, m, line_in.at[m])
            total = total + line_in[m]
        mine = (d * 4 + t) * wrows
        turned = pltpu.roll(jnp.broadcast_to(total, (8, width)), lax.rem(width - mine, width), 1)
        gown_row[...] = turned[:, :128]
        out(gown_row, gain_out)
        x = hid[...].astype(F32)
        inv = lax.rsqrt(jnp.mean(x * x, axis=1, keepdims=True) + EPSILON)
        from_inner(B, lambda kind, m, p: ln.landed_tensor(kind, m, grecv.at[m - 1]))

        @outer
        def _():
            gin[...] = grecv[0].astype(F32) + grecv[1].astype(F32)

        @inner
        def _():
            gin[...] = grecv[2].astype(F32) + gn_src[t].astype(F32)

        scaled = gin[...] * gains[0:1, :]
        gin[...] = (
            gres[...]
            + inv * scaled
            - x * (inv * inv * inv) * jnp.mean(scaled * x, axis=1, keepdims=True)
        )
        out(gin, gin_out)
        wo_full[...] = wo_src[t].astype(F32) + wo_line_sum.take()
        out(wo_full, wo_out)

        def columns_in(kind, m, p):
            ln.landed_tensor(kind, m, wq_all.at[m])
            wqkv[pl.ds(p - 1, 1)] = wq_all[pl.ds(m, 1)].astype(F32)

        from_inner(WL, columns_in)
        out(wqkv, wqkv_out)

        for m in (1, 2, 3):
            ln.over_tensor(TILE, m, tile, tiles.at[d, t]).wait_send()
            ln.over_tensor(R, m, gsum.at[0], line_in.at[m]).wait_send()
        to_inner(W, lambda g: wpack.at[g], w_at(w, d, t), gone)
        to_inner(X, lambda g: hid, x_of(t), gone)
        to_inner(GA, lambda g: gatt.at[g], rows_at(gall, t), gone)
        ln.gather_end(C, cot, c_of)
        ln.gather_end(N, normed2, x_of)
        for m in range(1, 8):
            ln.over_dp(DT, m, tiles.at[d], tiles.at[d]).wait_send()
            ln.over_dp(DR, m, gain.at[0], rows_in.at[d]).wait_send()

        @inner
        def _():
            for m in (1, 2, 3):
                ln.over_tensor(A, m, att.at[tensor_peer(t, m)], columns(t)).wait_send()
                ln.over_tensor(WL, m, wq_src.at[tensor_peer(t, m)], wq_all.at[m]).wait_send()
                to_row_owner(tensor_peer(t, m), m).wait_send()
            for s in (w_plane, wq_sum, wq_pair):
                s.end()

        for s in (layer_sum, wo_line_sum, *ff_sums, wo_sum):
            s.end()
        for c in stores:
            c.wait()

    pl.run_scoped(
        backward,
        V((8, seq, 128), BF16), V((8, seq, 128), F32), V((4, seq, 128), F32),
        V((4, seq, 128), F32), V((seq, width), BF16), V((4, rows, width), BF16),
        V((4, span, width), BF16),
        V((rows, width), BF16), V((rows, width), F32), V((2, wrows, width), F32),
        V((wrows, width), F32), V((3, half, units), F32),
    )


def layer(hid, cot, positions, gain_attn, gain_mlp, wq, wk, wv, wo, wg, wu, wd):
    rows, width = hid.shape
    wrows = wq.shape[0]
    units = wg.shape[1]
    seq = 4 * rows
    span = width // 4
    half = span // 2
    near_cos, near_sin, shift = rotary_tables(rows, 4)
    hbm = pl.BlockSpec(memory_space=pl.ANY)
    vmem = pl.BlockSpec(memory_space=pltpu.VMEM)
    V = pltpu.VMEM
    shapes = dict(
        layer=((rows, width), BF16), gin=((rows, width), F32), gain=((8, 128), F32),
        wqkv=((2, wrows, width), F32), wo=((wrows, width), F32),
        mlp=((3, half, units), F32),
    )
    wide = V((seq, width), BF16)
    thin, thin_f = V((rows, width), BF16), V((rows, width), F32)
    four = V((4, rows, width), BF16)
    pair = V((4, seq, 128), BF16)
    outs = pl.pallas_call(
        layer_kernel,
        out_shape=[jax.ShapeDtypeStruct(*v) for v in shapes.values()],
        in_specs=[vmem, hbm] + [vmem] * 6 + [hbm] * 4 + [vmem] * 3,
        out_specs=[hbm] * len(shapes),
        scratch_shapes=[
            wide, wide, wide, V((width, width), BF16), V((width, width), BF16),
            V((8, 4, 8, 128), F32), V((8, seq, 128), BF16), pair, pair,
            V((4, rows, 2 * span), BF16), thin, V((8, 1, seq), F32), V((1, seq), F32),
            V((8, width), F32), thin_f, thin,
            four, V((4, 3, half, units), BF16), four, V((2, rows, 2 * span), BF16), thin_f, thin,
            V((1, 1, width), F32),
            V((seq, 2 * span), BF16), four, V((6, 3, half, units // 2), BF16),
            V((4, half, width), BF16), V((6, half, width // 2), BF16),
            V((4, wrows, width), BF16), V((4, wrows, width), BF16),
            V((4, wrows, width), BF16), V((4, wrows, width), BF16),
            V((8, 1, width), F32), V((4, 1, width), F32), V((1, 1, width), F32),
            V((8, 128), F32), V((2, wrows, width), BF16), V((8, 128), F32), V((seq, seq), F32),
            pltpu.SemaphoreType.DMA((14, 6)), pltpu.SemaphoreType.DMA((14, 4)),
            pltpu.SemaphoreType.DMA((16, 8)), pltpu.SemaphoreType.DMA((16, 8)),
            pltpu.SemaphoreType.DMA((8,)), pltpu.SemaphoreType.DMA((8,)),
        ],
        name="layer",
        compiler_params=pltpu.CompilerParams(
            collective_id=0, has_side_effects=True, vmem_limit_bytes=VMEM_LIMIT
        ),
    )(
        hid, cot, positions.reshape(1, rows), gain_attn.reshape(1, wrows),
        gain_mlp.reshape(1, wrows), wq, wk, wv, wo, wg, wu, wd, near_cos, near_sin, shift,
    )
    return dict(zip(shapes, outs))


def finish_kernel(
    layer, gin, gain, wqkv, wo, mlp, wq, wk, wv, gain_one,
    layer_out, gin_out, gain_one_out, query_out, key_out, value_out, wo_out, gain_two_out,
    gate_out, up_out, down_out,
    lay, gi, ga, w4, wof, ff, one, query, key, value, two, load, store,
):
    moves = [
        (layer, lay, layer_out), (gin, gi, gin_out), (wo, wof, wo_out),
        (mlp.at[0], ff.at[0], gate_out), (mlp.at[1], ff.at[1], up_out),
        (mlp.at[2], ff.at[2], down_out), (wqkv, w4, None), (gain, ga, None),
    ]
    loads = [pltpu.make_async_copy(a, b, load.at[i]) for i, (a, b, _) in enumerate(moves)]
    for i in (6, 7, 0, 1, 2, 3, 4, 5):
        loads[i].start()
    stores = []

    def out(a, b):
        c = pltpu.make_async_copy(a, b, store.at[len(stores)])
        c.start()
        stores.append(c)

    wrows, span = query.shape[0], query.shape[1] // 4
    wide = 2 * span
    loads[6].wait()
    for g in range(2):
        query[:, g * wide : (g + 1) * wide] = w4[g, :, :wide]
        key[:, g * span : (g + 1) * span] = w4[g, :, wide : wide + span]
        value[:, g * span : (g + 1) * span] = w4[g, :, wide + span :]
    out(query, query_out)
    out(key, key_out)
    out(value, value_out)
    total = (
        jnp.sum(wq[...].astype(F32) * query[...], axis=1, keepdims=True)
        + jnp.sum(wk[...].astype(F32) * key[...], axis=1, keepdims=True)
        + jnp.sum(wv[...].astype(F32) * value[...], axis=1, keepdims=True)
    )
    tall = jnp.concatenate(
        [jnp.broadcast_to(total, (wrows, 128)), jnp.zeros((128 - wrows, 128), F32)], axis=0
    )
    one[...] = tall.T[0:1, :wrows] / gain_one[...].astype(F32)
    out(one, gain_one_out)
    loads[7].wait()
    two[...] = ga[0:1, :wrows]
    out(two, gain_two_out)
    for i in range(6):
        loads[i].wait()
        out(moves[i][1], moves[i][2])
    for c in stores:
        c.wait()


def finish(b, wq, wk, wv, gain_attn):
    rows, width = b["layer"].shape
    wrows, kv = wk.shape
    half, units = b["mlp"].shape[1:]
    hbm = pl.BlockSpec(memory_space=pl.ANY)
    vmem = pl.BlockSpec(memory_space=pltpu.VMEM)
    V = pltpu.VMEM
    thin = ((rows, width), F32)
    row = ((1, wrows), F32)
    weight, narrow = ((wrows, width), F32), ((wrows, kv), F32)
    shapes = [
        ((rows, width), BF16), thin, row, weight, narrow, narrow, weight, row,
        ((half, units), F32), ((half, units), F32), ((half, units), F32),
    ]
    return pl.pallas_call(
        finish_kernel,
        out_shape=[jax.ShapeDtypeStruct(*v) for v in shapes],
        in_specs=[hbm] * 6 + [vmem] * 4,
        out_specs=[hbm] * len(shapes),
        scratch_shapes=[
            V((rows, width), BF16), V(*thin), V((8, 128), F32), V((2, wrows, width), F32),
            V(*weight), V((3, half, units), F32), V(*row), V(*weight), V(*narrow), V(*narrow),
            V(*row),
            pltpu.SemaphoreType.DMA((8,)), pltpu.SemaphoreType.DMA((11,)),
        ],
        name="finish",
        compiler_params=pltpu.CompilerParams(vmem_limit_bytes=VMEM_LIMIT),
    )(
        b["layer"], b["gin"], b["gain"], b["wqkv"], b["wo"], b["mlp"], wq, wk, wv,
        gain_attn.reshape(1, wrows),
    )


QUERY_HEADS = 16
KEY_VALUE_HEADS = 8
HEAD_DIMENSION = 96


def angle_tables(pos_rows, head_size):
    half_size = head_size // 2
    freq_rates = ROPE_BASE ** (-(jnp.arange(half_size, dtype=jnp.float32) * 2.0) / head_size)
    turned = pos_rows.astype(jnp.float32)[:, None] * freq_rates[None, :]
    return (jnp.cos(turned)[:, None, :], jnp.sin(turned)[:, None, :])


def apply_rotary(tensor_in, cosine_table, sine_table):
    half_size = tensor_in.shape[-1] // 2
    lo_half = tensor_in[..., :half_size]
    hi_half = tensor_in[..., half_size:]
    return jnp.concatenate(
        [
            lo_half * cosine_table - hi_half * sine_table,
            hi_half * cosine_table + lo_half * sine_table,
        ],
        axis=-1,
    )


def shards(
    hidden_in,
    positions,
    gain_attn,
    w_query,
    key_matrix,
    value_matrix,
    w_output,
    gain_mlp,
    w_gate,
    w_up,
    w_down,
    cotangent,
):
    tok_rows = hidden_in.shape[0]
    model_width = hidden_in.shape[1]
    num_heads = QUERY_HEADS
    key_value_count = KEY_VALUE_HEADS
    head_size = HEAD_DIMENSION
    kv_width = key_value_count * head_size
    queries_per_group = num_heads // key_value_count
    seq_len = tok_rows * lax.axis_size("tensor")
    score_scale = 1.0 / math.sqrt(head_size)
    gathered = (
        lax.all_gather(gain_attn, ("dp", "tensor"), axis=0, tiled=True),
        lax.all_gather(w_query, ("dp", "tensor"), axis=0, tiled=True),
        lax.all_gather(key_matrix, ("dp", "tensor"), axis=0, tiled=True),
        lax.all_gather(value_matrix, ("dp", "tensor"), axis=0, tiled=True),
        lax.all_gather(w_output, ("dp", "tensor"), axis=0, tiled=True),
        lax.all_gather(gain_mlp, ("dp", "tensor"), axis=0, tiled=True),
    )
    gain_one, query_full, key_full, value_full, output_full, gain_two = gathered
    gain_one_f = gain_one.astype(jnp.float32)
    gain_two_f = gain_two.astype(jnp.float32)
    x_float = hidden_in.astype(jnp.float32)
    inv_one = lax.rsqrt(jnp.mean(x_float * x_float, axis=-1, keepdims=True) + EPSILON)
    normed_one = (x_float * inv_one * gain_one_f).astype(jnp.bfloat16)
    queries = jnp.dot(normed_one, query_full, preferred_element_type=jnp.float32)
    key_projected = jnp.dot(normed_one, key_full, preferred_element_type=jnp.float32)
    value_proj = jnp.dot(normed_one, value_full, preferred_element_type=jnp.float32)
    cosine_table, sine_table = angle_tables(positions, head_size)
    rotated_query_rows = apply_rotary(
        queries.reshape(tok_rows, num_heads, head_size), cosine_table, sine_table
    ).astype(jnp.bfloat16)
    rotated_key_rows = (
        apply_rotary(
            key_projected.reshape(tok_rows, key_value_count, head_size), cosine_table, sine_table
        )
        .astype(jnp.bfloat16)
        .reshape(tok_rows, kv_width)
    )
    value_rows_lowered = value_proj.astype(jnp.bfloat16)
    keys_all, values_all = (
        lax.all_gather(rotated_key_rows, "tensor", axis=0, tiled=True),
        lax.all_gather(value_rows_lowered, "tensor", axis=0, tiled=True),
    )
    offset = lax.axis_index("tensor") * tok_rows
    query_index = offset + jnp.arange(tok_rows, dtype=jnp.int32)
    key_index = jnp.arange(seq_len, dtype=jnp.int32)
    visible = (key_index[None, :] <= query_index[:, None]) & (
        key_index[None, :] >= (query_index - positions)[:, None]
    )
    visible = jnp.tile(visible, (queries_per_group, 1))

    def split_queries(tensor_in):
        return (
            tensor_in.reshape(tok_rows, key_value_count, queries_per_group, head_size)
            .transpose(1, 2, 0, 3)
            .reshape(key_value_count, queries_per_group * tok_rows, head_size)
        )

    def split_keys(tensor_in):
        return tensor_in.reshape(seq_len, key_value_count, head_size).transpose(1, 0, 2)

    def merge_heads(tensor_in):
        return (
            tensor_in.reshape(key_value_count, queries_per_group, tok_rows, head_size)
            .transpose(2, 0, 1, 3)
            .reshape(tok_rows, model_width)
        )

    query_heads = split_queries(rotated_query_rows)
    k_heads = split_keys(keys_all)
    value_heads = split_keys(values_all)

    def attend(head_items):
        q_block, k_block, v_block = head_items
        scores = (
            jnp.einsum("qd,kd->qk", q_block, k_block, preferred_element_type=jnp.float32)
            * score_scale
        )
        scores = jnp.where(visible, scores, MASKED)
        peak = jnp.max(scores, axis=-1, keepdims=True)
        exp_vals = jnp.exp(scores - peak)
        total = jnp.sum(exp_vals, axis=-1, keepdims=True)
        probs = exp_vals / total
        out_block = jnp.einsum(
            "qk,kd->qd", probs.astype(jnp.bfloat16), v_block, preferred_element_type=jnp.float32
        )
        return (out_block, peak[:, 0] + jnp.log(total[:, 0]))

    attended_rows, log_total = lax.map(attend, (query_heads, k_heads, value_heads))
    attended_low = merge_heads(attended_rows).astype(jnp.bfloat16)
    resid_sum = x_float + jnp.dot(attended_low, output_full, preferred_element_type=jnp.float32)
    inv_two = lax.rsqrt(jnp.mean(resid_sum * resid_sum, axis=-1, keepdims=True) + EPSILON)
    normed_two = (resid_sum * inv_two * gain_two_f).astype(jnp.bfloat16)
    rows_all = lax.all_gather(normed_two, "tensor", axis=0, tiled=True)
    gate_val = jnp.dot(rows_all, w_gate, preferred_element_type=jnp.float32)
    up_val = jnp.dot(rows_all, w_up, preferred_element_type=jnp.float32)
    sig_gate = jax.nn.sigmoid(gate_val)
    silu_gate = gate_val * sig_gate
    act_low = (silu_gate * up_val).astype(jnp.bfloat16)
    mlp_sum = lax.psum_scatter(
        jnp.dot(act_low, w_down, preferred_element_type=jnp.float32).astype(jnp.bfloat16),
        "tensor",
        scatter_dimension=0,
        tiled=True,
    ).astype(jnp.float32)
    layer_out = (resid_sum + mlp_sum).astype(jnp.bfloat16)
    grad_float = cotangent.astype(jnp.float32)
    grad_all = lax.all_gather(cotangent, "tensor", axis=0, tiled=True)
    grad_down = jnp.einsum("sf,sd->fd", act_low, grad_all, preferred_element_type=jnp.float32)
    g_act = jnp.einsum("sd,fd->sf", grad_all, w_down, preferred_element_type=jnp.float32)
    g_gate = (g_act * up_val * sig_gate * (1.0 + gate_val * (1.0 - sig_gate))).astype(jnp.bfloat16)
    g_up = (g_act * silu_gate).astype(jnp.bfloat16)
    grad_gate = jnp.einsum("sd,sf->df", rows_all, g_gate, preferred_element_type=jnp.float32)
    grad_up = jnp.einsum("sd,sf->df", rows_all, g_up, preferred_element_type=jnp.float32)
    g_norm_two = lax.psum_scatter(
        (
            jnp.einsum("sf,df->sd", g_gate, w_gate, preferred_element_type=jnp.float32)
            + jnp.einsum("sf,df->sd", g_up, w_up, preferred_element_type=jnp.float32)
        ).astype(jnp.bfloat16),
        "tensor",
        scatter_dimension=0,
        tiled=True,
    ).astype(jnp.float32)
    scaled_two = gain_two_f * g_norm_two
    grad_gain_two = jnp.sum(g_norm_two * resid_sum * inv_two, axis=0)
    g_resid = (
        grad_float
        + inv_two * scaled_two
        - resid_sum * inv_two**3 * jnp.mean(scaled_two * resid_sum, axis=-1, keepdims=True)
    )
    g_resid_low = g_resid.astype(jnp.bfloat16)
    grad_output = jnp.einsum(
        "tc,td->cd", attended_low, g_resid_low, preferred_element_type=jnp.float32
    )
    g_att = jnp.einsum(
        "td,cd->tc", g_resid_low, output_full, preferred_element_type=jnp.float32
    ).astype(jnp.bfloat16)
    g_heads = split_queries(g_att)

    def attend_back(head_items):
        q_block, k_block, v_block, log_block, g_block = head_items
        scores = (
            jnp.einsum("qd,kd->qk", q_block, k_block, preferred_element_type=jnp.float32)
            * score_scale
        )
        scores = jnp.where(visible, scores, MASKED)
        probs = jnp.exp(scores - log_block[:, None])
        g_probs = jnp.einsum("qd,kd->qk", g_block, v_block, preferred_element_type=jnp.float32)
        g_scores = (probs * (g_probs - jnp.sum(probs * g_probs, axis=-1, keepdims=True))).astype(
            jnp.bfloat16
        )
        g_rq = (
            jnp.einsum("qk,kd->qd", g_scores, k_block, preferred_element_type=jnp.float32)
            * score_scale
        )
        g_rk = (
            jnp.einsum("qk,qd->kd", g_scores, q_block, preferred_element_type=jnp.float32)
            * score_scale
        )
        g_val = jnp.einsum(
            "qk,qd->kd", probs.astype(jnp.bfloat16), g_block, preferred_element_type=jnp.float32
        )
        return (g_rq, g_rk, g_val)

    g_rq, g_rk, g_val = lax.map(
        attend_back, (query_heads, k_heads, value_heads, log_total, g_heads)
    )
    g_rk_flat = g_rk.transpose(1, 0, 2).reshape(seq_len, kv_width)
    g_val_flat = g_val.transpose(1, 0, 2).reshape(seq_len, kv_width)
    key_part, value_part = (
        lax.psum_scatter(
            g_rk_flat.astype(jnp.bfloat16), "tensor", scatter_dimension=0, tiled=True
        ).astype(jnp.float32),
        lax.psum_scatter(
            g_val_flat.astype(jnp.bfloat16), "tensor", scatter_dimension=0, tiled=True
        ).astype(jnp.float32),
    )
    g_queries = (
        apply_rotary(
            merge_heads(g_rq).reshape(tok_rows, num_heads, head_size), cosine_table, -sine_table
        )
        .reshape(tok_rows, model_width)
        .astype(jnp.bfloat16)
    )
    g_keys = (
        apply_rotary(
            key_part.reshape(tok_rows, key_value_count, head_size), cosine_table, -sine_table
        )
        .reshape(tok_rows, kv_width)
        .astype(jnp.bfloat16)
    )
    g_values = value_part.astype(jnp.bfloat16)
    grad_query = jnp.einsum("tc,td->cd", normed_one, g_queries, preferred_element_type=jnp.float32)
    grad_key = jnp.einsum("tc,td->cd", normed_one, g_keys, preferred_element_type=jnp.float32)
    grad_value = jnp.einsum("tc,td->cd", normed_one, g_values, preferred_element_type=jnp.float32)
    g_norm_one = (
        jnp.einsum("td,cd->tc", g_queries, query_full, preferred_element_type=jnp.float32)
        + jnp.einsum("td,cd->tc", g_keys, key_full, preferred_element_type=jnp.float32)
        + jnp.einsum("td,cd->tc", g_values, value_full, preferred_element_type=jnp.float32)
    )
    scaled_one = gain_one_f * g_norm_one
    grad_gain_one = jnp.sum(g_norm_one * x_float * inv_one, axis=0)
    grad_input = (
        g_resid
        + inv_one * scaled_one
        - x_float * inv_one**3 * jnp.mean(scaled_one * x_float, axis=-1, keepdims=True)
    )
    packed = jnp.concatenate([grad_query, grad_key, grad_value, grad_output], axis=1)
    packed_part = lax.psum_scatter(
        packed.astype(jnp.bfloat16), ("dp", "tensor"), scatter_dimension=0, tiled=True
    ).astype(jnp.float32)
    query_part = packed_part[:, :model_width]
    keyw_part = packed_part[:, model_width : model_width + kv_width]
    valuew_part = packed_part[:, model_width + kv_width : model_width + 2 * kv_width]
    out_part = packed_part[:, model_width + 2 * kv_width :]
    gain_one_part, gain_two_part = (
        lax.psum_scatter(grad_gain_one, ("dp", "tensor"), scatter_dimension=0, tiled=True),
        lax.psum_scatter(grad_gain_two, ("dp", "tensor"), scatter_dimension=0, tiled=True),
    )
    gate_sum, up_sum, down_sum = (
        lax.psum_scatter(
            grad_gate.astype(jnp.bfloat16), "dp", scatter_dimension=0, tiled=True
        ).astype(jnp.float32),
        lax.psum_scatter(
            grad_up.astype(jnp.bfloat16), "dp", scatter_dimension=0, tiled=True
        ).astype(jnp.float32),
        lax.psum_scatter(
            grad_down.astype(jnp.bfloat16), "dp", scatter_dimension=1, tiled=True
        ).astype(jnp.float32),
    )
    return (
        layer_out,
        grad_input,
        gain_one_part,
        query_part,
        keyw_part,
        valuew_part,
        out_part,
        gain_two_part,
        gate_sum,
        up_sum,
        down_sum,
    )


def fast_shards(
    hidden_in, positions, gain_attn, w_query, key_matrix, value_matrix, w_output, gain_mlp,
    w_gate, w_up, w_down, cotangent,
):
    b = layer(
        hidden_in, cotangent, positions, gain_attn, gain_mlp, w_query, key_matrix, value_matrix,
        w_output, w_gate, w_up, w_down,
    )
    o = finish(b, w_query, key_matrix, value_matrix, gain_attn)
    wrows = w_query.shape[0]
    return (
        o[0], o[1], o[2].reshape(wrows), o[3], o[4], o[5], o[6], o[7].reshape(wrows), o[8], o[9], o[10].T,
    )


def solution(mesh):
    placed = (
        P(("dp", "tensor"), None),
        P(("dp", "tensor")),
        P(("dp", "tensor")),
        P(("dp", "tensor"), None),
        P(("dp", "tensor"), None),
        P(("dp", "tensor"), None),
        P(("dp", "tensor"), None),
        P(("dp", "tensor")),
        P(None, "tensor"),
        P(None, "tensor"),
        P("tensor", None),
        P(("dp", "tensor"), None),
    )
    fits = mesh.shape["dp"] == 8 and mesh.shape["tensor"] == 4
    return jax.shard_map(
        fast_shards if fits else shards,
        mesh=mesh,
        in_specs=placed,
        out_specs=(
            P(("dp", "tensor"), None),
            P(("dp", "tensor"), None),
            P(("dp", "tensor")),
            P(("dp", "tensor"), None),
            P(("dp", "tensor"), None),
            P(("dp", "tensor"), None),
            P(("dp", "tensor"), None),
            P(("dp", "tensor")),
            P("dp", "tensor"),
            P("dp", "tensor"),
            P("tensor", "dp"),
        ),
        check_vma=False,
    )
```

```python
import functools
import math

import jax
import jax.numpy as jnp
import numpy as np
from jax import lax
from jax.experimental import pallas as pl
from jax.experimental.pallas import tpu as pltpu
from jax.sharding import PartitionSpec as P

F32 = jnp.float32
BF16 = jnp.bfloat16
MESH = pl.DeviceIdType.MESH
EPSILON = 1e-05
ROPE_BASE = 100000.0
MASKED = -1e30
HEAD = 96
VMEM_LIMIT = 64 * 2**20 - 65536


def rotary_tables(rows, shards_in_sequence):
    half = HEAD // 2
    lanes = np.arange(4 * HEAD) % half
    rates = ROPE_BASE ** (-(lanes * 2.0) / HEAD)
    near = np.arange(rows)[:, None] * rates[None, :]
    far = (np.arange(shards_in_sequence) * rows)[:, None] * rates[None, :]
    shift = np.concatenate([np.cos(far), np.sin(far)], axis=0)
    return (
        np.cos(near).astype(np.float32),
        np.sin(near).astype(np.float32),
        shift.astype(np.float32),
    )


def tensor_peer(t, m):
    if m == 1:
        return t + 1 - 2 * lax.rem(t, 2)
    if m == 2:
        return lax.rem(t + 2, 4)
    return 3 - t


def dp_peer(d, m):
    if m & 1:
        d = d + 1 - 2 * lax.rem(d, 2)
    if m & 2:
        d = d + 2 - 4 * lax.rem(lax.div(d, 2), 2)
    if m & 4:
        d = lax.rem(d + 4, 8)
    return d


class Links:
    def __init__(self, tsend, trecv, dsend, drecv):
        self.t = lax.axis_index("tensor")
        self.d = lax.axis_index("dp")
        self.mid = lax.rem(lax.div(self.t + 1, 2), 2)
        self.tsend, self.trecv, self.dsend, self.drecv = tsend, trecv, dsend, drecv

    def shard_at(self, i):
        t, mid = self.t, self.mid
        near, two, three = (tensor_peer(t, m) for m in (1, 2, 3))
        if isinstance(i, int):
            if i == 0:
                return t, 0
            if i == 1:
                return near, 1
            if i == 2:
                return two + mid * (three - two), 2 + mid
            return three + mid * (two - three), 3 - mid
        one_if = [1 - jnp.minimum(jnp.abs(i - k), 1) for k in range(4)]
        pairs = [self.shard_at(k) for k in range(4)]
        return (
            sum(f * p[0] for f, p in zip(one_if, pairs)),
            sum(f * p[1] for f, p in zip(one_if, pairs)),
        )

    def over_tensor(self, kind, m, src, dst, recv=None):
        peer = tensor_peer(self.t, m)
        return pltpu.make_async_remote_copy(
            src_ref=src,
            dst_ref=dst,
            send_sem=self.tsend.at[kind, m],
            recv_sem=self.trecv.at[kind, m if recv is None else recv],
            device_id={"dp": self.d, "tensor": peer},
            device_id_type=MESH,
        )

    def over_dp(self, kind, m, src, dst, to=None):
        peer = dp_peer(self.d, m if to is None else to)
        return pltpu.make_async_remote_copy(
            src_ref=src,
            dst_ref=dst,
            send_sem=self.dsend.at[kind, m],
            recv_sem=self.drecv.at[kind, m],
            device_id={"dp": peer, "tensor": self.t},
            device_id_type=MESH,
        )

    def landed_tensor(self, kind, m, ref):
        pltpu.make_async_copy(ref, ref, self.trecv.at[kind, m]).wait()

    def landed_dp(self, kind, m, ref):
        pltpu.make_async_copy(ref, ref, self.drecv.at[kind, m]).wait()

    def gather_start(self, kind, src, at):
        own = at(self.t)
        self.over_tensor(kind, 1, src, own).start()

        @pl.when(self.mid == 0)
        def _():
            self.over_tensor(kind, 2, src, own).start()

        @pl.when(self.mid == 1)
        def _():
            self.over_tensor(kind, 3, src, own).start()

    def gather_take(self, kind, i, at):
        shard, m = self.shard_at(i)
        block = at(shard)
        self.landed_tensor(kind, m, block)

        def hand_on():
            pltpu.make_async_remote_copy(
                src_ref=block,
                dst_ref=block,
                send_sem=self.tsend.at[kind, 2 + i],
                recv_sem=self.trecv.at[kind, 5 - m],
                device_id={"dp": self.d, "tensor": tensor_peer(self.t, 1)},
                device_id_type=MESH,
            ).start()

        if isinstance(i, int):
            if i >= 2:
                pl.when(self.mid == 1)(hand_on)
        else:
            pl.when((self.mid == 1) & (i >= 2))(hand_on)

    def gather_end(self, kind, src, at):
        own = at(self.t)
        self.over_tensor(kind, 1, src, own).wait_send()

        @pl.when(self.mid == 0)
        def _():
            self.over_tensor(kind, 2, src, own).wait_send()

        @pl.when(self.mid == 1)
        def _():
            self.over_tensor(kind, 3, src, own).wait_send()
            for i in (2, 3):
                shard, m = self.shard_at(i)
                pltpu.make_async_copy(at(shard), at(shard), self.tsend.at[kind, 2 + i]).wait()

    def greet(self, tensor_peers, dp_peers):
        sem = pltpu.get_barrier_semaphore()
        for m in tensor_peers:
            pl.semaphore_signal(
                sem,
                inc=1,
                device_id={"dp": self.d, "tensor": tensor_peer(self.t, m)},
                device_id_type=MESH,
            )
        for m in dp_peers:
            pl.semaphore_signal(
                sem,
                inc=1,
                device_id={"dp": dp_peer(self.d, m), "tensor": self.t},
                device_id_type=MESH,
            )
        return len(tensor_peers) + len(dp_peers)


def mm(a, b, dims=((1,), (0,))):
    return lax.dot_general(a, b, (dims, ((), ())), preferred_element_type=F32)


NN = ((1,), (0,))
NT = ((1,), (1,))
TN = ((0,), (0,))


def lane_roll(u, by):
    return pltpu.roll(u, by % u.shape[-1], u.ndim - 1)


def swap_halves(u):
    lane = lax.broadcasted_iota(jnp.int32, u.shape, 1)
    low = lax.rem(lane, HEAD) < HEAD // 2
    return jnp.where(low, -lane_roll(u, -(HEAD // 2)), lane_roll(u, HEAD // 2))


def turn_tables(near_cos, near_sin, shift, shard):
    c = shift[pl.ds(shard, 1), :]
    s = shift[pl.ds(shard + 4, 1), :]
    a, b = near_cos[...], near_sin[...]
    return a * c - b * s, b * c + a * s


class LineSum:
    def __init__(self, ln, kind, src, recv):
        self.ln, self.kind, self.src, self.recv = ln, kind, src, recv
        t = ln.t
        self.near, self.two, self.three = (tensor_peer(t, m) for m in (1, 2, 3))

    def copy(self, src, to, slot, sem):
        ln, kind = self.ln, self.kind
        return pltpu.make_async_remote_copy(
            src_ref=src,
            dst_ref=self.recv.at[slot],
            send_sem=ln.tsend.at[kind, sem],
            recv_sem=ln.trecv.at[kind, slot],
            device_id={"dp": ln.d, "tensor": to},
            device_id_type=MESH,
        )

    def first(self, i, shard):
        c = self.copy(self.src.at[shard], self.near, i, i)
        if isinstance(i, int):
            if i == 2:
                c.start()
            else:
                pl.when(self.ln.mid == 0)(c.start)
        else:
            pl.when((i == 2) | ((self.ln.mid == 0) & (i < 2)))(c.start)

    def start(self):
        for i, shard in enumerate((self.three, self.two, self.near)):
            self.first(i, shard)

    def hand_on(self):
        @pl.when(self.ln.mid == 1)
        def _():
            for i, shard in enumerate((self.two, self.three)):
                self.ln.landed_tensor(self.kind, i, self.recv.at[i])
                self.recv[i] = (
                    self.recv[i].astype(F32) + self.src[shard].astype(F32)
                ).astype(BF16)
                self.copy(self.recv.at[i], shard, 3, i).start()

    def take(self):
        for i in (2, 3):
            self.ln.landed_tensor(self.kind, i, self.recv.at[i])
        return self.recv[2].astype(F32) + self.recv[3].astype(F32)

    def end(self):
        for i in range(3):
            pltpu.make_async_copy(
                self.src.at[0], self.src.at[0], self.ln.tsend.at[self.kind, i]
            ).wait()


class PlaneSum:
    def __init__(self, ln, kind, src, slot, width):
        self.ln, self.kind, self.src, self.slot = ln, kind, src, slot
        j = lax.div(ln.d, 2)
        self.j = j
        self.x = j + 1 - 2 * lax.rem(j, 2)
        self.y = lax.rem(j + 2, 4)
        self.diag = lax.rem(self.x + 2, 4)
        self.lanes = width // 2

    def half(self, ref, h):
        spot = [slice(None)] * (len(ref.shape) - 1) + [pl.ds(h * self.lanes, self.lanes)]
        return ref.at[tuple(spot)]

    def copy(self, src, m, i):
        return self.ln.over_dp(self.kind, i, src, self.slot(i), to=m)

    def plan(self):
        return (
            (self.half(self.src(self.diag), 0), 2, 0),
            (self.half(self.src(self.diag), 1), 4, 2),
            (self.half(self.src(self.x), 0), 2, 1),
            (self.half(self.src(self.y), 1), 4, 3),
        )

    def start(self):
        for src, m, i in self.plan():
            self.copy(src, m, i).start()

    def hand_on(self):
        for i, h, block, m in ((0, 0, self.y, 4), (2, 1, self.x, 2)):
            self.ln.landed_dp(self.kind, i, self.slot(i))
            self.slot(i)[...] = (
                self.slot(i)[...].astype(F32) + self.half(self.src(block), h)[...].astype(F32)
            ).astype(BF16)
            self.copy_on(i, h, m).start()

    def copy_on(self, i, h, m):
        return self.ln.over_dp(self.kind, 4 + h, self.slot(i), self.slot(4 + h), to=m)

    def take(self, h):
        for i in (1 + 2 * h, 4 + h):
            self.ln.landed_dp(self.kind, i, self.slot(i))
        own = self.half(self.src(self.j), h)[...].astype(F32)
        return own + self.slot(1 + 2 * h)[...].astype(F32) + self.slot(4 + h)[...].astype(F32)

    def end(self):
        for src, m, i in self.plan():
            self.copy(src, m, i).wait_send()
        for i, h, m in ((0, 0, 4), (2, 1, 2)):
            self.copy_on(i, h, m).wait_send()


class PlaneGather:
    def __init__(self, ln, kind, hand, block, part):
        self.ln, self.kind, self.hand, self.block, self.part = ln, kind, hand, block, part

    def own(self, m):
        here = self.block(self.ln.d)
        return self.ln.over_dp(self.kind, m, here, here)

    def on(self, m):
        h, to, i = (0, 4, 3) if m == 2 else (1, 2, 5)
        piece = self.part(dp_peer(self.ln.d, m), h)
        return self.ln.over_dp(self.kind, i, piece, piece, to=to)

    def core(self, m):
        block = self.block(dp_peer(self.ln.d, m))
        return self.ln.over_dp(self.hand, m, block, block, to=1)

    def start(self):
        for m in (2, 4, 1):
            self.own(m).start()

    def hand_on(self):
        for m in (2, 4):
            self.ln.landed_dp(self.kind, m, self.block(dp_peer(self.ln.d, m)))
            self.on(m).start()
            self.core(m).start()

    def take(self):
        far = dp_peer(self.ln.d, 6)
        for h, i in ((0, 3), (1, 5)):
            self.ln.landed_dp(self.kind, i, self.part(far, h))
        self.core(6).start()
        self.ln.landed_dp(self.kind, 1, self.block(dp_peer(self.ln.d, 1)))
        for m in (2, 4, 6):
            self.ln.landed_dp(self.hand, m, self.block(dp_peer(self.ln.d, m ^ 1)))

    def end(self):
        for m in (2, 4, 1):
            self.own(m).wait_send()
        for m in (2, 4):
            self.on(m).wait_send()
        for m in (2, 4, 6):
            self.core(m).wait_send()


class CoreSum:
    def __init__(self, ln, kind, src, slot):
        self.ln, self.kind, self.src, self.slot = ln, kind, src, slot
        self.half = src.shape[1] // 2
        self.core = lax.rem(ln.d, 2)

    def side(self, which):
        return pl.ds(pl.multiple_of(which * self.half, self.half), self.half)

    def copy(self, j):
        ln = self.ln
        return pltpu.make_async_remote_copy(
            src_ref=self.src.at[j, self.side(1 - self.core), :],
            dst_ref=self.slot(j),
            send_sem=ln.dsend.at[self.kind, j],
            recv_sem=ln.drecv.at[self.kind, j],
            device_id={"dp": dp_peer(ln.d, 1), "tensor": ln.t},
            device_id_type=MESH,
        )

    def take(self):
        def one(j, carry):
            self.copy(j).wait_recv()
            self.slot(j)[...] = (
                self.slot(j)[...].astype(F32) + self.src[j, self.side(self.core), :].astype(F32)
            ).astype(BF16)
            return carry

        lax.fori_loop(0, 4, one, 0)

    def end(self):
        def one(j, carry):
            self.copy(j).wait_send()
            return carry

        lax.fori_loop(0, 4, one, 0)


def layer_kernel(
    hid, cot, pos, gain_one, gain_two, wq, wk, wv, wo, wg, wu, wd, near_cos, near_sin, shift,
    layer_out, gin_out, gain_out, wqkv_out, wo_out, mlpw_out,
    xall, nall, call, w, wof, tiles, qh, kh, vh, att, arow, lse, start, gains, resid, normed2,
    grecv, ff, msend, gatt, gres, low, gain,
    gall, mlp_in, ff_in, wo_core, wo_in, wo_src, wo_line, wq_src, wq_all,
    rows_in, line_in, gsum, tile, wpack, gown_row, bias,
    tsend, trecv, dsend, drecv, local, store,
):
    ln = Links(tsend, trecv, dsend, drecv)
    t, d = ln.t, ln.d
    rows, width = hid.shape
    units = wg.shape[1]
    seq = 4 * rows
    span = width // 4
    half = span // 2
    wide = 2 * span
    core = lax.rem(d, 2)
    wrows = wo.shape[0]
    srows = 4 * wrows
    TILE, W, X, O, C, A, N, G, GA, M, B, OL, WL, R = range(14)
    DT, DW, FW, DO, FO, DR, CO, DOS, CW, DWS, CK, DF = (*range(11), 13)
    V = pltpu.VMEM

    def ds_of(shard):
        return pl.ds(pl.multiple_of(shard * rows, rows), rows)

    def rows_at(ref, shard):
        return ref.at[ds_of(shard), :]

    def w_at(ref, dd, tt=None):
        if tt is None:
            return ref.at[pl.ds(pl.multiple_of(dd * srows, 16), srows), :]
        return ref.at[pl.ds(pl.multiple_of(dd * srows + tt * wrows, 16), wrows), :]

    x_of = functools.partial(rows_at, xall)
    c_of = functools.partial(rows_at, call)

    def wo_of(tt):
        return w_at(wof, d, tt)

    def columns(tt):
        return arow.at[:, pl.ds(pl.multiple_of((tt - 1) * wide, 128), wide)]

    at_own = ds_of(t)
    near, two, three = (tensor_peer(t, m) for m in (1, 2, 3))
    inner, outer = pl.when(ln.mid == 1), pl.when(ln.mid == 0)

    def to_inner(kind, src, dst, act):
        @outer
        def _():
            act(ln.over_tensor(kind, 1, src(near - 1), dst))
            act(ln.over_tensor(kind, 2, src(two - 1), dst))

        @inner
        def _():
            act(ln.over_tensor(kind, 3, src(three - 1), dst))

    def go(c):
        c.start()

    def gone(c):
        c.wait_send()

    def from_inner(kind, take):
        def one(m):
            take(kind, m, tensor_peer(t, m))

        @outer
        def _():
            one(1)
            one(2)

        @inner
        def _():
            one(3)

    def part_rows(ref, dd, h):
        return ref.at[pl.ds(pl.multiple_of(dd * srows + h * (srows // 2), 16), srows // 2), :]

    w_plane = PlaneGather(ln, DW, FW, lambda dd: w_at(w, dd), functools.partial(part_rows, w))
    o_plane = PlaneGather(ln, DO, FO, lambda dd: w_at(wof, dd), functools.partial(part_rows, wof))
    scale = 1.0 / math.sqrt(HEAD)
    layer_sum = LineSum(ln, M, msend, mlp_in)
    ff_sums = [
        PlaneSum(
            ln, DF + k, lambda j, k=k: ff.at[j, k], lambda i, k=k: ff_in.at[i, k], units
        )
        for k in range(3)
    ]

    def visible(shape, b):
        key = lax.broadcasted_iota(jnp.int32, shape, 0)
        query = lax.broadcasted_iota(jnp.int32, shape, 1) + b * rows
        first = start[:, b * rows : (b + 1) * rows].astype(jnp.int32)
        return (key <= query) & (key >= first)

    def front(outh):
        greeted = ln.greet((1, 2, 3), (1, 2, 3, 4, 5, 6, 7))
        tile[...] = jnp.zeros_like(tile)
        tile[0:1, :wrows] = gain_one[...].astype(F32)
        tile[1:2, :wrows] = gain_two[...].astype(F32)
        index = t * rows + lax.broadcasted_iota(jnp.int32, (1, rows), 1)
        tile[2:3, :] = (index - pos[...]).astype(F32)
        for g in range(2):
            wpack[g, :, :wide] = wq[:, g * wide : (g + 1) * wide]
            wpack[g, :, wide : wide + span] = wk[:, g * span : (g + 1) * span]
            wpack[g, :, wide + span :] = wv[:, g * span : (g + 1) * span]
        mine = [
            pltpu.make_async_copy(a, b, local.at[i])
            for i, (a, b) in enumerate(
                [(tile, tiles.at[d, t]), (wo, wo_of(t)), (hid, x_of(t)), (cot, c_of(t))]
            )
        ]
        for c in mine:
            c.start()
        own_w = pltpu.make_async_copy(wpack.at[t - 1], w_at(w, d, t), local.at[4])
        inner(own_w.start)
        pl.semaphore_wait(pltpu.get_barrier_semaphore(), greeted)
        for m in (1, 2, 3):
            ln.over_tensor(TILE, m, tile, tiles.at[d, t]).start()
        to_inner(W, lambda g: wpack.at[g], w_at(w, d, t), go)
        ln.gather_start(O, wo, wo_of)
        inner(ln.over_tensor(C, 1, cot, c_of(t)).start)
        to_inner(X, lambda g: hid, x_of(t), go)
        mine[0].wait()
        for m in (1, 2, 3):
            ln.landed_tensor(TILE, m, tiles.at[d, tensor_peer(t, m)])
        for m in range(1, 8):
            ln.over_dp(DT, m, tiles.at[d], tiles.at[d]).start()

        @inner
        def _():
            own_w.wait()
            for m in (1, 2, 3):
                ln.landed_tensor(W, m, w_at(w, d, tensor_peer(t, m)))
            w_plane.start()

        mine[1].wait()
        for i in (1, 2, 3):
            ln.gather_take(O, i, wo_of)
        outer(o_plane.start)
        mine[3].wait()
        inner(ln.over_tensor(C, 3, cot, c_of(t)).start)
        outer(lambda: ln.gather_start(C, cot, c_of))
        for m in range(1, 8):
            ln.landed_dp(DT, m, tiles.at[dp_peer(d, m)])
        for g in range(4):
            acc = jnp.zeros((8, 8 * wrows), F32)
            for j in range(8):
                r = 8 * g + j
                piece = jnp.concatenate(
                    [tiles[r // 4, r % 4], jnp.zeros((8, 8 * wrows - 128), F32)], axis=1
                )
                acc = acc + lane_roll(piece, wrows * j)
            gains[:, g * 8 * wrows : (g + 1) * 8 * wrows] = acc
        for s in range(4):
            start[:, s * rows : (s + 1) * rows] = tiles[d, s, 2:3, :]
        mine[2].wait()

        def project(s, carry):
            at = ds_of(s)
            x = xall[at, :].astype(F32)
            inv = lax.rsqrt(jnp.mean(x * x, axis=1, keepdims=True) + EPSILON)
            normed = (x * inv * gains[0:1, :]).astype(BF16)
            nall[at, :] = normed
            cosine, sine = turn_tables(near_cos, near_sin, shift, s)
            keep = lax.broadcasted_iota(jnp.int32, (rows, 128), 1) < HEAD

            def head(u, h):
                return jnp.where(keep, lane_roll(u, -HEAD * h)[:, :128], 0.0).astype(BF16)

            for g in range(4):
                u = mm(normed, w[:, g * span : (g + 1) * span])
                if g < 3:
                    u = u * cosine + swap_halves(u) * sine
                for h in range(4):
                    if g < 2:
                        qh[4 * g + h, at, :] = head(u, h)
                    elif g == 2:
                        kh[h, at, :] = head(u, h)
                    else:
                        vh[h, at, :] = head(u, h)
            return carry

        def attend(h, carry):
            @pl.when(h == 0)
            def _():
                for i in (1, 2):
                    ln.gather_take(C, i, c_of)

            c = lax.div(h, 2)
            for b in range(4):
                far = (b + 1) * rows
                here = slice(b * rows, far)
                sc = mm(kh[c, :far, :], qh[h, here, :], NT) * scale + bias[:far, here]
                peak = jnp.max(sc, axis=0, keepdims=True)
                e = jnp.exp(sc - peak)
                total = jnp.sum(e, axis=0, keepdims=True)
                p = (e * (1.0 / total)).astype(BF16)
                outh[h, here, :] = mm(p, vh[c, :far, :], TN)
                lse[h, :, here] = peak + jnp.log(total)
            return carry


        def pack(b, carry):
            for g in range(2):
                acc = jnp.zeros((rows, span), F32)
                for h in range(4):
                    piece = jnp.concatenate(
                        [outh[4 * g + h, ds_of(b), :], jnp.zeros((rows, span - 128), F32)], axis=1
                    )
                    acc = acc + lane_roll(piece, HEAD * h)
                att[b, :, g * span : (g + 1) * span] = acc.astype(BF16)
            return carry

        own = pltpu.make_async_copy(att.at[t], columns(t), local.at[0])

        @inner
        def _():
            for b in range(4):
                far = (b + 1) * rows
                bias[:far, b * rows : far] = jnp.where(visible((far, rows), b), 0.0, MASKED)
            w_plane.hand_on()
            o_plane.start()
            w_plane.take()
            for m in (1, 2, 3):
                ln.landed_tensor(X, m, x_of(tensor_peer(t, m)))
            lax.fori_loop(0, 4, project, 0)

        o_plane.hand_on()

        @inner
        def _():
            lax.fori_loop(0, 8, attend, 0)
            lax.fori_loop(0, 4, pack, 0)
            for m in (2, 1, 3):
                ln.over_tensor(A, m, att.at[tensor_peer(t, m)], columns(t)).start()
            own.start()
            ln.gather_take(C, 3, c_of)
            own.wait()

        o_plane.take()
        from_inner(A, lambda kind, m, p: ln.landed_tensor(kind, m, columns(p)))
        third = width // 3

        def project_out(n, carry):
            cols = pl.ds(pl.multiple_of(n * third, 128), third)
            resid[:, cols] = xall[at_own, cols].astype(F32) + mm(arow[...], wof[:, cols])
            return carry

        lax.fori_loop(0, 3, project_out, 0)
        r = resid[...]
        inv = lax.rsqrt(jnp.mean(r * r, axis=1, keepdims=True) + EPSILON)
        normed2[...] = (r * inv * gains[1:2, :]).astype(BF16)
        ln.gather_start(N, normed2, x_of)
        xall[at_own, :] = normed2[...]

    def feed(loads, gate_w, up_w, down_w, act, gg, gu, gsend, gown, part, gact):
        for c in loads:
            c.wait()

        def to_owner(shard, m):
            return pltpu.make_async_remote_copy(
                src_ref=gsend.at[shard],
                dst_ref=grecv.at[m - 1],
                send_sem=tsend.at[G, m],
                recv_sem=trecv.at[G, m],
                device_id={"dp": d, "tensor": shard},
                device_id_type=MESH,
            )

        @pl.when(ln.mid == 0)
        def _():
            for i in (1, 2, 3):
                ln.gather_take(C, i, c_of)

        piece = units // 4

        def one_shard(i, carry):
            shard, m = ln.shard_at(i)
            at = ds_of(shard)
            gact[...] = mm(call[at, :], down_w[...], NT)

            @pl.when(i > 0)
            def _():
                ln.gather_take(N, i, x_of)

            r = xall[at, :]
            for c in range(4):
                cols = slice(c * piece, (c + 1) * piece)
                gate = mm(r, gate_w[:, cols])
                up = mm(r, up_w[:, cols])
                sig = 1.0 / (1.0 + jnp.exp(-gate))
                silu = gate * sig
                act[at, cols] = (silu * up).astype(BF16)
                g_act = gact[:, cols]
                gg[at, cols] = (g_act * up * sig * (1.0 + gate * (1.0 - sig))).astype(BF16)
                gu[at, cols] = (g_act * silu).astype(BF16)
            g = mm(gg[at, :], gate_w[...], NT) + mm(gu[at, :], up_w[...], NT)

            @pl.when(i == 0)
            def _():
                gown[...] = g

            @pl.when(i > 0)
            def _():
                gsend[shard] = g.astype(BF16)
                to_owner(shard, m).start()

            return carry

        lax.fori_loop(0, 4, one_shard, 0)

        def side(which):
            return pl.ds(pl.multiple_of(which * half, half), half)

        def to_core(k, j):
            return pltpu.make_async_remote_copy(
                src_ref=part.at[j, side(1 - core), :],
                dst_ref=ff.at[j, k],
                send_sem=dsend.at[CK + k, j],
                recv_sem=drecv.at[CK + k, j],
                device_id={"dp": dp_peer(d, 1), "tensor": t},
                device_id_type=MESH,
            )

        def chip_sum(k, j):
            to_core(k, j).wait_recv()
            ff[j, k] = (
                part[j, side(core), :].astype(F32) + ff[j, k].astype(F32)
            ).astype(BF16)
            to_core(k, j).wait_send()

        for k, (a, b) in enumerate(((xall, gg), (xall, gu), (call, act))):

            def weights(j, carry, k=k, a=a, b=b):
                cols = pl.ds(pl.multiple_of(j * span, 128), span)
                if k > 0:

                    @pl.when(j == 2)
                    def _():
                        chip_sum(k - 1, 3)
                        ff_sums[k - 1].start()

                part[j] = mm(a[:, cols], b[...], TN).astype(BF16)
                to_core(k, j).start()

                @pl.when(j > 0)
                def _():
                    chip_sum(k, j - 1)

                return carry

            lax.fori_loop(0, 4, weights, 0)
        chip_sum(2, 3)
        ff_sums[2].start()

        def feed_sums(n, carry):
            third = width // 3
            cols = pl.ds(pl.multiple_of(n * third, 128), third)
            msend[:, :, cols] = mm(act[...], down_w[:, cols]).astype(BF16).reshape(4, rows, third)
            return carry

        lax.fori_loop(0, 3, feed_sums, 0)
        for m in (1, 2, 3):
            ln.landed_tensor(G, m, grecv.at[m - 1])
        g = gown[...]
        for m in (1, 2, 3):
            g = g + grecv[m - 1].astype(F32)
        r = resid[...]
        inv = lax.rsqrt(jnp.mean(r * r, axis=1, keepdims=True) + EPSILON)
        gain[0] = jnp.sum(g * r * inv, axis=0, keepdims=True)
        scaled = g * gains[1:2, :]
        gr = (
            call[at_own, :].astype(F32)
            + inv * scaled
            - r * (inv * inv * inv) * jnp.mean(scaled * r, axis=1, keepdims=True)
        )
        gres[...] = gr
        low[...] = gr.astype(BF16)
        for g in range(2):
            gatt[g] = mm(low[...], wof[g * wide : (g + 1) * wide, :], NT).astype(BF16)
        for m in (1, 2, 3):
            to_owner(tensor_peer(t, m), m).wait_send()

    def forward(gate_w, up_w, down_w):
        loads = [
            pltpu.make_async_copy(a, b, local.at[5 + i])
            for i, (a, b) in enumerate(((wg, gate_w), (wu, up_w), (wd, down_w)))
        ]
        for c in loads:
            c.start()
        pl.run_scoped(front, V((8, seq, 128), F32))
        hidden = V((seq, units), BF16)
        pl.run_scoped(
            functools.partial(feed, loads, gate_w, up_w, down_w),
            hidden, hidden, hidden, V((4, rows, width), BF16), V((rows, width), F32),
            V((4, span, units), BF16), V((rows, units), F32),
        )

    pl.run_scoped(
        forward, V((width, units), BF16), V((width, units), BF16), V((units, width), BF16)
    )

    def backward(gh, gq, gk, gv, gqkv, gn_src, wo_part, layer, gin, wqkv, wo_full, ffw):
        to_inner(GA, lambda g: gatt.at[g], rows_at(gall, t), go)
        own = [
            pltpu.make_async_copy(gatt.at[t - 1], rows_at(gall, t), local.at[0]),
            pltpu.make_async_copy(gain, rows_in.at[pl.ds(d, 1)], local.at[1]),
        ]
        inner(own[0].start)
        own[1].start()
        for m in range(1, 8):
            ln.over_dp(DR, m, gain.at[0], rows_in.at[d]).start()
        layer_sum.start()
        ln.gather_end(O, wo, wo_of)
        o_plane.end()
        wo_pair = CoreSum(ln, CO, wo_part, lambda j: wo_core.at[j])

        def output_weights(j, carry):
            cols = pl.ds(pl.multiple_of(j * span, 128), span)
            wo_part[j] = mm(arow[:, cols], low[...], TN).astype(BF16)
            wo_pair.copy(j).start()
            return carry

        lax.fori_loop(0, 4, output_weights, 0)
        for k in range(2):
            ff_sums[k].hand_on()
        keep = lax.broadcasted_iota(jnp.int32, (rows, 128), 1) < HEAD
        wo_pair.take()
        wo_sum = PlaneSum(ln, DOS, lambda j: wo_core.at[j], lambda i: wo_in.at[i], width)
        wo_sum.start()

        def split(b, carry):
            for g in range(2):
                u = gall[ds_of(b), g * span : (g + 1) * span].astype(F32)
                for h in range(4):
                    gh[4 * g + h, ds_of(b), :] = jnp.where(
                        keep, lane_roll(u, -HEAD * h)[:, :128], 0.0
                    ).astype(BF16)
            return carry

        def attend_back(h, carry):
            c = lax.div(h, 2)
            for b in range(4):
                far = (b + 1) * rows
                here = slice(b * rows, far)
                k, v, q, g = kh[c, :far, :], vh[c, :far, :], qh[h, here, :], gh[h, here, :]
                sc = mm(k, q, NT) * scale + bias[:far, here]
                p = jnp.exp(sc - lse[h, :, here])
                gp = mm(v, g, NT)
                gs = (p * (gp - jnp.sum(p * gp, axis=0, keepdims=True))).astype(BF16)
                gq[h, here, :] = mm(gs, k, TN)
                gk[c, :far, :] += mm(gs, q)
                gv[c, :far, :] += mm(p.astype(BF16), g)
            return carry


        def gather_heads(b, carry):
            at = ds_of(b)
            cosine, sine = turn_tables(near_cos, near_sin, shift, b)
            cosine, sine = cosine[:, :128], sine[:, :128]

            def placed(u, h):
                u = jnp.concatenate(
                    [jnp.where(keep, u, 0.0), jnp.zeros((rows, 4 * HEAD - 128), F32)], axis=1
                )
                return lane_roll(u, HEAD * h)

            def turned(u):
                u = u * scale
                return u * cosine - swap_halves(u) * sine

            parts = [
                [turned(gq[h, at, :]) for h in range(4)],
                [turned(gq[4 + h, at, :]) for h in range(4)],
                [turned(gk[c, at, :]) for c in range(4)],
                [gv[c, at, :] for c in range(4)],
            ]
            for g, heads in enumerate(parts):
                u = sum(placed(v, h) for h, v in enumerate(heads))
                gqkv[at, g * span : (g + 1) * span] = u.astype(BF16)
            return carry

        def to_row_owner(shard, m):
            return pltpu.make_async_remote_copy(
                src_ref=gn_src.at[shard],
                dst_ref=grecv.at[m - 1],
                send_sem=tsend.at[B, m],
                recv_sem=trecv.at[B, m],
                device_id={"dp": d, "tensor": shard},
                device_id_type=MESH,
            )

        def norm_grads(i, carry):
            shard, m = ln.shard_at(3 - i)
            gn_src[shard] = mm(gqkv[ds_of(shard), :], w[...], NT).astype(BF16)

            @pl.when(i < 3)
            def _():
                to_row_owner(shard, m).start()

            return carry

        @inner
        def _():
            own[0].wait()
            for m in (1, 2, 3):
                ln.landed_tensor(GA, m, rows_at(gall, tensor_peer(t, m)))
            lax.fori_loop(0, 4, split, 0)
            gk[...] = jnp.zeros_like(gk)
            gv[...] = jnp.zeros_like(gv)
            lax.fori_loop(0, 8, attend_back, 0)
            lax.fori_loop(0, 4, gather_heads, 0)
            wo_sum.hand_on()
            lax.fori_loop(0, 4, norm_grads, 0)

        outer(wo_sum.hand_on)
        ff_sums[2].hand_on()

        def in_wo(j):
            return wof.at[pl.ds(pl.multiple_of(j * half, half), half), :]

        def in_wo_half(i):
            return wof.at[(4 + i // 2) * half : (5 + i // 2) * half, (i % 2) * wide : (i % 2 + 1) * wide]

        wo_pair.end()
        wq_pair = CoreSum(ln, CW, wo_part, in_wo)
        wq_sum = PlaneSum(ln, DWS, in_wo, in_wo_half, width)

        def head_weights(j, carry):
            cols = pl.ds(pl.multiple_of(j * span, 128), span)
            wo_part[j] = mm(nall[:, cols], gqkv[...], TN).astype(BF16)
            wq_pair.copy(j).start()
            return carry

        @inner
        def _():
            lax.fori_loop(0, 4, head_weights, 0)

        def to_rows(total, dst):
            lanes = total.lanes
            for h in range(2):
                u = total.take(h).astype(BF16)
                for s in range(4):
                    dst[s, :, h * lanes : (h + 1) * lanes] = u[s * wrows : (s + 1) * wrows, :]

        to_rows(wo_sum, wo_src)
        wo_line_sum = LineSum(ln, OL, wo_src, wo_line)
        wo_line_sum.start()
        @inner
        def _():
            wq_pair.take()
            wq_sum.start()

        own[1].wait()
        for m in range(1, 8):
            ln.landed_dp(DR, m, rows_in.at[dp_peer(d, m)])
        gsum[0] = sum(rows_in[i] for i in range(8))
        for m in (1, 2, 3):
            ln.over_tensor(R, m, gsum.at[0], line_in.at[m]).start()
        layer_sum.hand_on()
        stores = []

        def out(a, b):
            c = pltpu.make_async_copy(a, b, store.at[len(stores)])
            c.start()
            stores.append(c)

        def feed_weights(k):
            lanes = units // 2
            for h in range(2):
                ffw[k, :, h * lanes : (h + 1) * lanes] = ff_sums[k].take(h)
            out(ffw.at[k], mlpw_out.at[k])

        inner(wq_sum.hand_on)
        layer[...] = (resid[...] + msend[t].astype(F32) + layer_sum.take()).astype(BF16)
        out(layer, layer_out)
        for k in range(3):
            feed_weights(k)

        @inner
        def _():
            to_rows(wq_sum, wq_src)
            for m in (2, 1, 3):
                ln.over_tensor(WL, m, wq_src.at[tensor_peer(t, m)], wq_all.at[m]).start()
            wqkv[pl.ds(t - 1, 1)] = wq_src[pl.ds(t, 1)].astype(F32)

        wo_line_sum.hand_on()
        total = gsum[0]
        for m in (1, 2, 3):
            ln.landed_tensor(R, m, line_in.at[m])
            total = total + line_in[m]
        mine = (d * 4 + t) * wrows
        turned = pltpu.roll(jnp.broadcast_to(total, (8, width)), lax.rem(width - mine, width), 1)
        gown_row[...] = turned[:, :128]
        out(gown_row, gain_out)
        x = hid[...].astype(F32)
        inv = lax.rsqrt(jnp.mean(x * x, axis=1, keepdims=True) + EPSILON)
        from_inner(B, lambda kind, m, p: ln.landed_tensor(kind, m, grecv.at[m - 1]))

        @outer
        def _():
            gin[...] = grecv[0].astype(F32) + grecv[1].astype(F32)

        @inner
        def _():
            gin[...] = grecv[2].astype(F32) + gn_src[t].astype(F32)

        scaled = gin[...] * gains[0:1, :]
        gin[...] = (
            gres[...]
            + inv * scaled
            - x * (inv * inv * inv) * jnp.mean(scaled * x, axis=1, keepdims=True)
        )
        out(gin, gin_out)
        wo_full[...] = wo_src[t].astype(F32) + wo_line_sum.take()
        out(wo_full, wo_out)

        def columns_in(kind, m, p):
            ln.landed_tensor(kind, m, wq_all.at[m])
            wqkv[pl.ds(p - 1, 1)] = wq_all[pl.ds(m, 1)].astype(F32)

        from_inner(WL, columns_in)
        out(wqkv, wqkv_out)

        for m in (1, 2, 3):
            ln.over_tensor(TILE, m, tile, tiles.at[d, t]).wait_send()
            ln.over_tensor(R, m, gsum.at[0], line_in.at[m]).wait_send()
        to_inner(W, lambda g: wpack.at[g], w_at(w, d, t), gone)
        to_inner(X, lambda g: hid, x_of(t), gone)
        to_inner(GA, lambda g: gatt.at[g], rows_at(gall, t), gone)
        ln.gather_end(C, cot, c_of)
        ln.gather_end(N, normed2, x_of)
        for m in range(1, 8):
            ln.over_dp(DT, m, tiles.at[d], tiles.at[d]).wait_send()
            ln.over_dp(DR, m, gain.at[0], rows_in.at[d]).wait_send()

        @inner
        def _():
            for m in (1, 2, 3):
                ln.over_tensor(A, m, att.at[tensor_peer(t, m)], columns(t)).wait_send()
                ln.over_tensor(WL, m, wq_src.at[tensor_peer(t, m)], wq_all.at[m]).wait_send()
                to_row_owner(tensor_peer(t, m), m).wait_send()
            for s in (w_plane, wq_sum, wq_pair):
                s.end()

        for s in (layer_sum, wo_line_sum, *ff_sums, wo_sum):
            s.end()
        for c in stores:
            c.wait()

    pl.run_scoped(
        backward,
        V((8, seq, 128), BF16), V((8, seq, 128), F32), V((4, seq, 128), F32),
        V((4, seq, 128), F32), V((seq, width), BF16), V((4, rows, width), BF16),
        V((4, span, width), BF16),
        V((rows, width), BF16), V((rows, width), F32), V((2, wrows, width), F32),
        V((wrows, width), F32), V((3, half, units), F32),
    )


def layer(hid, cot, positions, gain_attn, gain_mlp, wq, wk, wv, wo, wg, wu, wd):
    rows, width = hid.shape
    wrows = wq.shape[0]
    units = wg.shape[1]
    seq = 4 * rows
    span = width // 4
    half = span // 2
    near_cos, near_sin, shift = rotary_tables(rows, 4)
    hbm = pl.BlockSpec(memory_space=pl.ANY)
    vmem = pl.BlockSpec(memory_space=pltpu.VMEM)
    V = pltpu.VMEM
    shapes = dict(
        layer=((rows, width), BF16), gin=((rows, width), F32), gain=((8, 128), F32),
        wqkv=((2, wrows, width), F32), wo=((wrows, width), F32),
        mlp=((3, half, units), F32),
    )
    wide = V((seq, width), BF16)
    thin, thin_f = V((rows, width), BF16), V((rows, width), F32)
    four = V((4, rows, width), BF16)
    pair = V((4, seq, 128), BF16)
    outs = pl.pallas_call(
        layer_kernel,
        out_shape=[jax.ShapeDtypeStruct(*v) for v in shapes.values()],
        in_specs=[vmem, hbm] + [vmem] * 6 + [hbm] * 4 + [vmem] * 3,
        out_specs=[hbm] * len(shapes),
        scratch_shapes=[
            wide, wide, wide, V((width, width), BF16), V((width, width), BF16),
            V((8, 4, 8, 128), F32), V((8, seq, 128), BF16), pair, pair,
            V((4, rows, 2 * span), BF16), thin, V((8, 1, seq), F32), V((1, seq), F32),
            V((8, width), F32), thin_f, thin,
            four, V((4, 3, half, units), BF16), four, V((2, rows, 2 * span), BF16), thin_f, thin,
            V((1, 1, width), F32),
            V((seq, 2 * span), BF16), four, V((6, 3, half, units // 2), BF16),
            V((4, half, width), BF16), V((6, half, width // 2), BF16),
            V((4, wrows, width), BF16), V((4, wrows, width), BF16),
            V((4, wrows, width), BF16), V((4, wrows, width), BF16),
            V((8, 1, width), F32), V((4, 1, width), F32), V((1, 1, width), F32),
            V((8, 128), F32), V((2, wrows, width), BF16), V((8, 128), F32), V((seq, seq), F32),
            pltpu.SemaphoreType.DMA((14, 6)), pltpu.SemaphoreType.DMA((14, 4)),
            pltpu.SemaphoreType.DMA((16, 8)), pltpu.SemaphoreType.DMA((16, 8)),
            pltpu.SemaphoreType.DMA((8,)), pltpu.SemaphoreType.DMA((8,)),
        ],
        name="layer",
        compiler_params=pltpu.CompilerParams(
            collective_id=0, has_side_effects=True, vmem_limit_bytes=VMEM_LIMIT
        ),
    )(
        hid, cot, positions.reshape(1, rows), gain_attn.reshape(1, wrows),
        gain_mlp.reshape(1, wrows), wq, wk, wv, wo, wg, wu, wd, near_cos, near_sin, shift,
    )
    return dict(zip(shapes, outs))


def finish_kernel(
    layer, gin, gain, wqkv, wo, mlp, wq, wk, wv, gain_one,
    layer_out, gin_out, gain_one_out, query_out, key_out, value_out, wo_out, gain_two_out,
    gate_out, up_out, down_out,
    lay, gi, ga, w4, wof, ff, one, query, key, value, two, load, store,
):
    moves = [
        (layer, lay, layer_out), (gin, gi, gin_out), (wo, wof, wo_out),
        (mlp.at[0], ff.at[0], gate_out), (mlp.at[1], ff.at[1], up_out),
        (mlp.at[2], ff.at[2], down_out), (wqkv, w4, None), (gain, ga, None),
    ]
    loads = [pltpu.make_async_copy(a, b, load.at[i]) for i, (a, b, _) in enumerate(moves)]
    for i in (6, 7, 0, 1, 2, 3, 4, 5):
        loads[i].start()
    stores = []

    def out(a, b):
        c = pltpu.make_async_copy(a, b, store.at[len(stores)])
        c.start()
        stores.append(c)

    wrows, span = query.shape[0], query.shape[1] // 4
    wide = 2 * span
    loads[6].wait()
    for g in range(2):
        query[:, g * wide : (g + 1) * wide] = w4[g, :, :wide]
        key[:, g * span : (g + 1) * span] = w4[g, :, wide : wide + span]
        value[:, g * span : (g + 1) * span] = w4[g, :, wide + span :]
    out(query, query_out)
    out(key, key_out)
    out(value, value_out)
    total = (
        jnp.sum(wq[...].astype(F32) * query[...], axis=1, keepdims=True)
        + jnp.sum(wk[...].astype(F32) * key[...], axis=1, keepdims=True)
        + jnp.sum(wv[...].astype(F32) * value[...], axis=1, keepdims=True)
    )
    tall = jnp.concatenate(
        [jnp.broadcast_to(total, (wrows, 128)), jnp.zeros((128 - wrows, 128), F32)], axis=0
    )
    one[...] = tall.T[0:1, :wrows] / gain_one[...].astype(F32)
    out(one, gain_one_out)
    loads[7].wait()
    two[...] = ga[0:1, :wrows]
    out(two, gain_two_out)
    for i in range(6):
        loads[i].wait()
        out(moves[i][1], moves[i][2])
    for c in stores:
        c.wait()


def finish(b, wq, wk, wv, gain_attn):
    rows, width = b["layer"].shape
    wrows, kv = wk.shape
    half, units = b["mlp"].shape[1:]
    hbm = pl.BlockSpec(memory_space=pl.ANY)
    vmem = pl.BlockSpec(memory_space=pltpu.VMEM)
    V = pltpu.VMEM
    thin = ((rows, width), F32)
    row = ((1, wrows), F32)
    weight, narrow = ((wrows, width), F32), ((wrows, kv), F32)
    shapes = [
        ((rows, width), BF16), thin, row, weight, narrow, narrow, weight, row,
        ((half, units), F32), ((half, units), F32), ((half, units), F32),
    ]
    return pl.pallas_call(
        finish_kernel,
        out_shape=[jax.ShapeDtypeStruct(*v) for v in shapes],
        in_specs=[hbm] * 6 + [vmem] * 4,
        out_specs=[hbm] * len(shapes),
        scratch_shapes=[
            V((rows, width), BF16), V(*thin), V((8, 128), F32), V((2, wrows, width), F32),
            V(*weight), V((3, half, units), F32), V(*row), V(*weight), V(*narrow), V(*narrow),
            V(*row),
            pltpu.SemaphoreType.DMA((8,)), pltpu.SemaphoreType.DMA((11,)),
        ],
        name="finish",
        compiler_params=pltpu.CompilerParams(vmem_limit_bytes=VMEM_LIMIT),
    )(
        b["layer"], b["gin"], b["gain"], b["wqkv"], b["wo"], b["mlp"], wq, wk, wv,
        gain_attn.reshape(1, wrows),
    )


QUERY_HEADS = 16
KEY_VALUE_HEADS = 8
HEAD_DIMENSION = 96


def angle_tables(pos_rows, head_size):
    half_size = head_size // 2
    freq_rates = ROPE_BASE ** (-(jnp.arange(half_size, dtype=jnp.float32) * 2.0) / head_size)
    turned = pos_rows.astype(jnp.float32)[:, None] * freq_rates[None, :]
    return (jnp.cos(turned)[:, None, :], jnp.sin(turned)[:, None, :])


def apply_rotary(tensor_in, cosine_table, sine_table):
    half_size = tensor_in.shape[-1] // 2
    lo_half = tensor_in[..., :half_size]
    hi_half = tensor_in[..., half_size:]
    return jnp.concatenate(
        [
            lo_half * cosine_table - hi_half * sine_table,
            hi_half * cosine_table + lo_half * sine_table,
        ],
        axis=-1,
    )


def shards(
    hidden_in,
    positions,
    gain_attn,
    w_query,
    key_matrix,
    value_matrix,
    w_output,
    gain_mlp,
    w_gate,
    w_up,
    w_down,
    cotangent,
):
    tok_rows = hidden_in.shape[0]
    model_width = hidden_in.shape[1]
    num_heads = QUERY_HEADS
    key_value_count = KEY_VALUE_HEADS
    head_size = HEAD_DIMENSION
    kv_width = key_value_count * head_size
    queries_per_group = num_heads // key_value_count
    seq_len = tok_rows * lax.axis_size("tensor")
    score_scale = 1.0 / math.sqrt(head_size)
    gathered = (
        lax.all_gather(gain_attn, ("dp", "tensor"), axis=0, tiled=True),
        lax.all_gather(w_query, ("dp", "tensor"), axis=0, tiled=True),
        lax.all_gather(key_matrix, ("dp", "tensor"), axis=0, tiled=True),
        lax.all_gather(value_matrix, ("dp", "tensor"), axis=0, tiled=True),
        lax.all_gather(w_output, ("dp", "tensor"), axis=0, tiled=True),
        lax.all_gather(gain_mlp, ("dp", "tensor"), axis=0, tiled=True),
    )
    gain_one, query_full, key_full, value_full, output_full, gain_two = gathered
    gain_one_f = gain_one.astype(jnp.float32)
    gain_two_f = gain_two.astype(jnp.float32)
    x_float = hidden_in.astype(jnp.float32)
    inv_one = lax.rsqrt(jnp.mean(x_float * x_float, axis=-1, keepdims=True) + EPSILON)
    normed_one = (x_float * inv_one * gain_one_f).astype(jnp.bfloat16)
    queries = jnp.dot(normed_one, query_full, preferred_element_type=jnp.float32)
    key_projected = jnp.dot(normed_one, key_full, preferred_element_type=jnp.float32)
    value_proj = jnp.dot(normed_one, value_full, preferred_element_type=jnp.float32)
    cosine_table, sine_table = angle_tables(positions, head_size)
    rotated_query_rows = apply_rotary(
        queries.reshape(tok_rows, num_heads, head_size), cosine_table, sine_table
    ).astype(jnp.bfloat16)
    rotated_key_rows = (
        apply_rotary(
            key_projected.reshape(tok_rows, key_value_count, head_size), cosine_table, sine_table
        )
        .astype(jnp.bfloat16)
        .reshape(tok_rows, kv_width)
    )
    value_rows_lowered = value_proj.astype(jnp.bfloat16)
    keys_all, values_all = (
        lax.all_gather(rotated_key_rows, "tensor", axis=0, tiled=True),
        lax.all_gather(value_rows_lowered, "tensor", axis=0, tiled=True),
    )
    offset = lax.axis_index("tensor") * tok_rows
    query_index = offset + jnp.arange(tok_rows, dtype=jnp.int32)
    key_index = jnp.arange(seq_len, dtype=jnp.int32)
    visible = (key_index[None, :] <= query_index[:, None]) & (
        key_index[None, :] >= (query_index - positions)[:, None]
    )
    visible = jnp.tile(visible, (queries_per_group, 1))

    def split_queries(tensor_in):
        return (
            tensor_in.reshape(tok_rows, key_value_count, queries_per_group, head_size)
            .transpose(1, 2, 0, 3)
            .reshape(key_value_count, queries_per_group * tok_rows, head_size)
        )

    def split_keys(tensor_in):
        return tensor_in.reshape(seq_len, key_value_count, head_size).transpose(1, 0, 2)

    def merge_heads(tensor_in):
        return (
            tensor_in.reshape(key_value_count, queries_per_group, tok_rows, head_size)
            .transpose(2, 0, 1, 3)
            .reshape(tok_rows, model_width)
        )

    query_heads = split_queries(rotated_query_rows)
    k_heads = split_keys(keys_all)
    value_heads = split_keys(values_all)

    def attend(head_items):
        q_block, k_block, v_block = head_items
        scores = (
            jnp.einsum("qd,kd->qk", q_block, k_block, preferred_element_type=jnp.float32)
            * score_scale
        )
        scores = jnp.where(visible, scores, MASKED)
        peak = jnp.max(scores, axis=-1, keepdims=True)
        exp_vals = jnp.exp(scores - peak)
        total = jnp.sum(exp_vals, axis=-1, keepdims=True)
        probs = exp_vals / total
        out_block = jnp.einsum(
            "qk,kd->qd", probs.astype(jnp.bfloat16), v_block, preferred_element_type=jnp.float32
        )
        return (out_block, peak[:, 0] + jnp.log(total[:, 0]))

    attended_rows, log_total = lax.map(attend, (query_heads, k_heads, value_heads))
    attended_low = merge_heads(attended_rows).astype(jnp.bfloat16)
    resid_sum = x_float + jnp.dot(attended_low, output_full, preferred_element_type=jnp.float32)
    inv_two = lax.rsqrt(jnp.mean(resid_sum * resid_sum, axis=-1, keepdims=True) + EPSILON)
    normed_two = (resid_sum * inv_two * gain_two_f).astype(jnp.bfloat16)
    rows_all = lax.all_gather(normed_two, "tensor", axis=0, tiled=True)
    gate_val = jnp.dot(rows_all, w_gate, preferred_element_type=jnp.float32)
    up_val = jnp.dot(rows_all, w_up, preferred_element_type=jnp.float32)
    sig_gate = jax.nn.sigmoid(gate_val)
    silu_gate = gate_val * sig_gate
    act_low = (silu_gate * up_val).astype(jnp.bfloat16)
    mlp_sum = lax.psum_scatter(
        jnp.dot(act_low, w_down, preferred_element_type=jnp.float32).astype(jnp.bfloat16),
        "tensor",
        scatter_dimension=0,
        tiled=True,
    ).astype(jnp.float32)
    layer_out = (resid_sum + mlp_sum).astype(jnp.bfloat16)
    grad_float = cotangent.astype(jnp.float32)
    grad_all = lax.all_gather(cotangent, "tensor", axis=0, tiled=True)
    grad_down = jnp.einsum("sf,sd->fd", act_low, grad_all, preferred_element_type=jnp.float32)
    g_act = jnp.einsum("sd,fd->sf", grad_all, w_down, preferred_element_type=jnp.float32)
    g_gate = (g_act * up_val * sig_gate * (1.0 + gate_val * (1.0 - sig_gate))).astype(jnp.bfloat16)
    g_up = (g_act * silu_gate).astype(jnp.bfloat16)
    grad_gate = jnp.einsum("sd,sf->df", rows_all, g_gate, preferred_element_type=jnp.float32)
    grad_up = jnp.einsum("sd,sf->df", rows_all, g_up, preferred_element_type=jnp.float32)
    g_norm_two = lax.psum_scatter(
        (
            jnp.einsum("sf,df->sd", g_gate, w_gate, preferred_element_type=jnp.float32)
            + jnp.einsum("sf,df->sd", g_up, w_up, preferred_element_type=jnp.float32)
        ).astype(jnp.bfloat16),
        "tensor",
        scatter_dimension=0,
        tiled=True,
    ).astype(jnp.float32)
    scaled_two = gain_two_f * g_norm_two
    grad_gain_two = jnp.sum(g_norm_two * resid_sum * inv_two, axis=0)
    g_resid = (
        grad_float
        + inv_two * scaled_two
        - resid_sum * inv_two**3 * jnp.mean(scaled_two * resid_sum, axis=-1, keepdims=True)
    )
    g_resid_low = g_resid.astype(jnp.bfloat16)
    grad_output = jnp.einsum(
        "tc,td->cd", attended_low, g_resid_low, preferred_element_type=jnp.float32
    )
    g_att = jnp.einsum(
        "td,cd->tc", g_resid_low, output_full, preferred_element_type=jnp.float32
    ).astype(jnp.bfloat16)
    g_heads = split_queries(g_att)

    def attend_back(head_items):
        q_block, k_block, v_block, log_block, g_block = head_items
        scores = (
            jnp.einsum("qd,kd->qk", q_block, k_block, preferred_element_type=jnp.float32)
            * score_scale
        )
        scores = jnp.where(visible, scores, MASKED)
        probs = jnp.exp(scores - log_block[:, None])
        g_probs = jnp.einsum("qd,kd->qk", g_block, v_block, preferred_element_type=jnp.float32)
        g_scores = (probs * (g_probs - jnp.sum(probs * g_probs, axis=-1, keepdims=True))).astype(
            jnp.bfloat16
        )
        g_rq = (
            jnp.einsum("qk,kd->qd", g_scores, k_block, preferred_element_type=jnp.float32)
            * score_scale
        )
        g_rk = (
            jnp.einsum("qk,qd->kd", g_scores, q_block, preferred_element_type=jnp.float32)
            * score_scale
        )
        g_val = jnp.einsum(
            "qk,qd->kd", probs.astype(jnp.bfloat16), g_block, preferred_element_type=jnp.float32
        )
        return (g_rq, g_rk, g_val)

    g_rq, g_rk, g_val = lax.map(
        attend_back, (query_heads, k_heads, value_heads, log_total, g_heads)
    )
    g_rk_flat = g_rk.transpose(1, 0, 2).reshape(seq_len, kv_width)
    g_val_flat = g_val.transpose(1, 0, 2).reshape(seq_len, kv_width)
    key_part, value_part = (
        lax.psum_scatter(
            g_rk_flat.astype(jnp.bfloat16), "tensor", scatter_dimension=0, tiled=True
        ).astype(jnp.float32),
        lax.psum_scatter(
            g_val_flat.astype(jnp.bfloat16), "tensor", scatter_dimension=0, tiled=True
        ).astype(jnp.float32),
    )
    g_queries = (
        apply_rotary(
            merge_heads(g_rq).reshape(tok_rows, num_heads, head_size), cosine_table, -sine_table
        )
        .reshape(tok_rows, model_width)
        .astype(jnp.bfloat16)
    )
    g_keys = (
        apply_rotary(
            key_part.reshape(tok_rows, key_value_count, head_size), cosine_table, -sine_table
        )
        .reshape(tok_rows, kv_width)
        .astype(jnp.bfloat16)
    )
    g_values = value_part.astype(jnp.bfloat16)
    grad_query = jnp.einsum("tc,td->cd", normed_one, g_queries, preferred_element_type=jnp.float32)
    grad_key = jnp.einsum("tc,td->cd", normed_one, g_keys, preferred_element_type=jnp.float32)
    grad_value = jnp.einsum("tc,td->cd", normed_one, g_values, preferred_element_type=jnp.float32)
    g_norm_one = (
        jnp.einsum("td,cd->tc", g_queries, query_full, preferred_element_type=jnp.float32)
        + jnp.einsum("td,cd->tc", g_keys, key_full, preferred_element_type=jnp.float32)
        + jnp.einsum("td,cd->tc", g_values, value_full, preferred_element_type=jnp.float32)
    )
    scaled_one = gain_one_f * g_norm_one
    grad_gain_one = jnp.sum(g_norm_one * x_float * inv_one, axis=0)
    grad_input = (
        g_resid
        + inv_one * scaled_one
        - x_float * inv_one**3 * jnp.mean(scaled_one * x_float, axis=-1, keepdims=True)
    )
    packed = jnp.concatenate([grad_query, grad_key, grad_value, grad_output], axis=1)
    packed_part = lax.psum_scatter(
        packed.astype(jnp.bfloat16), ("dp", "tensor"), scatter_dimension=0, tiled=True
    ).astype(jnp.float32)
    query_part = packed_part[:, :model_width]
    keyw_part = packed_part[:, model_width : model_width + kv_width]
    valuew_part = packed_part[:, model_width + kv_width : model_width + 2 * kv_width]
    out_part = packed_part[:, model_width + 2 * kv_width :]
    gain_one_part, gain_two_part = (
        lax.psum_scatter(grad_gain_one, ("dp", "tensor"), scatter_dimension=0, tiled=True),
        lax.psum_scatter(grad_gain_two, ("dp", "tensor"), scatter_dimension=0, tiled=True),
    )
    gate_sum, up_sum, down_sum = (
        lax.psum_scatter(
            grad_gate.astype(jnp.bfloat16), "dp", scatter_dimension=0, tiled=True
        ).astype(jnp.float32),
        lax.psum_scatter(
            grad_up.astype(jnp.bfloat16), "dp", scatter_dimension=0, tiled=True
        ).astype(jnp.float32),
        lax.psum_scatter(
            grad_down.astype(jnp.bfloat16), "dp", scatter_dimension=1, tiled=True
        ).astype(jnp.float32),
    )
    return (
        layer_out,
        grad_input,
        gain_one_part,
        query_part,
        keyw_part,
        valuew_part,
        out_part,
        gain_two_part,
        gate_sum,
        up_sum,
        down_sum,
    )


def fast_shards(
    hidden_in, positions, gain_attn, w_query, key_matrix, value_matrix, w_output, gain_mlp,
    w_gate, w_up, w_down, cotangent,
):
    b = layer(
        hidden_in, cotangent, positions, gain_attn, gain_mlp, w_query, key_matrix, value_matrix,
        w_output, w_gate, w_up, w_down,
    )
    o = finish(b, w_query, key_matrix, value_matrix, gain_attn)
    wrows = w_query.shape[0]
    return (
        o[0], o[1], o[2].reshape(wrows), o[3], o[4], o[5], o[6], o[7].reshape(wrows), o[8], o[9], o[10].T,
    )


def solution(mesh):
    placed = (
        P(("dp", "tensor"), None),
        P(("dp", "tensor")),
        P(("dp", "tensor")),
        P(("dp", "tensor"), None),
        P(("dp", "tensor"), None),
        P(("dp", "tensor"), None),
        P(("dp", "tensor"), None),
        P(("dp", "tensor")),
        P(None, "tensor"),
        P(None, "tensor"),
        P("tensor", None),
        P(("dp", "tensor"), None),
    )
    fits = mesh.shape["dp"] == 8 and mesh.shape["tensor"] == 4
    return jax.shard_map(
        fast_shards if fits else shards,
        mesh=mesh,
        in_specs=placed,
        out_specs=(
            P(("dp", "tensor"), None),
            P(("dp", "tensor"), None),
            P(("dp", "tensor")),
            P(("dp", "tensor"), None),
            P(("dp", "tensor"), None),
            P(("dp", "tensor"), None),
            P(("dp", "tensor"), None),
            P(("dp", "tensor")),
            P("dp", "tensor"),
            P("dp", "tensor"),
            P("tensor", "dp"),
        ),
        check_vma=False,
    )
```
